32 devices in a mesh: shot: 4 (over y, x), sub: 8 (over z, core).
Axes of the slice: x: 2, y: 2, z: 4, core: 2. Of those that a mesh axis runs over, the one named last changes fastest.
Arguments:
- vel_model: bfloat16 [4, 32, 320, 128], P('shot', 'sub'), may hold values from 0.5 to 1
- den_model: bfloat16 [4, 32, 320, 128], P('shot', 'sub'), may hold values from 1 to 4
- cover: int32 [4, 8], replicated, may hold values from 0 to 3
- receivers: int32 [4, 512], P('shot'), may hold values from 0 to 1310719
- observed: float32 [4, 4, 512], P('shot'), may hold values from -6 to 6
- p_now: float32 [4, 32, 320, 128], P('shot', 'sub'), may hold values from -6 to 6
- p_before: float32 [4, 32, 320, 128], P('shot', 'sub'), may hold values from -6 to 6
- q_now: float32 [4, 32, 320, 128], P('shot', 'sub'), may hold values from -6 to 6
- q_before: float32 [4, 32, 320, 128], P('shot', 'sub'), may hold values from -6 to 6
Outputs:
- grad_vel: float32 [4, 32, 320, 128], P('shot', 'sub')
- grad_den: float32 [4, 32, 320, 128], P('shot', 'sub')
The draws below stay inside these ranges and needn't reach their ends.
All inputs are finite; a program needn't handle non-finite values.
Results may differ from the reference program's by a relative error of at most 0.011.
Values may be sent and summed in bfloat16 or wider, within the bound.
No kernel may reach another device: no remote copies, remote signals or barrier semaphores. Data moves between devices by JAX's collectives and lax.ppermute only.
A program may use at most 64 MiB of HBM per device.

```python
import math
import jax
import jax.numpy as jnp
from jax import lax

SX = 4
AY = 320
AZ = 128
ITERS = 4
NREC = 512
AX = 32
N_SHOT = 4
N_SUB = 8


def place_ends(drawn, own_key, least, high):
    spot = [jax.random.randint(jax.random.fold_in(own_key, axis), (), 0, length) for axis, length in enumerate(drawn.shape)]
    main_axis = drawn.shape.index(max(drawn.shape))
    beside = spot[:main_axis] + [(spot[main_axis] + 1) % drawn.shape[main_axis]] + spot[main_axis + 1:]
    return drawn.at[tuple(spot)].set(least).at[tuple(beside)].set(high)


def block_scale(key, extent, pieces, low, top_value):
    level, own = 1.0, jax.random.fold_in(key, 6)
    for axis_at, blocks in pieces:
        draws = jnp.exp(jax.random.uniform(jax.random.fold_in(own, axis_at), (blocks,), jnp.float32, low / len(pieces), top_value / len(pieces)))
        level = level * jnp.repeat(draws, extent[axis_at] // blocks).reshape([-1 if axis == axis_at else 1 for axis in range(len(extent))])
    return level


def scatter_about(own_key, dims, scale, limit, split=(), kind=jnp.bfloat16):
    gain = block_scale(own_key, dims, split, -0.22, 0.18) if split else 1.0
    array = jax.random.normal(own_key, dims, jnp.float32) * scale * gain
    return jnp.minimum(jnp.maximum(array, -limit), limit).astype(kind)


def setup_inputs(seed: int = 0) -> dict:
    seeds = jax.random.split(jax.random.key(seed), 10)
    return {
        "vel_model": jnp.clip(0.5 + 0.5 * jax.random.uniform(seeds[0], (N_SHOT, AX, AY, AZ), jnp.float32) ** block_scale(seeds[0], (N_SHOT, AX, AY, AZ), ((0, 4), (1, 8)), -0.2, 0.2), 0.5, 1.0).astype(jnp.bfloat16),
        "den_model": jnp.clip(jnp.exp(math.log(4.0) - 1.3862944 * jax.random.uniform(seeds[1], (N_SHOT, AX, AY, AZ), jnp.float32) ** block_scale(seeds[1], (N_SHOT, AX, AY, AZ), ((0, 4), (1, 8)), -0.2, 0.2)), 1.0, 4.0).astype(jnp.bfloat16),
        "cover": place_ends(jax.random.randint(seeds[2], (N_SHOT, N_SUB), 0, N_SHOT), jax.random.fold_in(seeds[2], 1), 0, N_SHOT - 1).astype(jnp.int32),
        "receivers": place_ends(jax.random.randint(seeds[3], (N_SHOT, NREC), 0, SX * N_SUB * AY * AZ), jax.random.fold_in(seeds[3], 1), 0, (SX * N_SUB * AY * AZ) - 1).astype(jnp.int32),
        "observed": scatter_about(seeds[4], (N_SHOT, ITERS, NREC), 1.0, 6.0, ((0, 4),), jnp.float32),
        "p_now": scatter_about(seeds[5], (N_SHOT, AX, AY, AZ), 1.0, 6.0, ((0, 4), (1, 8)), jnp.float32),
        "p_before": scatter_about(seeds[6], (N_SHOT, AX, AY, AZ), 1.0, 6.0, ((0, 4), (1, 8)), jnp.float32),
        "q_now": scatter_about(seeds[7], (N_SHOT, AX, AY, AZ), 1.0, 6.0, ((0, 4), (1, 8)), jnp.float32),
        "q_before": scatter_about(seeds[8], (N_SHOT, AX, AY, AZ), 1.0, 6.0, ((0, 4), (1, 8)), jnp.float32),
    }


SECOND = (-205.0 / 72.0, 8.0 / 5.0, -1.0 / 5.0, 8.0 / 315.0, -1.0 / 560.0)
FIRST = (4.0 / 5.0, -1.0 / 5.0, 4.0 / 105.0, -1.0 / 280.0)
SPEED = 0.15


def moved(padded, direction, offset):
    window = [slice(4, padded.shape[0] - 4), slice(4, padded.shape[1] - 4), slice(4, padded.shape[2] - 4)]
    window[direction] = slice(4 + offset, padded.shape[direction] - 4 + offset)
    return padded[tuple(window)]


def stencil(padded):
    center = moved(padded, 0, 0)
    laplace = (3.0 * SECOND[0]) * center
    first_diffs = []
    for direction in range(3):
        slope_sum = jnp.zeros_like(center)
        for distance in range(1, 5):
            above_part = moved(padded, direction, distance)
            below_part = moved(padded, direction, -distance)
            laplace = laplace + SECOND[distance] * (above_part + below_part)
            slope_sum = slope_sum + FIRST[distance - 1] * (above_part - below_part)
        first_diffs.append(slope_sum)
    return laplace, first_diffs


def operate(laplace, first_diffs, slopes):
    return laplace - (slopes[0] * first_diffs[0] + slopes[1] * first_diffs[1] + slopes[2] * first_diffs[2])


def reference(vel_model, den_model, cover, receivers, observed, p_now, p_before, q_now, q_before):
    columns = jnp.arange(SX * N_SUB, dtype=jnp.int32)
    grad_vel = jnp.zeros(vel_model.shape, jnp.float32)
    grad_den = jnp.zeros(den_model.shape, jnp.float32)
    for group in range(N_SHOT):
        rows = cover[group][columns // SX].astype(jnp.int32)
        velocity = vel_model[rows, columns].astype(jnp.float32)
        density = den_model[rows, columns].astype(jnp.float32)
        log_den = jnp.log(density)
        unused_lap, slopes = stencil(jnp.pad(log_den, 4))
        scale = SPEED * velocity * velocity
        shape = velocity.shape
        cells = velocity.size
        stations = receivers[group]
        stored = []
        misfits = []
        previous, current = p_before[group], p_now[group]
        for time_step in range(ITERS):
            laplace, diffs = stencil(jnp.pad(current, 4))
            applied = operate(laplace, diffs, slopes)
            stored.append((applied, diffs))
            previous, current = current, 2.0 * current - previous + scale * applied
            misfits.append(current.reshape(-1)[stations] - observed[group, time_step])
        sum_vel = jnp.zeros(shape, jnp.float32)
        sum_den = jnp.zeros(shape, jnp.float32)
        previous, current = q_before[group], q_now[group]
        for time_step in range(ITERS):
            source = jnp.zeros((cells,), jnp.float32).at[stations].add(misfits[ITERS - 1 - time_step]).reshape(shape)
            adjoint = current + source
            laplace, diffs = stencil(jnp.pad(adjoint, 4))
            applied = operate(laplace, diffs, slopes)
            forward_applied, forward_diffs = stored[ITERS - 1 - time_step]
            sum_vel = sum_vel + adjoint * forward_applied
            sum_den = sum_den + (diffs[0] * forward_diffs[0] + diffs[1] * forward_diffs[1] + diffs[2] * forward_diffs[2])
            previous, current = current, 2.0 * adjoint - previous + scale * applied
        shot_vel = ((2.0 * SPEED) * velocity * sum_vel).astype(jnp.bfloat16)
        shot_den = (scale / density * sum_den).astype(jnp.bfloat16)
        grad_vel = grad_vel.at[rows, columns].add(lax.optimization_barrier(shot_vel).astype(jnp.float32))
        grad_den = grad_den.at[rows, columns].add(lax.optimization_barrier(shot_den).astype(jnp.float32))
    return grad_vel, grad_den
```

```python
import math

import jax
import jax.numpy as jnp
from jax import lax
from jax.experimental import pallas as pl
from jax.experimental.pallas import tpu as pltpu
from jax.sharding import PartitionSpec as P

ITERS = 4
SECOND = (-205.0 / 72.0, 8.0 / 5.0, -1.0 / 5.0, 8.0 / 315.0, -1.0 / 560.0)
FIRST = (4.0 / 5.0, -1.0 / 5.0, 4.0 / 105.0, -1.0 / 280.0)
SPEED = 0.15
PAD = 8
F32, BF16 = jnp.float32, jnp.bfloat16
VMEM_LIMIT = 4 << 20

VM = pl.BlockSpec(memory_space=pltpu.VMEM)
SM = pl.BlockSpec(memory_space=pltpu.SMEM)


def call(kernel, outs, ins, specs, out_specs=None, scratch=(), flops=0):
    outs = tuple(jax.ShapeDtypeStruct(shape, dtype) for shape, dtype in outs)
    moved_bytes = sum(math.prod(x.shape) * x.dtype.itemsize for x in (*ins, *outs))
    return pl.pallas_call(
        kernel,
        out_shape=outs,
        in_specs=list(specs),
        out_specs=tuple(out_specs or [VM] * len(outs)),
        scratch_shapes=list(scratch),
        cost_estimate=pl.CostEstimate(flops=flops, bytes_accessed=moved_bytes, transcendentals=0),
        compiler_params=pltpu.CompilerParams(vmem_limit_bytes=VMEM_LIMIT),
    )(*ins)


def weighted(pairs):
    lap, first = None, None
    for m, (ahead, behind) in enumerate(pairs, 1):
        s = SECOND[m] * (ahead + behind)
        t = FIRST[m - 1] * (ahead - behind)
        lap = s if lap is None else lap + s
        first = t if first is None else first + t
    return lap, first


def y_pairs(ref, layer, row, rows):
    return [
        (ref[layer, pl.ds(row + m, rows), :], ref[layer, pl.ds(row - m, rows), :])
        for m in range(1, 5)
    ]


def z_masks(rows, depth):
    lane = lax.broadcasted_iota(jnp.int32, (rows, depth), 1)
    return [(lane < depth - m, lane >= m) for m in range(1, 5)]


def z_pairs(value, masks):
    depth = value.shape[1]
    return [
        (
            jnp.where(ahead, pltpu.roll(value, depth - m, 1), 0.0),
            jnp.where(behind, pltpu.roll(value, m, 1), 0.0),
        )
        for m, (ahead, behind) in enumerate(masks, 1)
    ]


def x_values(flags_ref, own, on_ref, off_ref, rows):
    even = flags_ref[0] == 1
    valid = flags_ref[1] == 1
    count = len(own)
    on = [on_ref[l, rows, :].astype(F32) for l in range(count)]
    off = [jnp.where(valid, off_ref[l, rows, :].astype(F32), 0.0) for l in range(count)]
    low = [jnp.where(even, b, a) for a, b in zip(on, off)]
    high = [jnp.where(even, a, b) for a, b in zip(on, off)]
    return low[count - 4 :] + own + high[:4]


def x_pairs(values, layer):
    return [(values[4 + layer + m], values[4 + layer - m]) for m in range(1, 5)]


def zero_pads(ref):
    layers, tall, depth = ref.shape
    zeros = jnp.zeros((PAD, depth), F32)
    for l in range(layers):
        ref[l, pl.ds(0, PAD), :] = zeros
        ref[l, pl.ds(tall - PAD, PAD), :] = zeros


def prepare_kernel(p_ref, q_ref, pw_ref, qw_ref, ph_ref, qh_ref):
    layers, width, _ = p_ref.shape
    for src, wide, half in ((p_ref, pw_ref, ph_ref), (q_ref, qw_ref, qh_ref)):
        zero_pads(wide)

        @pl.loop(0, width // 16)
        def _(j, src=src, wide=wide, half=half):
            at = pl.multiple_of(16 * j, 16)
            for l in range(layers):
                v = src[l, pl.ds(at, 16), :]
                wide[l, pl.ds(at + PAD, 16), :] = v
                half[l, pl.ds(at, 16), :] = v.astype(BF16)


def list_kernel(row_ref, lane_ref, list_row, list_lane, list_at, count_ref):
    def step(i, count):
        row = row_ref[i]
        list_row[count] = row
        list_lane[count] = lane_ref[i]
        list_at[count] = i
        return count + jnp.where(row >= 0, 1, 0)

    count_ref[0] = lax.fori_loop(0, row_ref.shape[0], step, jnp.int32(0))


def add_receivers(n, field_ref, into_ref, lists, observed_ref):
    list_row, list_lane, list_at, count_ref = lists
    tall = field_ref.shape[1]
    lane = lax.broadcasted_iota(jnp.int32, (1, field_ref.shape[2]), 1)

    def step(c, carry):
        row = list_row[c]
        layer = row // tall
        y = row - layer * tall
        seen = observed_ref[n, list_at[c]]
        term = jnp.where(lane == list_lane[c], field_ref[layer, pl.ds(y, 1), :] - seen, 0.0)
        into_ref[layer, pl.ds(y, 1), :] += term
        return carry

    lax.fori_loop(0, count_ref[0], step, 0)


def receivers_kernel(n, field_ref, lr, ll, la, lc, observed_ref, source_ref):
    source_ref[...] = jnp.zeros(source_ref.shape, F32)
    add_receivers(n, field_ref, source_ref, (lr, ll, la, lc), observed_ref)


def first_adjoint_kernel(n, p_ref, q_ref, lr, ll, la, lc, observed_ref, a_ref, half_ref):
    a_ref[...] = q_ref[...]
    add_receivers(n, p_ref, a_ref, (lr, ll, la, lc), observed_ref)
    layers, width, _ = half_ref.shape

    @pl.loop(0, width // 16)
    def _(j):
        at = pl.multiple_of(16 * j, 16)
        for l in range(layers):
            half_ref[l, pl.ds(at, 16), :] = a_ref[l, pl.ds(at + PAD, 16), :].astype(BF16)


def log_kernel(den_ref, log_ref, s2_ref, s3_ref):
    layers, width, depth = den_ref.shape
    zero_pads(log_ref)

    @pl.loop(0, width // 16)
    def _(j):
        at = pl.multiple_of(16 * j, 16)
        for l in range(layers):
            log_ref[l, pl.ds(at + PAD, 16), :] = jnp.log(den_ref[l, pl.ds(at, 16), :].astype(F32))

    masks = z_masks(8, depth)

    @pl.loop(0, width // 8)
    def _(j):
        at = pl.multiple_of(8 * j, 8)
        for l in range(layers):
            s2_ref[l, pl.ds(at, 8), :] = weighted(y_pairs(log_ref, l, at + PAD, 8))[1]
            s3_ref[l, pl.ds(at, 8), :] = weighted(z_pairs(log_ref[l, pl.ds(at + PAD, 8), :], masks))[1]


def slope_x_kernel(flags_ref, log_ref, on_ref, off_ref, vel_ref, s1_ref, scale_ref):
    layers, width, _ = s1_ref.shape
    even = flags_ref[0] == 1
    valid = flags_ref[1] == 1

    @pl.loop(0, width // 16)
    def _(j):
        at = pl.multiple_of(16 * j, 16)
        rows = pl.ds(at, 16)
        own = [log_ref[l, pl.ds(at + PAD, 16), :] for l in range(layers)]
        on = [jnp.log(on_ref[l, rows, :].astype(F32)) for l in range(layers)]
        off = [jnp.log(jnp.where(valid, off_ref[l, rows, :].astype(F32), 1.0)) for l in range(layers)]
        low = [jnp.where(even, b, a) for a, b in zip(on, off)]
        high = [jnp.where(even, a, b) for a, b in zip(on, off)]
        values = low[layers - 4 :] + own + high[:4]
        for l in range(layers):
            s1_ref[l, rows, :] = weighted(x_pairs(values, l))[1]
            v = vel_ref[l, rows, :].astype(F32)
            scale_ref[l, rows, :] = SPEED * v * v


def yz_terms(f_ref, s2_ref, s3_ref, l, at, masks):
    f = f_ref[l, pl.ds(at + PAD, 8), :]
    lap_y, d_y = weighted(y_pairs(f_ref, l, at + PAD, 8))
    lap_z, d_z = weighted(z_pairs(f, masks))
    rows = pl.ds(at, 8)
    part = (3.0 * SECOND[0]) * f + lap_y + lap_z
    part = part - (s2_ref[l, rows, :] * d_y + s3_ref[l, rows, :] * d_z)
    return f, part, d_y, d_z


def forward_yz_kernel(f_ref, s2_ref, s3_ref, part_ref, dy_ref, dz_ref):
    layers, width, depth = part_ref.shape
    masks = z_masks(8, depth)

    @pl.loop(0, width // 8)
    def _(j):
        at = pl.multiple_of(8 * j, 8)
        rows = pl.ds(at, 8)
        for l in range(layers):
            f, part, d_y, d_z = yz_terms(f_ref, s2_ref, s3_ref, l, at, masks)
            part_ref[l, rows, :] = part
            dy_ref[l, rows, :] = d_y
            dz_ref[l, rows, :] = d_z


def forward_x_kernel(
    flags_ref, f_ref, on_ref, off_ref, part_ref, s1_ref, scale_ref, before_ref,
    dx_ref, applied_ref, next_ref, half_ref,
):
    layers, width, _ = part_ref.shape
    zero_pads(next_ref)
    shift = before_ref.shape[1] != width

    @pl.loop(0, width // 16)
    def _(j):
        at = pl.multiple_of(16 * j, 16)
        rows = pl.ds(at, 16)
        wide = pl.ds(at + PAD, 16)
        own = [f_ref[l, wide, :] for l in range(layers)]
        values = x_values(flags_ref, own, on_ref, off_ref, rows)
        for l in range(layers):
            lap, d_x = weighted(x_pairs(values, l))
            applied = part_ref[l, rows, :] + (lap - s1_ref[l, rows, :] * d_x)
            before = before_ref[l, wide if shift else rows, :]
            later = 2.0 * own[l] - before + scale_ref[l, rows, :] * applied
            dx_ref[l, rows, :] = d_x
            applied_ref[l, rows, :] = applied
            next_ref[l, wide, :] = later
            half_ref[l, rows, :] = later.astype(BF16)


def adjoint_yz_kernel(
    first, f_ref, s2_ref, s3_ref, fdy_ref, fdz_ref, fapplied_ref, *refs,
):
    if first:
        part_ref, vel_ref, den_ref = refs
    else:
        vel_in, den_in, part_ref, vel_ref, den_ref = refs
    layers, width, depth = part_ref.shape
    masks = z_masks(8, depth)

    @pl.loop(0, width // 8)
    def _(j):
        at = pl.multiple_of(8 * j, 8)
        rows = pl.ds(at, 8)
        for l in range(layers):
            f, part, d_y, d_z = yz_terms(f_ref, s2_ref, s3_ref, l, at, masks)
            part_ref[l, rows, :] = part
            sum_vel = f * fapplied_ref[l, rows, :]
            sum_den = d_y * fdy_ref[l, rows, :] + d_z * fdz_ref[l, rows, :]
            if not first:
                sum_vel = vel_in[l, rows, :] + sum_vel
                sum_den = den_in[l, rows, :] + sum_den
            vel_ref[l, rows, :] = sum_vel
            den_ref[l, rows, :] = sum_den


def adjoint_x_kernel(
    last, flags_ref, f_ref, on_ref, off_ref, part_ref, s1_ref, scale_ref, before_ref,
    source_ref, fdx_ref, den_in, *refs,
):
    if last:
        vel_in, fapplied_ref, vmodel_ref, q_ref, a_ref, half_ref, den_ref, shot_ref = refs
    else:
        q_ref, a_ref, half_ref, den_ref = refs
    layers, width, _ = part_ref.shape
    zero_pads(a_ref)
    shift = before_ref.shape[1] != width

    @pl.loop(0, width // 16)
    def _(j):
        at = pl.multiple_of(16 * j, 16)
        rows = pl.ds(at, 16)
        wide = pl.ds(at + PAD, 16)
        own = [f_ref[l, wide, :] for l in range(layers)]
        values = x_values(flags_ref, own, on_ref, off_ref, rows)
        for l in range(layers):
            lap, d_x = weighted(x_pairs(values, l))
            applied = part_ref[l, rows, :] + (lap - s1_ref[l, rows, :] * d_x)
            before = before_ref[l, wide if shift else rows, :]
            later = 2.0 * own[l] - before + scale_ref[l, rows, :] * applied
            if not last:
                q_ref[l, rows, :] = later
            adjoint = later + source_ref[l, wide, :]
            a_ref[l, wide, :] = adjoint
            half_ref[l, rows, :] = adjoint.astype(BF16)
            den_ref[l, rows, :] = den_in[l, rows, :] + d_x * fdx_ref[l, rows, :]
            if last:
                total = vel_in[l, rows, :] + adjoint * fapplied_ref[l, rows, :]
                v = vmodel_ref[l, rows, :].astype(F32)
                shot_ref[l, rows, :] = ((2.0 * SPEED) * v * total).astype(BF16)
    if last:
        q_ref[...] = jnp.zeros(q_ref.shape, F32)


def last_yz_kernel(f_ref, fdy_ref, fdz_ref, den_in, den_ref):
    layers, width, depth = den_ref.shape
    masks = z_masks(8, depth)

    @pl.loop(0, width // 8)
    def _(j):
        at = pl.multiple_of(8 * j, 8)
        rows = pl.ds(at, 8)
        for l in range(layers):
            d_y = weighted(y_pairs(f_ref, l, at + PAD, 8))[1]
            d_z = weighted(z_pairs(f_ref[l, pl.ds(at + PAD, 8), :], masks))[1]
            den_ref[l, rows, :] = den_in[l, rows, :] + (
                d_y * fdy_ref[l, rows, :] + d_z * fdz_ref[l, rows, :]
            )


def last_x_kernel(flags_ref, f_ref, on_ref, off_ref, fdx_ref, den_in, scale_ref, dmodel_ref, shot_ref):
    layers, width, _ = shot_ref.shape

    @pl.loop(0, width // 16)
    def _(j):
        at = pl.multiple_of(16 * j, 16)
        rows = pl.ds(at, 16)
        own = [f_ref[l, pl.ds(at + PAD, 16), :] for l in range(layers)]
        values = x_values(flags_ref, own, on_ref, off_ref, rows)
        for l in range(layers):
            d_x = weighted(x_pairs(values, l))[1]
            total = den_in[l, rows, :] + d_x * fdx_ref[l, rows, :]
            density = dmodel_ref[l, rows, :].astype(F32)
            shot_ref[l, rows, :] = (scale_ref[l, rows, :] / density * total).astype(BF16)


def swap_over(axis, count, bit, value):
    return lax.ppermute(value, axis, [(i, i ^ bit) for i in range(count)])


def beside(half):
    groups, count = lax.axis_size("shot"), lax.axis_size("sub")
    on = lax.ppermute(half, "sub", [(i, i ^ 1) for i in range(count)])
    pairs = []
    for s in range(groups):
        for i in range(1, count - 1, 2):
            pairs += [(s * count + i, s * count + i + 1), (s * count + i + 1, s * count + i)]
        if groups % 2 == 0:
            for i in (0, count - 1):
                pairs.append((s * count + i, (s ^ 1) * count + i))
    off = lax.ppermute(half, ("shot", "sub"), pairs)
    return on, off


def bits_of(groups):
    return [1 << k for k in range(groups.bit_length() - 1)]


def fetch(tile, wanted_all, me, bits):
    groups = wanted_all.shape[0]
    held = [(0, tile)]
    for bit in bits[:-1]:
        block = jnp.concatenate([t for _, t in held], axis=0) if len(held) > 1 else held[0][1]
        got = swap_over("shot", groups, bit, block)
        size = tile.shape[0]
        held = held + [
            (offset ^ bit, lax.slice_in_dim(got, n * size, (n + 1) * size, axis=0))
            for n, (offset, _) in enumerate(held)
        ]
    bit = bits[-1]

    def pick(row):
        out = held[0][1]
        for offset, t in held[1:]:
            out = jnp.where(row == (me ^ offset), t, out)
        return out

    far = swap_over("shot", groups, bit, pick(wanted_all[me ^ bit]))
    mine = wanted_all[me]
    return jnp.where((mine & bit) == (me & bit), pick(mine), far)


def give_back(tile, wanted_all, me, bits):
    groups = wanted_all.shape[0]
    mine, bit = wanted_all[me], bits[0]
    got = swap_over("shot", groups, bit, tile)
    parts = [(mine, tile), (wanted_all[me ^ bit], got)]

    def bucket(row):
        total = None
        for target, t in parts:
            term = jnp.where(target == row, t, jnp.zeros_like(t)).astype(F32)
            total = term if total is None else total + term
        return total

    offsets = [0]
    for b in reversed(bits[1:]):
        offsets = offsets + [o ^ b for o in offsets]
    sums = {o: bucket(me ^ o) for o in offsets}
    for b in bits[1:]:
        away = [o for o in sums if o & b]
        got = swap_over(
            "shot", groups, b, jnp.stack([sums[o].astype(BF16) for o in away], axis=0)
        )
        kept = [o ^ b for o in away]
        sums = {o: sums[o] + got[n].astype(F32) for n, o in enumerate(kept)}
    return sums[0]


def split_fetch(tile, wanted_all, me, groups):
    bits = bits_of(groups)
    layers = tile.shape[0] // 2
    return jnp.concatenate(
        [
            fetch(tile[:layers], wanted_all, me, bits),
            fetch(tile[layers:], wanted_all, me, bits[::-1]),
        ],
        axis=0,
    )


def split_give_back(tile, wanted_all, me, groups):
    bits = bits_of(groups)
    layers = tile.shape[0] // 2
    return jnp.concatenate(
        [
            give_back(tile[:layers], wanted_all, me, bits),
            give_back(tile[layers:], wanted_all, me, bits[::-1]),
        ],
        axis=0,
    )


def body(vel_model, den_model, cover, receivers, observed, p_now, p_before, q_now, q_before):
    me = lax.axis_index("shot")
    column = lax.axis_index("sub")
    groups, columns = lax.axis_size("shot"), lax.axis_size("sub")
    layers, width, depth = p_now.shape[1:]
    tall = width + 2 * PAD
    narrow, padded = ((layers, width, depth), F32), ((layers, tall, depth), F32)
    half = ((layers, width, depth), BF16)
    wanted_all = cover[:, column]

    even = (column & 1) == 0
    valid = (column > 0) & (column < columns - 1)
    flags = jnp.stack([even, valid]).astype(jnp.int32)

    den = split_fetch(den_model[0], wanted_all, me, groups)
    vel = split_fetch(vel_model[0], wanted_all, me, groups)

    p, q, p_half, q_half = call(prepare_kernel, [padded, padded, half, half], [p_now[0], q_now[0]], [VM] * 2)

    cells = layers * width * depth
    local = receivers[0] - column * cells
    inside = (local >= 0) & (local < cells)
    line = local // depth
    row = jnp.where(inside, line + (2 * PAD) * (line // width) + PAD, -1)
    lane = local & (depth - 1) if depth & (depth - 1) == 0 else local % depth
    n_rec = row.shape[0]
    ints = ((n_rec,), jnp.int32)
    lists = call(
        list_kernel, [ints, ints, ints, ((1,), jnp.int32)], [row, lane], [SM, SM], [SM] * 4
    )
    seen = observed[0]
    list_specs = [SM] * 5

    log_den, s2, s3 = call(log_kernel, [padded, narrow, narrow], [den], [VM])
    den_on, den_off = beside(den)
    s1, scale = call(
        slope_x_kernel, [narrow, narrow], [flags, log_den, den_on, den_off, vel], [SM] + [VM] * 4
    )

    stored, sources = [], []
    before = p_before[0]
    for step in range(ITERS):
        on, off = beside(p_half)
        part, d_y, d_z = call(forward_yz_kernel, [narrow] * 3, [p, s2, s3], [VM] * 3)
        if step > 0:
            sources += call(
                lambda *refs, n=step - 1: receivers_kernel(n, *refs),
                [padded], [p, *lists, seen], [VM] + list_specs,
            )
        d_x, applied, later, p_half = call(
            forward_x_kernel, [narrow, narrow, padded, half],
            [flags, p, on, off, part, s1, scale, before], [SM] + [VM] * 7,
        )
        stored.append((applied, d_x, d_y, d_z))
        before, p = p, later

    a, a_half = call(
        lambda *refs: first_adjoint_kernel(ITERS - 1, *refs),
        [padded, half], [p, q, *lists, seen], [VM, VM] + list_specs,
    )
    before, current = q_before[0], q
    sums = ()
    for step in range(ITERS - 1):
        f_applied, f_dx, f_dy, f_dz = stored[ITERS - 1 - step]
        last = step == ITERS - 2
        on, off = beside(a_half)
        part, sum_vel, sum_den = call(
            lambda *refs, first=step == 0: adjoint_yz_kernel(first, *refs),
            [narrow] * 3, [a, s2, s3, f_dy, f_dz, f_applied, *sums], [VM] * (6 + len(sums)),
        )
        extra = [sum_vel, stored[0][0], vel] if last else []
        later, a, a_half, sum_den, *shot = call(
            lambda *refs, last=last: adjoint_x_kernel(last, *refs),
            [((8, 128), F32) if last else narrow, padded, half, narrow] + ([half] if last else []),
            [flags, a, on, off, part, s1, scale, before, sources[ITERS - 2 - step], f_dx, sum_den, *extra],
            [SM] + [VM] * (10 + len(extra)),
        )
        before, current = current, later
        sums = (sum_vel, sum_den)
    shot_vel = shot[0]
    _, f_dx, f_dy, f_dz = stored[0]
    on, off = beside(a_half)
    grad_vel = split_give_back(shot_vel, wanted_all, me, groups)
    (sum_den,) = call(last_yz_kernel, [narrow], [a, f_dy, f_dz, sum_den], [VM] * 4)
    (shot_den,) = call(
        last_x_kernel, [half], [flags, a, on, off, f_dx, sum_den, scale, den], [SM] + [VM] * 7
    )
    grad_den = split_give_back(shot_den, wanted_all, me, groups)
    return grad_vel[None], grad_den[None]


def solution(mesh):
    return jax.shard_map(
        body,
        mesh=mesh,
        in_specs=(
            P("shot", "sub", None, None),
            P("shot", "sub", None, None),
            P(),
            P("shot", None),
            P("shot", None, None),
            P("shot", "sub", None, None),
            P("shot", "sub", None, None),
            P("shot", "sub", None, None),
            P("shot", "sub", None, None),
        ),
        out_specs=(P("shot", "sub", None, None), P("shot", "sub", None, None)),
        check_vma=False,
    )
```

```python
import math

import jax
import jax.numpy as jnp
import numpy as np
from jax import lax
from jax.experimental import pallas as pl
from jax.experimental.pallas import tpu as pltpu
from jax.sharding import PartitionSpec as P

ITERS = 4
SECOND = (-205.0 / 72.0, 8.0 / 5.0, -1.0 / 5.0, 8.0 / 315.0, -1.0 / 560.0)
FIRST = (4.0 / 5.0, -1.0 / 5.0, 4.0 / 105.0, -1.0 / 280.0)
SPEED = 0.15
PAD = 8
UNROLL = 4
F32, BF16 = jnp.float32, jnp.bfloat16
VMEM_LIMIT = 4 << 20

VM = pl.BlockSpec(memory_space=pltpu.VMEM)
SM = pl.BlockSpec(memory_space=pltpu.SMEM)


def call(kernel, outs, ins, specs, out_specs=None, scratch=(), flops=0):
    outs = tuple(jax.ShapeDtypeStruct(shape, dtype) for shape, dtype in outs)
    moved_bytes = sum(math.prod(x.shape) * x.dtype.itemsize for x in (*ins, *outs))
    return pl.pallas_call(
        kernel,
        out_shape=outs,
        in_specs=list(specs),
        out_specs=tuple(out_specs or [VM] * len(outs)),
        scratch_shapes=list(scratch),
        cost_estimate=pl.CostEstimate(flops=flops, bytes_accessed=moved_bytes, transcendentals=0),
        compiler_params=pltpu.CompilerParams(vmem_limit_bytes=VMEM_LIMIT),
    )(*ins)


def weighted(pairs):
    lap, first = None, None
    for m, (ahead, behind) in enumerate(pairs, 1):
        s = SECOND[m] * (ahead + behind)
        t = FIRST[m - 1] * (ahead - behind)
        lap = s if lap is None else lap + s
        first = t if first is None else first + t
    return lap, first


def y_pairs(ref, layer, row, rows):
    return [
        (ref[layer, pl.ds(row + m, rows), :], ref[layer, pl.ds(row - m, rows), :])
        for m in range(1, 5)
    ]


def z_matrix(depth):
    both = np.zeros((depth, 2 * depth), np.float64)
    for out in range(depth):
        for m in range(1, 5):
            for source, sign in ((out + m, 1.0), (out - m, -1.0)):
                if 0 <= source < depth:
                    both[source, out] += SECOND[m]
                    both[source, depth + out] += sign * FIRST[m - 1]
    high = both.astype(np.float32).astype(jnp.bfloat16)
    low = (both - high.astype(np.float64)).astype(np.float32).astype(jnp.bfloat16)
    return jnp.asarray(np.concatenate([high, high, low], axis=0))


def z_terms(f_ref, matrix_ref, z_ref):
    layers, width, _ = z_ref.shape
    for l in range(layers):
        f = f_ref[l, pl.ds(PAD, width), :]
        high = f.astype(BF16)
        low = (f - high.astype(F32)).astype(BF16)
        split = jnp.concatenate([high, low, high], axis=1)
        z_ref[l, :, :] = jnp.dot(split, matrix_ref[...], preferred_element_type=F32)


def where_am_i():
    column, columns = lax.axis_index("sub"), lax.axis_size("sub")
    even = (column & 1) == 0
    valid = jnp.logical_and(column > 0, column < columns - 1)
    return even, valid


def x_values(own, on_ref, off_ref, rows):
    even, valid = where_am_i()
    count = len(own)
    on = [on_ref[l, rows, :].astype(F32) for l in range(count)]
    off = [jnp.where(valid, off_ref[l, rows, :].astype(F32), 0.0) for l in range(count)]
    low = [jnp.where(even, b, a) for a, b in zip(on, off)]
    high = [jnp.where(even, a, b) for a, b in zip(on, off)]
    return low[count - 4 :] + own + high[:4]


def x_pairs(values, layer):
    return [(values[4 + layer + m], values[4 + layer - m]) for m in range(1, 5)]


def zero_pads(ref):
    layers, tall, depth = ref.shape
    zeros = jnp.zeros((PAD, depth), F32)
    for l in range(layers):
        ref[l, pl.ds(0, PAD), :] = zeros
        ref[l, pl.ds(tall - PAD, PAD), :] = zeros


def prepare_kernel(p_ref, q_ref, pw_ref, qw_ref, ph_ref, qh_ref):
    layers, width, _ = p_ref.shape
    for src, wide, half in ((p_ref, pw_ref, ph_ref), (q_ref, qw_ref, qh_ref)):
        zero_pads(wide)

        @pl.loop(0, width // 16)
        def _(j, src=src, wide=wide, half=half):
            at = pl.multiple_of(16 * j, 16)
            for l in range(layers):
                v = src[l, pl.ds(at, 16), :]
                wide[l, pl.ds(at + PAD, 16), :] = v
                half[l, pl.ds(at, 16), :] = v.astype(BF16)


def list_kernel(rec_ref, layers, width, depth, list_ref):
    total = rec_ref.shape[1]
    cells = layers * width * depth
    first = lax.axis_index("sub") * cells

    def step(i, count):
        local = rec_ref[0, i] - first
        inside = jnp.logical_and(local >= 0, local < cells)
        skip = jnp.int32(PAD * depth)
        for l in range(1, layers):
            skip += jnp.where(local >= l * width * depth, 2 * PAD * depth, 0)
        list_ref[count] = local + skip
        list_ref[total + UNROLL + count] = i
        return count + jnp.where(inside, 1, 0)

    count = lax.fori_loop(0, total, step, jnp.int32(0))
    for n in range(UNROLL):
        list_ref[count + n] = -1
        list_ref[total + UNROLL + count + n] = 0
    list_ref[2 * (total + UNROLL)] = count


def add_receivers(n, field_ref, into_ref, list_ref, observed_ref):
    depth = field_ref.shape[1]
    lane = lax.broadcasted_iota(jnp.int32, (1, depth), 1)
    start = (list_ref.shape[0] - 1) // 2
    count = list_ref[2 * start]

    @pl.loop(0, (count + UNROLL - 1) // UNROLL)
    def _(c):
        rows, terms = [], []
        for k in range(UNROLL):
            at = list_ref[c * UNROLL + k]
            real = at >= 0
            row = jnp.where(real, lax.div(at, depth), 0)
            spot = jnp.where(real, lax.rem(at, depth), depth)
            seen = observed_ref[n, list_ref[start + c * UNROLL + k]]
            rows.append(row)
            terms.append(jnp.where(lane == spot, field_ref[pl.ds(row, 1), :] - seen, 0.0))
        for row, term in zip(rows, terms):
            into_ref[pl.ds(row, 1), :] += term


def receivers_kernel(n, field_ref, list_ref, observed_ref, source_ref):
    source_ref[...] = jnp.zeros(source_ref.shape, F32)
    add_receivers(n, field_ref, source_ref, list_ref, observed_ref)


def first_adjoint_kernel(n, p_ref, q_ref, list_ref, observed_ref, a_ref, half_ref):
    a_ref[...] = q_ref[...]
    add_receivers(n, p_ref, a_ref, list_ref, observed_ref)
    layers, width, _ = half_ref.shape
    tall = width + 2 * PAD

    @pl.loop(0, width // 16)
    def _(j):
        at = pl.multiple_of(16 * j, 16)
        for l in range(layers):
            from_row = pl.multiple_of(at + l * tall + PAD, 8)
            half_ref[l, pl.ds(at, 16), :] = a_ref[pl.ds(from_row, 16), :].astype(BF16)


def log_kernel(den_ref, matrix_ref, log_ref, s2_ref, s3_ref, z_ref):
    layers, width, depth = den_ref.shape
    zero_pads(log_ref)

    @pl.loop(0, width // 16)
    def _(j):
        at = pl.multiple_of(16 * j, 16)
        for l in range(layers):
            log_ref[l, pl.ds(at + PAD, 16), :] = jnp.log(den_ref[l, pl.ds(at, 16), :].astype(F32))

    z_terms(log_ref, matrix_ref, z_ref)

    @pl.loop(0, width // 8)
    def _(j):
        at = pl.multiple_of(8 * j, 8)
        for l in range(layers):
            s2_ref[l, pl.ds(at, 8), :] = weighted(y_pairs(log_ref, l, at + PAD, 8))[1]
            s3_ref[l, pl.ds(at, 8), :] = z_ref[l, pl.ds(at, 8), pl.ds(depth, depth)]


def slope_x_kernel(log_ref, on_ref, off_ref, vel_ref, s1_ref, scale_ref):
    layers, width, _ = s1_ref.shape
    even, valid = where_am_i()

    @pl.loop(0, width // 16)
    def _(j):
        at = pl.multiple_of(16 * j, 16)
        rows = pl.ds(at, 16)
        own = [log_ref[l, pl.ds(at + PAD, 16), :] for l in range(layers)]
        on = [jnp.log(on_ref[l, rows, :].astype(F32)) for l in range(layers)]
        off = [jnp.log(jnp.where(valid, off_ref[l, rows, :].astype(F32), 1.0)) for l in range(layers)]
        low = [jnp.where(even, b, a) for a, b in zip(on, off)]
        high = [jnp.where(even, a, b) for a, b in zip(on, off)]
        values = low[layers - 4 :] + own + high[:4]
        for l in range(layers):
            s1_ref[l, rows, :] = weighted(x_pairs(values, l))[1]
            v = vel_ref[l, rows, :].astype(F32)
            scale_ref[l, rows, :] = SPEED * v * v


def yz_terms(f_ref, s2_ref, s3_ref, z_ref, l, at):
    f = f_ref[l, pl.ds(at + PAD, 8), :]
    lap_y, d_y = weighted(y_pairs(f_ref, l, at + PAD, 8))
    rows, depth = pl.ds(at, 8), f.shape[1]
    lap_z, d_z = z_ref[l, rows, pl.ds(0, depth)], z_ref[l, rows, pl.ds(depth, depth)]
    part = (3.0 * SECOND[0]) * f + lap_y + lap_z
    part = part - (s2_ref[l, rows, :] * d_y + s3_ref[l, rows, :] * d_z)
    return f, part, d_y, d_z


def forward_yz_kernel(f_ref, s2_ref, s3_ref, matrix_ref, part_ref, dy_ref, dz_ref, z_ref):
    layers, width, depth = part_ref.shape
    z_terms(f_ref, matrix_ref, z_ref)

    @pl.loop(0, width // 8)
    def _(j):
        at = pl.multiple_of(8 * j, 8)
        rows = pl.ds(at, 8)
        for l in range(layers):
            f, part, d_y, d_z = yz_terms(f_ref, s2_ref, s3_ref, z_ref, l, at)
            part_ref[l, rows, :] = part
            dy_ref[l, rows, :] = d_y
            dz_ref[l, rows, :] = d_z


def forward_x_kernel(
    f_ref, on_ref, off_ref, part_ref, s1_ref, scale_ref, before_ref,
    dx_ref, applied_ref, next_ref, half_ref,
):
    layers, width, _ = part_ref.shape
    zero_pads(next_ref)
    shift = before_ref.shape[1] != width

    @pl.loop(0, width // 16)
    def _(j):
        at = pl.multiple_of(16 * j, 16)
        rows = pl.ds(at, 16)
        wide = pl.ds(at + PAD, 16)
        own = [f_ref[l, wide, :] for l in range(layers)]
        values = x_values(own, on_ref, off_ref, rows)
        for l in range(layers):
            lap, d_x = weighted(x_pairs(values, l))
            applied = part_ref[l, rows, :] + (lap - s1_ref[l, rows, :] * d_x)
            before = before_ref[l, wide if shift else rows, :]
            later = 2.0 * own[l] - before + scale_ref[l, rows, :] * applied
            dx_ref[l, rows, :] = d_x
            applied_ref[l, rows, :] = applied
            next_ref[l, wide, :] = later
            half_ref[l, rows, :] = later.astype(BF16)


def adjoint_yz_kernel(
    first, f_ref, s2_ref, s3_ref, matrix_ref, fdy_ref, fdz_ref, fapplied_ref, *refs,
):
    if first:
        part_ref, vel_ref, den_ref, z_ref = refs
    else:
        vel_in, den_in, part_ref, vel_ref, den_ref, z_ref = refs
    layers, width, depth = part_ref.shape
    z_terms(f_ref, matrix_ref, z_ref)

    @pl.loop(0, width // 8)
    def _(j):
        at = pl.multiple_of(8 * j, 8)
        rows = pl.ds(at, 8)
        for l in range(layers):
            f, part, d_y, d_z = yz_terms(f_ref, s2_ref, s3_ref, z_ref, l, at)
            part_ref[l, rows, :] = part
            sum_vel = f * fapplied_ref[l, rows, :]
            sum_den = d_y * fdy_ref[l, rows, :] + d_z * fdz_ref[l, rows, :]
            if not first:
                sum_vel = vel_in[l, rows, :] + sum_vel
                sum_den = den_in[l, rows, :] + sum_den
            vel_ref[l, rows, :] = sum_vel
            den_ref[l, rows, :] = sum_den


def adjoint_x_kernel(
    last, f_ref, on_ref, off_ref, part_ref, s1_ref, scale_ref, before_ref,
    source_ref, fdx_ref, den_in, *refs,
):
    if last:
        vel_in, fapplied_ref, vmodel_ref, q_ref, a_ref, half_ref, den_ref, shot_ref = refs
    else:
        q_ref, a_ref, half_ref, den_ref = refs
    layers, width, _ = part_ref.shape
    zero_pads(a_ref)
    shift = before_ref.shape[1] != width

    @pl.loop(0, width // 16)
    def _(j):
        at = pl.multiple_of(16 * j, 16)
        rows = pl.ds(at, 16)
        wide = pl.ds(at + PAD, 16)
        own = [f_ref[l, wide, :] for l in range(layers)]
        values = x_values(own, on_ref, off_ref, rows)
        for l in range(layers):
            lap, d_x = weighted(x_pairs(values, l))
            applied = part_ref[l, rows, :] + (lap - s1_ref[l, rows, :] * d_x)
            before = before_ref[l, wide if shift else rows, :]
            later = 2.0 * own[l] - before + scale_ref[l, rows, :] * applied
            if not last:
                q_ref[l, rows, :] = later
            adjoint = later + source_ref[l, wide, :]
            a_ref[l, wide, :] = adjoint
            half_ref[l, rows, :] = adjoint.astype(BF16)
            den_ref[l, rows, :] = den_in[l, rows, :] + d_x * fdx_ref[l, rows, :]
            if last:
                total = vel_in[l, rows, :] + adjoint * fapplied_ref[l, rows, :]
                v = vmodel_ref[l, rows, :].astype(F32)
                shot_ref[l, rows, :] = ((2.0 * SPEED) * v * total).astype(BF16)
    if last:
        q_ref[...] = jnp.zeros(q_ref.shape, F32)


def last_yz_kernel(f_ref, matrix_ref, fdy_ref, fdz_ref, den_in, den_ref, z_ref):
    layers, width, depth = den_ref.shape
    z_terms(f_ref, matrix_ref, z_ref)

    @pl.loop(0, width // 8)
    def _(j):
        at = pl.multiple_of(8 * j, 8)
        rows = pl.ds(at, 8)
        for l in range(layers):
            d_y = weighted(y_pairs(f_ref, l, at + PAD, 8))[1]
            d_z = z_ref[l, rows, pl.ds(depth, depth)]
            den_ref[l, rows, :] = den_in[l, rows, :] + (
                d_y * fdy_ref[l, rows, :] + d_z * fdz_ref[l, rows, :]
            )


def last_x_kernel(f_ref, on_ref, off_ref, fdx_ref, den_in, scale_ref, dmodel_ref, shot_ref):
    layers, width, _ = shot_ref.shape

    @pl.loop(0, width // 16)
    def _(j):
        at = pl.multiple_of(16 * j, 16)
        rows = pl.ds(at, 16)
        own = [f_ref[l, pl.ds(at + PAD, 16), :] for l in range(layers)]
        values = x_values(own, on_ref, off_ref, rows)
        for l in range(layers):
            d_x = weighted(x_pairs(values, l))[1]
            total = den_in[l, rows, :] + d_x * fdx_ref[l, rows, :]
            density = dmodel_ref[l, rows, :].astype(F32)
            shot_ref[l, rows, :] = (scale_ref[l, rows, :] / density * total).astype(BF16)


def swap_over(axis, count, bit, value):
    return lax.ppermute(value, axis, [(i, i ^ bit) for i in range(count)])


def beside(half):
    groups, count = lax.axis_size("shot"), lax.axis_size("sub")
    on = lax.ppermute(half, "sub", [(i, i ^ 1) for i in range(count)])
    pairs = []
    for s in range(groups):
        for i in range(1, count - 1, 2):
            pairs += [(s * count + i, s * count + i + 1), (s * count + i + 1, s * count + i)]
        if groups % 2 == 0:
            for i in (0, count - 1):
                pairs.append((s * count + i, (s ^ 1) * count + i))
    off = lax.ppermute(half, ("shot", "sub"), pairs)
    return on, off


def bits_of(groups):
    return [1 << k for k in range(groups.bit_length() - 1)]


def pick_into(out_ref, spot, held, me, row):
    for offset, ref in held:

        @pl.when(row == (me ^ offset))
        def _(ref=ref):
            if spot is None:
                out_ref[...] = ref[...]
            else:
                out_ref[spot, :, :] = ref[...]


def pick_kernel(offsets, bits, cover_ref, *refs):
    me, column = lax.axis_index("shot"), lax.axis_index("sub")
    outs = refs[-2:]
    count = len(refs) // 2 - 1
    for way in range(2):
        held = list(zip(offsets[way], refs[way * count : (way + 1) * count]))
        pick_into(outs[way], None, held, me, cover_ref[me ^ bits[way], column])


def gather_kernel(offsets, bits, cover_ref, *refs):
    me, column = lax.axis_index("shot"), lax.axis_index("sub")
    out_ref = refs[-1]
    count = (len(refs) - 1) // 2
    mine = cover_ref[me, column]
    layers = out_ref.shape[0] // 2
    for way in range(2):
        *near, far = refs[way * count : (way + 1) * count]
        spot = pl.ds(way * layers, layers)
        pick_into(out_ref, spot, list(zip(offsets[way], near)), me, mine)

        @pl.when((mine & bits[way]) != (me & bits[way]))
        def _(far=far, spot=spot):
            out_ref[spot, :, :] = far[...]


def fetch(tile, cover):
    groups = cover.shape[0]
    layers = tile.shape[0] // 2
    small = (layers, *tile.shape[1:])
    ways = [bits_of(groups), bits_of(groups)[::-1]]
    held = [[tile[:layers]], [tile[layers:]]]
    offsets = [[0], [0]]
    for stage in range(len(ways[0]) - 1):
        for way in range(2):
            bit = ways[way][stage]
            block = jnp.concatenate(held[way], axis=0) if len(held[way]) > 1 else held[way][0]
            got = swap_over("shot", groups, bit, block)
            held[way] = held[way] + [
                lax.slice_in_dim(got, n * layers, (n + 1) * layers, axis=0)
                for n in range(len(held[way]))
            ]
            offsets[way] = offsets[way] + [o ^ bit for o in offsets[way]]
    last = [way[-1] for way in ways]
    count = len(held[0])
    sends = call(
        lambda *refs: pick_kernel(offsets, last, *refs),
        [(small, BF16)] * 2, [cover, *held[0], *held[1]], [SM] + [VM] * (2 * count),
    )
    far = [swap_over("shot", groups, last[way], sends[way]) for way in range(2)]
    (out,) = call(
        lambda *refs: gather_kernel(offsets, last, *refs),
        [(tile.shape, BF16)], [cover, *held[0], far[0], *held[1], far[1]],
        [SM] + [VM] * (2 * count + 2),
    )
    return out


def bucket_kernel(offsets, bits, cover_ref, tile_ref, *refs):
    me, column = lax.axis_index("shot"), lax.axis_index("sub")
    layers = tile_ref.shape[0] // 2
    got, outs = refs[:2], refs[2:]
    mine = cover_ref[me, column]
    for way in range(2):
        theirs = cover_ref[me ^ bits[way], column]
        own_ref = tile_ref.at[pl.ds(way * layers, layers)]
        for n, offset in enumerate(offsets[way]):
            out = outs[way * len(offsets[way]) + n]
            a = jnp.where(mine == (me ^ offset), own_ref[...].astype(F32), 0.0)
            b = jnp.where(theirs == (me ^ offset), got[way][...].astype(F32), 0.0)
            out[...] = (a + b).astype(out.dtype)


def give_back(tile, cover):
    groups = cover.shape[0]
    layers = tile.shape[0] // 2
    small = (layers, *tile.shape[1:])
    ways = [bits_of(groups), bits_of(groups)[::-1]]
    got = [
        swap_over("shot", groups, ways[way][0], tile[way * layers : (way + 1) * layers])
        for way in range(2)
    ]
    offsets, types = [], []
    for way in ways:
        own = [0]
        for b in reversed(way[1:]):
            own = own + [o ^ b for o in own]
        offsets.append(own)
        types += [BF16 if o & way[1] else F32 for o in own]
    sums = call(
        lambda *refs: bucket_kernel(offsets, [way[0] for way in ways], *refs),
        [(small, kind) for kind in types], [cover, tile, *got], [SM] + [VM] * 3,
    )
    parts = []
    for way in range(2):
        count = len(offsets[way])
        left = dict(zip(offsets[way], sums[way * count : (way + 1) * count]))
        for b in ways[way][1:]:
            away = [o for o in left if o & b]
            block = jnp.concatenate([left[o].astype(BF16) for o in away], axis=0)
            came = swap_over("shot", groups, b, block)
            left = {
                o ^ b: left[o ^ b] + came[n * layers : (n + 1) * layers].astype(F32)
                for n, o in enumerate(away)
            }
        parts.append(left[0])
    return jnp.concatenate(parts, axis=0)


def body(vel_model, den_model, cover, receivers, observed, p_now, p_before, q_now, q_before):
    layers, width, depth = p_now.shape[1:]
    tall = width + 2 * PAD
    narrow, padded = ((layers, width, depth), F32), ((layers, tall, depth), F32)
    half, flat = ((layers, width, depth), BF16), ((layers * tall, depth), F32)
    z_scratch = [pltpu.VMEM((layers, width, 2 * depth), F32)]
    matrix = z_matrix(depth)
    seen = observed[0]

    den = fetch(den_model[0], cover)
    vel = fetch(vel_model[0], cover)

    p, q, p_half, q_half = call(prepare_kernel, [padded, padded, half, half], [p_now[0], q_now[0]], [VM] * 2)
    n_rec = receivers.shape[1]
    (lists,) = call(
        lambda rec, out: list_kernel(rec, layers, width, depth, out),
        [((2 * (n_rec + UNROLL) + 1,), jnp.int32)], [receivers], [SM], [SM],
    )
    p, lists = lax.optimization_barrier((p, lists))

    log_den, s2, s3 = call(log_kernel, [padded, narrow, narrow], [den, matrix], [VM] * 2, scratch=z_scratch)
    den_on, den_off = beside(den)
    s1, scale = call(slope_x_kernel, [narrow, narrow], [log_den, den_on, den_off, vel], [VM] * 4)

    stored, sources = [], []
    before = p_before[0]
    for step in range(ITERS):
        on, off = beside(p_half)
        part, d_y, d_z = call(
            forward_yz_kernel, [narrow] * 3, [p, s2, s3, matrix], [VM] * 4, scratch=z_scratch
        )
        if step > 0:
            (source,) = call(
                lambda *refs, n=step - 1: receivers_kernel(n, *refs),
                [flat], [p.reshape(flat[0]), lists, seen], [VM, SM, SM],
            )
            sources.append(source.reshape(padded[0]))
        d_x, applied, later, p_half = call(
            forward_x_kernel, [narrow, narrow, padded, half],
            [p, on, off, part, s1, scale, before], [VM] * 7,
        )
        stored.append((applied, d_x, d_y, d_z))
        before, p = p, later

    a, a_half = call(
        lambda *refs: first_adjoint_kernel(ITERS - 1, *refs),
        [flat, half], [p.reshape(flat[0]), q.reshape(flat[0]), lists, seen], [VM, VM, SM, SM],
    )
    a = a.reshape(padded[0])
    before, current = q_before[0], q
    sums = ()
    for step in range(ITERS - 1):
        f_applied, f_dx, f_dy, f_dz = stored[ITERS - 1 - step]
        last = step == ITERS - 2
        on, off = beside(a_half)
        part, sum_vel, sum_den = call(
            lambda *refs, first=step == 0: adjoint_yz_kernel(first, *refs),
            [narrow] * 3, [a, s2, s3, matrix, f_dy, f_dz, f_applied, *sums], [VM] * (7 + len(sums)),
            scratch=z_scratch,
        )
        extra = [sum_vel, stored[0][0], vel] if last else []
        later, a, a_half, sum_den, *shot = call(
            lambda *refs, last=last: adjoint_x_kernel(last, *refs),
            [((8, 128), F32) if last else narrow, padded, half, narrow] + ([half] if last else []),
            [a, on, off, part, s1, scale, before, sources[ITERS - 2 - step], f_dx, sum_den, *extra],
            [VM] * (10 + len(extra)),
        )
        before, current = current, later
        sums = (sum_vel, sum_den)
    shot_vel = shot[0]
    _, f_dx, f_dy, f_dz = stored[0]
    on, off = beside(a_half)
    grad_vel = give_back(shot_vel, cover)
    (sum_den,) = call(
        last_yz_kernel, [narrow], [a, matrix, f_dy, f_dz, sum_den], [VM] * 5, scratch=z_scratch
    )
    (shot_den,) = call(
        last_x_kernel, [half], [a, on, off, f_dx, sum_den, scale, den], [VM] * 7
    )
    grad_den = give_back(shot_den, cover)
    return grad_vel[None], grad_den[None]


def solution(mesh):
    return jax.shard_map(
        body,
        mesh=mesh,
        in_specs=(
            P("shot", "sub", None, None),
            P("shot", "sub", None, None),
            P(),
            P("shot", None),
            P("shot", None, None),
            P("shot", "sub", None, None),
            P("shot", "sub", None, None),
            P("shot", "sub", None, None),
            P("shot", "sub", None, None),
        ),
        out_specs=(P("shot", "sub", None, None), P("shot", "sub", None, None)),
        check_vma=False,
    )
```

```python
import math

import jax
import jax.numpy as jnp
import numpy as np
from jax import lax
from jax.experimental import pallas as pl
from jax.experimental.pallas import tpu as pltpu
from jax.sharding import PartitionSpec as P

ITERS = 4
SECOND = (-205.0 / 72.0, 8.0 / 5.0, -1.0 / 5.0, 8.0 / 315.0, -1.0 / 560.0)
FIRST = (4.0 / 5.0, -1.0 / 5.0, 4.0 / 105.0, -1.0 / 280.0)
SPEED = 0.15
PAD = 8
PARTS = 2
UNROLL = 4
F32, BF16 = jnp.float32, jnp.bfloat16
VMEM_LIMIT = 4 << 20

VM = pl.BlockSpec(memory_space=pltpu.VMEM)
SM = pl.BlockSpec(memory_space=pltpu.SMEM)


def call(kernel, outs, ins, specs=None, out_specs=None, scratch=(), flops=0, aliases=None):
    outs = tuple(jax.ShapeDtypeStruct(shape, dtype) for shape, dtype in outs)
    moved_bytes = sum(math.prod(x.shape) * x.dtype.itemsize for x in (*ins, *outs))
    return pl.pallas_call(
        kernel,
        out_shape=outs,
        in_specs=list(specs or [VM] * len(ins)),
        out_specs=tuple(out_specs or [VM] * len(outs)),
        scratch_shapes=list(scratch),
        input_output_aliases=aliases or {},
        cost_estimate=pl.CostEstimate(flops=flops, bytes_accessed=moved_bytes, transcendentals=0),
        compiler_params=pltpu.CompilerParams(vmem_limit_bytes=VMEM_LIMIT),
    )(*ins)


def weighted(pairs):
    lap, first = None, None
    for m, (ahead, behind) in enumerate(pairs, 1):
        s = SECOND[m] * (ahead + behind)
        t = FIRST[m - 1] * (ahead - behind)
        lap = s if lap is None else lap + s
        first = t if first is None else first + t
    return lap, first


def y_pairs(ref, layer, row, rows):
    return [
        (ref[layer, pl.ds(row + m, rows), :], ref[layer, pl.ds(row - m, rows), :])
        for m in range(1, 5)
    ]


def z_matrix(depth):
    both = np.zeros((depth, 2 * depth), np.float64)
    for out in range(depth):
        for m in range(1, 5):
            for source, sign in ((out + m, 1.0), (out - m, -1.0)):
                if 0 <= source < depth:
                    both[source, out] += SECOND[m]
                    both[source, depth + out] += sign * FIRST[m - 1]
    high = both.astype(np.float32).astype(jnp.bfloat16)
    low = (both - high.astype(np.float64)).astype(np.float32).astype(jnp.bfloat16)
    return jnp.asarray(np.concatenate([high, high, low], axis=0))


def z_terms(f_ref, matrix_ref, z_ref):
    layers, width, _ = z_ref.shape
    for l in range(layers):
        f = f_ref[l, pl.ds(PAD, width), :]
        high = f.astype(BF16)
        low = (f - high.astype(F32)).astype(BF16)
        split = jnp.concatenate([high, low, high], axis=1)
        z_ref[l, :, :] = jnp.dot(split, matrix_ref[...], preferred_element_type=F32)


def where_am_i():
    column, columns = lax.axis_index("sub"), lax.axis_size("sub")
    even = (column & 1) == 0
    valid = jnp.logical_and(column > 0, column < columns - 1)
    return even, valid


def x_values(own, on_ref, off_ref, rows, off_rows):
    even, valid = where_am_i()
    count = len(own)
    on = [on_ref[l, rows, :].astype(F32) for l in range(count)]
    off = [jnp.where(valid, off_ref[l, off_rows, :].astype(F32), 0.0) for l in range(count)]
    low = [jnp.where(even, b, a) for a, b in zip(on, off)]
    high = [jnp.where(even, a, b) for a, b in zip(on, off)]
    return low[count - 4 :] + own + high[:4]


def part_rows(part, width, off_ref, body):
    size = width // PARTS
    first = part * size
    back = first if off_ref.shape[1] == size else 0

    @pl.loop(0, size // 16)
    def _(j):
        at = pl.multiple_of(first + 16 * j, 16)
        off_at = pl.multiple_of(first - back + 16 * j, 16)
        body(pl.ds(at, 16), pl.ds(off_at, 16), pl.ds(at + PAD, 16), pl.ds(pl.multiple_of(16 * j, 16), 16))


def x_pairs(values, layer):
    return [(values[4 + layer + m], values[4 + layer - m]) for m in range(1, 5)]


def zero_pads(ref):
    layers, tall, depth = ref.shape
    zeros = jnp.zeros((PAD, depth), F32)
    for l in range(layers):
        ref[l, pl.ds(0, PAD), :] = zeros
        ref[l, pl.ds(tall - PAD, PAD), :] = zeros


def prepare_kernel(p_ref, pw_ref, *half_refs):
    layers, width, _ = p_ref.shape
    zero_pads(pw_ref)

    @pl.loop(0, width // 16)
    def _(j):
        at = pl.multiple_of(16 * j, 16)
        for l in range(layers):
            v = p_ref[l, pl.ds(at, 16), :]
            pw_ref[l, pl.ds(at + PAD, 16), :] = v
            for half_ref in half_refs:
                half_ref[l, pl.ds(at, 16), :] = v.astype(BF16)


def list_kernel(rec_ref, layers, width, depth, list_ref):
    total = rec_ref.shape[1]
    cells = layers * width * depth
    first = lax.axis_index("sub") * cells

    def step(i, count):
        local = rec_ref[0, i] - first
        list_ref[count] = i
        inside = jnp.bitwise_or(local, cells - 1 - local) >= 0
        return count + jnp.where(inside, 1, 0)

    count = lax.fori_loop(0, total, step, jnp.int32(0), unroll=8)

    @pl.loop(0, count)
    def _(c):
        i = list_ref[c]
        local = rec_ref[0, i] - first
        skip = jnp.int32(PAD * depth)
        for l in range(1, layers):
            skip += jnp.where(local >= l * width * depth, 2 * PAD * depth, 0)
        list_ref[c] = local + skip
        list_ref[total + UNROLL + c] = i

    for n in range(UNROLL):
        list_ref[count + n] = -1
        list_ref[total + UNROLL + count + n] = 0
    list_ref[2 * (total + UNROLL)] = count


def add_receivers(n, field_ref, into_ref, list_ref, observed_ref):
    depth = field_ref.shape[1]
    lane = lax.broadcasted_iota(jnp.int32, (1, depth), 1)
    start = (list_ref.shape[0] - 1) // 2
    count = list_ref[2 * start]

    @pl.loop(0, (count + UNROLL - 1) // UNROLL)
    def _(c):
        rows, terms = [], []
        for k in range(UNROLL):
            at = list_ref[c * UNROLL + k]
            real = at >= 0
            row = jnp.where(real, lax.div(at, depth), 0)
            spot = jnp.where(real, lax.rem(at, depth), depth)
            seen = observed_ref[n, list_ref[start + c * UNROLL + k]]
            rows.append(row)
            terms.append(jnp.where(lane == spot, field_ref[pl.ds(row, 1), :] - seen, 0.0))
        for row, term in zip(rows, terms):
            into_ref[pl.ds(row, 1), :] += term


def receivers_kernel(n, field_ref, list_ref, observed_ref, source_ref):
    source_ref[...] = jnp.zeros(source_ref.shape, F32)
    add_receivers(n, field_ref, source_ref, list_ref, observed_ref)


def first_adjoint_kernel(n, p_ref, q_ref, list_ref, observed_ref, a_ref, half_ref, *part_refs):
    a_ref[...] = q_ref[...]
    add_receivers(n, p_ref, a_ref, list_ref, observed_ref)
    layers, width, _ = half_ref.shape
    tall = width + 2 * PAD

    for n, part_ref in enumerate(part_refs):
        size = part_ref.shape[1]

        @pl.loop(0, size // 16)
        def _(j, n=n, size=size, part_ref=part_ref):
            at = pl.multiple_of(16 * j, 16)
            for l in range(layers):
                from_row = pl.multiple_of(at + n * size + l * tall + PAD, 8)
                value = a_ref[pl.ds(from_row, 16), :].astype(BF16)
                half_ref[l, pl.ds(pl.multiple_of(at + n * size, 16), 16), :] = value
                part_ref[l, pl.ds(at, 16), :] = value


def log_kernel(den_ref, matrix_ref, log_ref, s2_ref, s3_ref, z_ref):
    layers, width, depth = den_ref.shape
    zero_pads(log_ref)

    @pl.loop(0, width // 16)
    def _(j):
        at = pl.multiple_of(16 * j, 16)
        for l in range(layers):
            log_ref[l, pl.ds(at + PAD, 16), :] = jnp.log(den_ref[l, pl.ds(at, 16), :].astype(F32))

    z_terms(log_ref, matrix_ref, z_ref)

    @pl.loop(0, width // 8)
    def _(j):
        at = pl.multiple_of(8 * j, 8)
        for l in range(layers):
            s2_ref[l, pl.ds(at, 8), :] = weighted(y_pairs(log_ref, l, at + PAD, 8))[1]
            s3_ref[l, pl.ds(at, 8), :] = z_ref[l, pl.ds(at, 8), pl.ds(depth, depth)]


def slope_x_kernel(log_ref, on_ref, off_ref, vel_ref, s1_ref, scale_ref):
    layers, width, _ = s1_ref.shape
    even, valid = where_am_i()

    @pl.loop(0, width // 16)
    def _(j):
        at = pl.multiple_of(16 * j, 16)
        rows = pl.ds(at, 16)
        own = [log_ref[l, pl.ds(at + PAD, 16), :] for l in range(layers)]
        on = [jnp.log(on_ref[l, rows, :].astype(F32)) for l in range(layers)]
        off = [jnp.log(jnp.where(valid, off_ref[l, rows, :].astype(F32), 1.0)) for l in range(layers)]
        low = [jnp.where(even, b, a) for a, b in zip(on, off)]
        high = [jnp.where(even, a, b) for a, b in zip(on, off)]
        values = low[layers - 4 :] + own + high[:4]
        for l in range(layers):
            s1_ref[l, rows, :] = weighted(x_pairs(values, l))[1]
            v = vel_ref[l, rows, :].astype(F32)
            scale_ref[l, rows, :] = SPEED * v * v


def yz_terms(f_ref, s2_ref, s3_ref, z_ref, l, at):
    f = f_ref[l, pl.ds(at + PAD, 8), :]
    lap_y, d_y = weighted(y_pairs(f_ref, l, at + PAD, 8))
    rows, depth = pl.ds(at, 8), f.shape[1]
    lap_z, d_z = z_ref[l, rows, pl.ds(0, depth)], z_ref[l, rows, pl.ds(depth, depth)]
    part = (3.0 * SECOND[0]) * f + lap_y + lap_z
    part = part - (s2_ref[l, rows, :] * d_y + s3_ref[l, rows, :] * d_z)
    return f, part, d_y, d_z


def forward_yz_kernel(f_ref, s2_ref, s3_ref, matrix_ref, part_ref, dy_ref, dz_ref, z_ref):
    layers, width, depth = part_ref.shape
    z_terms(f_ref, matrix_ref, z_ref)

    @pl.loop(0, width // 8)
    def _(j):
        at = pl.multiple_of(8 * j, 8)
        rows = pl.ds(at, 8)
        for l in range(layers):
            f, part, d_y, d_z = yz_terms(f_ref, s2_ref, s3_ref, z_ref, l, at)
            part_ref[l, rows, :] = part
            dy_ref[l, rows, :] = d_y
            dz_ref[l, rows, :] = d_z


def forward_x_kernel(part, f_ref, on_ref, off_ref, part_ref, s1_ref, scale_ref, before_ref, *refs):
    dx_ref, applied_ref, next_ref, half_ref, send_ref = refs[-5:]
    layers, width, _ = part_ref.shape
    shift = before_ref.shape[1] != width
    if part == 0:
        zero_pads(next_ref)

    def body(rows, off_rows, wide, send_rows):
        own = [f_ref[l, wide, :] for l in range(layers)]
        values = x_values(own, on_ref, off_ref, rows, off_rows)
        for l in range(layers):
            lap, d_x = weighted(x_pairs(values, l))
            applied = part_ref[l, rows, :] + (lap - s1_ref[l, rows, :] * d_x)
            before = before_ref[l, wide if shift else rows, :]
            later = 2.0 * own[l] - before + scale_ref[l, rows, :] * applied
            dx_ref[l, rows, :] = d_x
            applied_ref[l, rows, :] = applied
            next_ref[l, wide, :] = later
            narrow = later.astype(BF16)
            half_ref[l, rows, :] = narrow
            send_ref[l, send_rows, :] = narrow

    part_rows(part, width, off_ref, body)


def adjoint_yz_kernel(
    first, f_ref, s2_ref, s3_ref, matrix_ref, fdy_ref, fdz_ref, fapplied_ref, *refs,
):
    if first:
        part_ref, vel_ref, den_ref, z_ref = refs
    else:
        vel_in, den_in, part_ref, vel_ref, den_ref, z_ref = refs
    layers, width, depth = part_ref.shape
    z_terms(f_ref, matrix_ref, z_ref)

    @pl.loop(0, width // 8)
    def _(j):
        at = pl.multiple_of(8 * j, 8)
        rows = pl.ds(at, 8)
        for l in range(layers):
            f, part, d_y, d_z = yz_terms(f_ref, s2_ref, s3_ref, z_ref, l, at)
            part_ref[l, rows, :] = part
            sum_vel = f * fapplied_ref[l, rows, :]
            sum_den = d_y * fdy_ref[l, rows, :] + d_z * fdz_ref[l, rows, :]
            if not first:
                sum_vel = vel_in[l, rows, :] + sum_vel
                sum_den = den_in[l, rows, :] + sum_den
            vel_ref[l, rows, :] = sum_vel
            den_ref[l, rows, :] = sum_den


def adjoint_x_kernel(
    part, last, f_ref, on_ref, off_ref, part_ref, s1_ref, scale_ref, before_ref,
    source_ref, fdx_ref, den_in, *refs,
):
    if last:
        vel_in, fapplied_ref, vmodel_ref = refs[:3]
        a_ref, half_ref, den_ref, send_ref, shot_ref = refs[-5:]
    else:
        a_ref, half_ref, den_ref, q_ref, send_ref = refs[-5:]
    layers, width, _ = part_ref.shape
    shift = before_ref.shape[1] != width
    if part == 0:
        zero_pads(a_ref)

    def body(rows, off_rows, wide, send_rows):
        own = [f_ref[l, wide, :] for l in range(layers)]
        values = x_values(own, on_ref, off_ref, rows, off_rows)
        for l in range(layers):
            lap, d_x = weighted(x_pairs(values, l))
            applied = part_ref[l, rows, :] + (lap - s1_ref[l, rows, :] * d_x)
            before = before_ref[l, wide if shift else rows, :]
            later = 2.0 * own[l] - before + scale_ref[l, rows, :] * applied
            if not last:
                q_ref[l, rows, :] = later
            adjoint = later + source_ref[l, wide, :]
            a_ref[l, wide, :] = adjoint
            narrow = adjoint.astype(BF16)
            half_ref[l, rows, :] = narrow
            send_ref[l, send_rows, :] = narrow
            den_ref[l, rows, :] = den_in[l, rows, :] + d_x * fdx_ref[l, rows, :]
            if last:
                total = vel_in[l, rows, :] + adjoint * fapplied_ref[l, rows, :]
                v = vmodel_ref[l, rows, :].astype(F32)
                shot_ref[l, send_rows, :] = ((2.0 * SPEED) * v * total).astype(BF16)

    part_rows(part, width, off_ref, body)


def last_yz_kernel(f_ref, matrix_ref, fdy_ref, fdz_ref, den_in, den_ref, z_ref):
    layers, width, depth = den_ref.shape
    z_terms(f_ref, matrix_ref, z_ref)

    @pl.loop(0, width // 8)
    def _(j):
        at = pl.multiple_of(8 * j, 8)
        rows = pl.ds(at, 8)
        for l in range(layers):
            d_y = weighted(y_pairs(f_ref, l, at + PAD, 8))[1]
            d_z = z_ref[l, rows, pl.ds(depth, depth)]
            den_ref[l, rows, :] = den_in[l, rows, :] + (
                d_y * fdy_ref[l, rows, :] + d_z * fdz_ref[l, rows, :]
            )


def last_x_kernel(part, f_ref, on_ref, off_ref, fdx_ref, den_in, scale_ref, dmodel_ref, shot_ref):
    layers, width, _ = den_in.shape

    def body(rows, off_rows, wide, send_rows):
        own = [f_ref[l, wide, :] for l in range(layers)]
        values = x_values(own, on_ref, off_ref, rows, off_rows)
        for l in range(layers):
            d_x = weighted(x_pairs(values, l))[1]
            total = den_in[l, rows, :] + d_x * fdx_ref[l, rows, :]
            density = dmodel_ref[l, rows, :].astype(F32)
            shot_ref[l, send_rows, :] = (scale_ref[l, rows, :] / density * total).astype(BF16)

    part_rows(part, width, off_ref, body)


def swap_over(axis, count, bit, value):
    return lax.ppermute(value, axis, [(i, i ^ bit) for i in range(count)])


def paired(half):
    count = lax.axis_size("sub")
    return lax.ppermute(half, "sub", [(i, i ^ 1) for i in range(count)])


def across(half, fill=True):
    groups, count = lax.axis_size("shot"), lax.axis_size("sub")
    pairs = []
    for s in range(groups):
        for i in range(1, count - 1, 2):
            pairs += [(s * count + i, s * count + i + 1), (s * count + i + 1, s * count + i)]
        if fill and groups % 2 == 0:
            for i in (0, count - 1):
                pairs.append((s * count + i, (s ^ 1) * count + i))
    return lax.ppermute(half, ("shot", "sub"), pairs)


def bits_of(groups):
    return [1 << k for k in range(groups.bit_length() - 1)]


def pick_into(out_ref, spot, held, me, row):
    for offset, ref in held:

        @pl.when(row == (me ^ offset))
        def _(ref=ref):
            if spot is None:
                out_ref[...] = ref[...]
            else:
                out_ref[spot, :, :] = ref[...]


def pick_kernel(offsets, bits, cover_ref, *refs):
    me, column = lax.axis_index("shot"), lax.axis_index("sub")
    outs = refs[-2:]
    count = len(refs) // 2 - 1
    for way in range(2):
        held = list(zip(offsets[way], refs[way * count : (way + 1) * count]))
        pick_into(outs[way], None, held, me, cover_ref[me ^ bits[way], column])


def gather_kernel(offsets, bits, cover_ref, *refs):
    me, column = lax.axis_index("shot"), lax.axis_index("sub")
    out_ref = refs[-1]
    count = (len(refs) - 1) // 2
    mine = cover_ref[me, column]
    layers = out_ref.shape[0] // 2
    for way in range(2):
        *near, far = refs[way * count : (way + 1) * count]
        spot = pl.ds(way * layers, layers)
        pick_into(out_ref, spot, list(zip(offsets[way], near)), me, mine)

        @pl.when((mine & bits[way]) != (me & bits[way]))
        def _(far=far, spot=spot):
            out_ref[spot, :, :] = far[...]


def fetch(tile, cover, tie=lambda x: x, tie_last=lambda x: x):
    groups = cover.shape[0]
    layers = tile.shape[0] // 2
    small = (layers, *tile.shape[1:])
    ways = [bits_of(groups), bits_of(groups)[::-1]]
    held = [[tile[:layers]], [tile[layers:]]]
    offsets = [[0], [0]]
    for stage in range(len(ways[0]) - 1):
        for way in range(2):
            bit = ways[way][stage]
            block = jnp.concatenate(held[way], axis=0) if len(held[way]) > 1 else held[way][0]
            got = swap_over("shot", groups, bit, block)
            held[way] = held[way] + [
                lax.slice_in_dim(got, n * layers, (n + 1) * layers, axis=0)
                for n in range(len(held[way]))
            ]
            offsets[way] = offsets[way] + [o ^ bit for o in offsets[way]]
    last = [way[-1] for way in ways]
    count = len(held[0])
    held = tie(held)
    sends = call(
        lambda *refs: pick_kernel(offsets, last, *refs),
        [(small, BF16)] * 2, [cover, *held[0], *held[1]], [SM] + [VM] * (2 * count),
    )
    far = [swap_over("shot", groups, last[way], sends[way]) for way in range(2)]
    far = tie_last(far)
    (out,) = call(
        lambda *refs: gather_kernel(offsets, last, *refs),
        [(tile.shape, BF16)], [cover, *held[0], far[0], *held[1], far[1]],
        [SM] + [VM] * (2 * count + 2),
    )
    return out


def bucket_kernel(offsets, bits, cover_ref, *refs):
    me, column = lax.axis_index("shot"), lax.axis_index("sub")
    own, got, outs = refs[:1], refs[1:2], refs[2:]
    mine = cover_ref[me, column]
    for way in range(1):
        theirs = cover_ref[me ^ bits[way], column]
        own_ref = own[way]
        for n, offset in enumerate(offsets[way]):
            out = outs[way * len(offsets[way]) + n]
            a = jnp.where(mine == (me ^ offset), own_ref[...].astype(F32), 0.0)
            b = jnp.where(theirs == (me ^ offset), got[way][...].astype(F32), 0.0)
            out[...] = (a + b).astype(out.dtype)


def give_back(part, way, cover):
    groups = cover.shape[0]
    layers = part.shape[0]
    bits = bits_of(groups)[:: 1 if way == 0 else -1]
    got = swap_over("shot", groups, bits[0], part)
    offsets = [0]
    for b in reversed(bits[1:]):
        offsets = offsets + [o ^ b for o in offsets]
    types = [BF16 if o & bits[1] else F32 for o in offsets]
    sums = call(
        lambda *refs: bucket_kernel([offsets], [bits[0]], *refs),
        [(part.shape, kind) for kind in types], [cover, part, got], [SM, VM, VM],
    )
    left = dict(zip(offsets, sums))
    for b in bits[1:]:
        away = [o for o in left if o & b]
        block = jnp.concatenate([left[o].astype(BF16) for o in away], axis=0)
        came = swap_over("shot", groups, b, block)
        left = {
            o ^ b: left[o ^ b] + came[n * layers : (n + 1) * layers].astype(F32)
            for n, o in enumerate(away)
        }
    return left[0]


def body(vel_model, den_model, cover, receivers, observed, p_now, p_before, q_now, q_before):
    layers, width, depth = p_now.shape[1:]
    tall = width + 2 * PAD
    narrow, padded = ((layers, width, depth), F32), ((layers, tall, depth), F32)
    half, flat = ((layers, width, depth), BF16), ((layers * tall, depth), F32)
    z_scratch = [pltpu.VMEM((layers, width, 2 * depth), F32)]
    matrix = z_matrix(depth)
    seen = observed[0]

    size = width // PARTS
    part_half = ((layers, size, depth), BF16)
    parts = range(PARTS)

    p, p_half = call(prepare_kernel, [padded, half], [p_now[0]])
    n_rec = receivers.shape[1]
    (lists,) = call(
        lambda rec, out: list_kernel(rec, layers, width, depth, out),
        [((2 * (n_rec + UNROLL) + 1,), jnp.int32)], [receivers], [SM], [SM],
    )
    on, off = paired(p_half), across(p_half, fill=False)
    kept = {}

    def tie(held):
        held, kept["p"] = lax.optimization_barrier((held, p))
        return held

    def tie_last(far):
        far, kept["lists"], kept["on"], kept["off"] = lax.optimization_barrier((far, lists, on, off))
        return far

    den = fetch(den_model[0], cover, tie, tie_last)
    vel = fetch(vel_model[0], cover)
    p, lists, on, offs = kept["p"], kept["lists"], kept["on"], [kept["off"]] * PARTS

    log_den, s2, s3 = call(log_kernel, [padded, narrow, narrow], [den, matrix], scratch=z_scratch)
    s1, scale = call(slope_x_kernel, [narrow, narrow], [log_den, paired(den), across(den), vel])

    stored, sources = [], []
    before = p_before[0]
    for step in range(ITERS):
        part, d_y, d_z = call(forward_yz_kernel, [narrow] * 3, [p, s2, s3, matrix], scratch=z_scratch)
        if step > 0:
            (source,) = call(
                lambda *refs, n=step - 1: receivers_kernel(n, *refs),
                [flat], [p.reshape(flat[0]), lists, seen], [VM, SM, SM],
            )
            sources.append(source.reshape(padded[0]))
        made, sends = (), []
        for k in parts:
            ins = [p, on, offs[k], part, s1, scale, before]
            *made, send = call(
                lambda *refs, k=k: forward_x_kernel(k, *refs),
                [narrow, narrow, padded, half, part_half], [*ins, *made],
                aliases={len(ins) + n: n for n in range(len(made))},
            )
            if step < ITERS - 1:
                sends.append(across(send))
        d_x, applied, later, p_half = made
        if step < ITERS - 1:
            on, offs = paired(p_half), sends
        stored.append((applied, d_x, d_y, d_z))
        before, p = p, later

    (q,) = call(prepare_kernel, [padded], [q_now[0]])
    a, a_half, *sends = call(
        lambda *refs: first_adjoint_kernel(ITERS - 1, *refs),
        [flat, half] + [part_half] * PARTS, [p.reshape(flat[0]), q.reshape(flat[0]), lists, seen],
        [VM, VM, SM, SM],
    )
    offs = [across(send) for send in sends]
    on = paired(a_half)
    a = a.reshape(padded[0])
    before, current = q_before[0], q
    sums = ()
    for step in range(ITERS - 1):
        f_applied, f_dx, f_dy, f_dz = stored[ITERS - 1 - step]
        last = step == ITERS - 2
        part, sum_vel, sum_den = call(
            lambda *refs, first=step == 0: adjoint_yz_kernel(first, *refs),
            [narrow] * 3, [a, s2, s3, matrix, f_dy, f_dz, f_applied, *sums], scratch=z_scratch,
        )
        extra = [sum_vel, stored[0][0], vel] if last else []
        made, sends, shot_vel = (), [], []
        for k in parts:
            ins = [
                a, on, offs[k], part, s1, scale, before, sources[ITERS - 2 - step], f_dx, sum_den, *extra,
            ]
            kinds = [padded, half, narrow] + ([] if last else [narrow])
            outs = call(
                lambda *refs, k=k, last=last: adjoint_x_kernel(k, last, *refs),
                kinds + [part_half] * (2 if last else 1), [*ins, *made],
                aliases={len(ins) + n: n for n in range(len(made))},
            )
            made = outs[: len(kinds)]
            sends.append(across(outs[len(kinds)]))
            shot_vel += outs[len(kinds) + 1 :]
        a, a_half, sum_den, *later = made
        on, offs = paired(a_half), sends
        if not last:
            before, current = current, later[0]
        sums = (sum_vel, sum_den)
    _, f_dx, f_dy, f_dz = stored[0]
    grad_vel = [give_back(shot_vel[k], k, cover) for k in parts]
    (sum_den,) = call(last_yz_kernel, [narrow], [a, matrix, f_dy, f_dz, sum_den], scratch=z_scratch)
    grad_den = []
    for k in parts:
        (shot_den,) = call(
            lambda *refs, k=k: last_x_kernel(k, *refs),
            [part_half], [a, on, offs[k], f_dx, sum_den, scale, den],
        )
        grad_den.append(give_back(shot_den, k, cover))
    return jnp.concatenate(grad_vel, axis=1)[None], jnp.concatenate(grad_den, axis=1)[None]


def solution(mesh):
    return jax.shard_map(
        body,
        mesh=mesh,
        in_specs=(
            P("shot", "sub", None, None),
            P("shot", "sub", None, None),
            P(),
            P("shot", None),
            P("shot", None, None),
            P("shot", "sub", None, None),
            P("shot", "sub", None, None),
            P("shot", "sub", None, None),
            P("shot", "sub", None, None),
        ),
        out_specs=(P("shot", "sub", None, None), P("shot", "sub", None, None)),
        check_vma=False,
    )
```

```python
import math

import jax
import jax.numpy as jnp
import numpy as np
from jax import lax
from jax.experimental import pallas as pl
from jax.experimental.pallas import tpu as pltpu
from jax.sharding import PartitionSpec as P


ITERS = 4
SECOND = (-205.0 / 72.0, 8.0 / 5.0, -1.0 / 5.0, 8.0 / 315.0, -1.0 / 560.0)
FIRST = (4.0 / 5.0, -1.0 / 5.0, 4.0 / 105.0, -1.0 / 280.0)
SPEED = 0.15
PAD = 8
PARTS = 2
UNROLL = 4
F32, BF16 = jnp.float32, jnp.bfloat16
VMEM_LIMIT = 4 << 20

VM = pl.BlockSpec(memory_space=pltpu.VMEM)
SM = pl.BlockSpec(memory_space=pltpu.SMEM)


def call(kernel, outs, ins, specs=None, out_specs=None, scratch=(), flops=0, aliases=None):
    outs = tuple(jax.ShapeDtypeStruct(shape, dtype) for shape, dtype in outs)
    moved_bytes = sum(math.prod(x.shape) * x.dtype.itemsize for x in (*ins, *outs))
    return pl.pallas_call(
        kernel,
        out_shape=outs,
        in_specs=list(specs or [VM] * len(ins)),
        out_specs=tuple(out_specs or [VM] * len(outs)),
        scratch_shapes=list(scratch),
        input_output_aliases=aliases or {},
        cost_estimate=pl.CostEstimate(flops=flops, bytes_accessed=moved_bytes, transcendentals=0),
        compiler_params=pltpu.CompilerParams(vmem_limit_bytes=VMEM_LIMIT),
    )(*ins)


def weighted(pairs):
    lap, first = None, None
    for m, (ahead, behind) in enumerate(pairs, 1):
        s = SECOND[m] * (ahead + behind)
        t = FIRST[m - 1] * (ahead - behind)
        lap = s if lap is None else lap + s
        first = t if first is None else first + t
    return lap, first


def y_pairs(ref, layer, row, rows):
    return [
        (ref[layer, pl.ds(row + m, rows), :], ref[layer, pl.ds(row - m, rows), :])
        for m in range(1, 5)
    ]


def z_matrix(depth):
    both = np.zeros((depth, 2 * depth), np.float64)
    for out in range(depth):
        for m in range(1, 5):
            for source, sign in ((out + m, 1.0), (out - m, -1.0)):
                if 0 <= source < depth:
                    both[source, out] += SECOND[m]
                    both[source, depth + out] += sign * FIRST[m - 1]
    high = both.astype(np.float32).astype(jnp.bfloat16)
    low = (both - high.astype(np.float64)).astype(np.float32).astype(jnp.bfloat16)
    return jnp.asarray(np.concatenate([high, high, low], axis=0))


def z_terms(f_ref, matrix_ref, z_ref):
    layers, width, _ = z_ref.shape
    for l in range(layers):
        f = f_ref[l, pl.ds(PAD, width), :]
        high = f.astype(BF16)
        low = (f - high.astype(F32)).astype(BF16)
        split = jnp.concatenate([high, low, high], axis=1)
        z_ref[l, :, :] = jnp.dot(split, matrix_ref[...], preferred_element_type=F32)


def where_am_i():
    column, columns = lax.axis_index("sub"), lax.axis_size("sub")
    even = (column & 1) == 0
    valid = jnp.logical_and(column > 0, column < columns - 1)
    return even, valid


def x_values(own, on_ref, off_ref, rows, off_rows):
    even, valid = where_am_i()
    count = len(own)
    on = [on_ref[l, rows, :].astype(F32) for l in range(count)]
    off = [jnp.where(valid, off_ref[l, off_rows, :].astype(F32), 0.0) for l in range(count)]
    low = [jnp.where(even, b, a) for a, b in zip(on, off)]
    high = [jnp.where(even, a, b) for a, b in zip(on, off)]
    return low[count - 4 :] + own + high[:4]


def part_rows(part, width, off_ref, body):
    size = width // PARTS
    first = part * size
    back = first if off_ref.shape[1] == size else 0

    @pl.loop(0, size // 16)
    def _(j):
        at = pl.multiple_of(first + 16 * j, 16)
        off_at = pl.multiple_of(first - back + 16 * j, 16)
        body(pl.ds(at, 16), pl.ds(off_at, 16), pl.ds(at + PAD, 16), pl.ds(pl.multiple_of(16 * j, 16), 16))


def x_pairs(values, layer):
    return [(values[4 + layer + m], values[4 + layer - m]) for m in range(1, 5)]


def zero_pads(ref):
    layers, tall, depth = ref.shape
    zeros = jnp.zeros((PAD, depth), F32)
    for l in range(layers):
        ref[l, pl.ds(0, PAD), :] = zeros
        ref[l, pl.ds(tall - PAD, PAD), :] = zeros


def prepare_kernel(p_ref, pw_ref, *half_refs):
    layers, width, _ = p_ref.shape
    zero_pads(pw_ref)

    @pl.loop(0, width // 16)
    def _(j):
        at = pl.multiple_of(16 * j, 16)
        for l in range(layers):
            v = p_ref[l, pl.ds(at, 16), :]
            pw_ref[l, pl.ds(at + PAD, 16), :] = v
            for half_ref in half_refs:
                half_ref[l, pl.ds(at, 16), :] = v.astype(BF16)


def list_kernel(rec_ref, layers, width, depth, list_ref):
    total = rec_ref.shape[1]
    cells = layers * width * depth
    local = rec_ref[...] - lax.axis_index("sub") * cells
    inside = jnp.logical_and(local >= 0, local < cells)
    line = lax.shift_right_arithmetic(local, depth.bit_length() - 1)
    row = line + PAD
    for l in range(1, layers):
        row += jnp.where(line >= l * width, 2 * PAD, 0)
    number = lax.broadcasted_iota(jnp.int32, (1, total), 1)
    down = lax.broadcasted_iota(jnp.int32, (total, total), 0)
    across_ = lax.broadcasted_iota(jnp.int32, (total, total), 1)
    earlier = jnp.where(down < across_, 1.0, 0.0).astype(BF16)
    counted = jnp.broadcast_to(jnp.where(inside, 1.0, 0.0), (8, total))
    place = jnp.dot(counted.astype(BF16), earlier, preferred_element_type=F32)[:1]
    place = jnp.where(inside, place.astype(jnp.int32), -1)
    spots = jnp.where(down == place, 1.0, 0.0).astype(BF16)
    pieces = [local & (depth - 1), row & 255, row >> 8, number & 255, number >> 8]
    kind = lax.broadcasted_iota(jnp.int32, (8, total), 0)
    values = jnp.zeros((8, total), jnp.int32)
    for n, piece in enumerate(pieces):
        values = jnp.where(kind == n, piece, values)
    listed = lax.dot_general(
        values.astype(F32).astype(BF16), spots, (((1,), (1,)), ((), ())), preferred_element_type=F32
    ).astype(jnp.int32)
    count = jnp.sum(counted[:1], axis=1, keepdims=True).astype(jnp.int32)
    code = (listed[2:3] * 256 + listed[1:2]) * (2 * depth) + listed[0:1]
    list_ref[0:1, :] = jnp.where(number < count, code, depth)
    list_ref[1:2, :] = listed[3:4] + 256 * listed[4:5]
    list_ref[2:3, :] = jnp.broadcast_to(count, (1, total))
    list_ref[3:4, :] = jnp.zeros((1, total), jnp.int32)


def add_receivers(n, field_ref, into_ref, list_ref, observed_ref):
    depth = field_ref.shape[1]
    lane = lax.broadcasted_iota(jnp.int32, (1, depth), 1)
    count = list_ref[2, 0]

    @pl.loop(0, (count + UNROLL - 1) // UNROLL)
    def _(c):
        rows, terms = [], []
        for k in range(UNROLL):
            code = list_ref[0, c * UNROLL + k]
            row = lax.div(code, 2 * depth)
            spot = code - row * (2 * depth)
            seen = observed_ref[n, list_ref[1, c * UNROLL + k]]
            rows.append(row)
            terms.append(jnp.where(lane == spot, field_ref[pl.ds(row, 1), :] - seen, 0.0))
        for row, term in zip(rows, terms):
            into_ref[pl.ds(row, 1), :] += term


def receivers_kernel(*refs):
    count = (len(refs) - 2) // 2
    fields, (list_ref, observed_ref), outs = refs[:count], refs[count : count + 2], refs[count + 2 :]
    for n, (field_ref, source_ref) in enumerate(zip(fields, outs)):
        source_ref[...] = jnp.zeros(source_ref.shape, F32)
        add_receivers(n, field_ref, source_ref, list_ref, observed_ref)


def first_adjoint_kernel(n, p_ref, q_ref, list_ref, observed_ref, a_ref, half_ref, *part_refs):
    a_ref[...] = q_ref[...]
    add_receivers(n, p_ref, a_ref, list_ref, observed_ref)
    layers, width, _ = half_ref.shape
    tall = width + 2 * PAD

    for n, part_ref in enumerate(part_refs):
        size = part_ref.shape[1]

        @pl.loop(0, size // 16)
        def _(j, n=n, size=size, part_ref=part_ref):
            at = pl.multiple_of(16 * j, 16)
            for l in range(layers):
                from_row = pl.multiple_of(at + n * size + l * tall + PAD, 8)
                value = a_ref[pl.ds(from_row, 16), :].astype(BF16)
                half_ref[l, pl.ds(pl.multiple_of(at + n * size, 16), 16), :] = value
                part_ref[l, pl.ds(at, 16), :] = value


def log_kernel(den_ref, matrix_ref, before_ref, log_ref, s2_ref, s3_ref, z_ref):
    layers, width, depth = den_ref.shape
    zero_pads(log_ref)

    @pl.loop(0, width // 16)
    def _(j):
        at = pl.multiple_of(16 * j, 16)
        for l in range(layers):
            log_ref[l, pl.ds(at + PAD, 16), :] = jnp.log(den_ref[l, pl.ds(at, 16), :].astype(F32))

    z_terms(log_ref, matrix_ref, z_ref)

    @pl.loop(0, width // 8)
    def _(j):
        at = pl.multiple_of(8 * j, 8)
        for l in range(layers):
            s2_ref[l, pl.ds(at, 8), :] = weighted(y_pairs(log_ref, l, at + PAD, 8))[1]
            s3_ref[l, pl.ds(at, 8), :] = z_ref[l, pl.ds(at, 8), pl.ds(depth, depth)]


def slope_x_kernel(log_ref, on_ref, off_ref, vel_ref, s1_ref, scale_ref):
    layers, width, _ = s1_ref.shape
    even, valid = where_am_i()

    @pl.loop(0, width // 16)
    def _(j):
        at = pl.multiple_of(16 * j, 16)
        rows = pl.ds(at, 16)
        own = [log_ref[l, pl.ds(at + PAD, 16), :] for l in range(layers)]
        on = [jnp.log(on_ref[l, rows, :].astype(F32)) for l in range(layers)]
        off = [jnp.log(jnp.where(valid, off_ref[l, rows, :].astype(F32), 1.0)) for l in range(layers)]
        low = [jnp.where(even, b, a) for a, b in zip(on, off)]
        high = [jnp.where(even, a, b) for a, b in zip(on, off)]
        values = low[layers - 4 :] + own + high[:4]
        for l in range(layers):
            s1_ref[l, rows, :] = weighted(x_pairs(values, l))[1]
            v = vel_ref[l, rows, :].astype(F32)
            scale_ref[l, rows, :] = SPEED * v * v


def yz_terms(f_ref, s2_ref, s3_ref, z_ref, l, at):
    f = f_ref[l, pl.ds(at + PAD, 8), :]
    lap_y, d_y = weighted(y_pairs(f_ref, l, at + PAD, 8))
    rows, depth = pl.ds(at, 8), f.shape[1]
    lap_z, d_z = z_ref[l, rows, pl.ds(0, depth)], z_ref[l, rows, pl.ds(depth, depth)]
    part = (3.0 * SECOND[0]) * f + lap_y + lap_z
    part = part - (s2_ref[l, rows, :] * d_y + s3_ref[l, rows, :] * d_z)
    return f, part, d_y, d_z


def forward_yz_kernel(f_ref, s2_ref, s3_ref, matrix_ref, part_ref, dy_ref, dz_ref, z_ref):
    layers, width, _ = part_ref.shape
    z_terms(f_ref, matrix_ref, z_ref)

    @pl.loop(0, width // 8)
    def _(j):
        at = pl.multiple_of(8 * j, 8)
        rows = pl.ds(at, 8)
        for l in range(layers):
            _, part, d_y, d_z = yz_terms(f_ref, s2_ref, s3_ref, z_ref, l, at)
            part_ref[l, rows, :] = part
            dy_ref[l, rows, :] = d_y
            dz_ref[l, rows, :] = d_z


def forward_x_kernel(part, send, f_ref, on_ref, off_ref, part_ref, s1_ref, scale_ref, before_ref, *refs):
    sending = send
    if sending:
        dx_ref, applied_ref, next_ref, half_ref, send_ref = refs[-5:]
    else:
        dx_ref, applied_ref, next_ref = refs[-3:]
    layers, width, _ = part_ref.shape
    shift = before_ref.shape[1] != width
    if part == 0:
        zero_pads(next_ref)

    def body(rows, off_rows, wide, send_rows):
        own = [f_ref[l, wide, :] for l in range(layers)]
        values = x_values(own, on_ref, off_ref, rows, off_rows)
        for l in range(layers):
            lap, d_x = weighted(x_pairs(values, l))
            applied = part_ref[l, rows, :] + (lap - s1_ref[l, rows, :] * d_x)
            before = before_ref[l, wide if shift else rows, :]
            later = 2.0 * own[l] - before + scale_ref[l, rows, :] * applied
            dx_ref[l, rows, :] = d_x
            applied_ref[l, rows, :] = applied
            next_ref[l, wide, :] = later
            if sending:
                narrow = later.astype(BF16)
                half_ref[l, rows, :] = narrow
                send_ref[l, send_rows, :] = narrow

    part_rows(part, width, off_ref, body)


def adjoint_yz_kernel(
    first, f_ref, s2_ref, s3_ref, matrix_ref, fdy_ref, fdz_ref, fapplied_ref, *refs,
):
    if first:
        part_ref, vel_ref, den_ref, z_ref = refs
    else:
        vel_in, den_in, part_ref, vel_ref, den_ref, z_ref = refs
    layers, width, _ = part_ref.shape
    z_terms(f_ref, matrix_ref, z_ref)

    @pl.loop(0, width // 8)
    def _(j):
        at = pl.multiple_of(8 * j, 8)
        rows = pl.ds(at, 8)
        for l in range(layers):
            f, part, d_y, d_z = yz_terms(f_ref, s2_ref, s3_ref, z_ref, l, at)
            part_ref[l, rows, :] = part
            sum_vel = f * fapplied_ref[l, rows, :]
            sum_den = d_y * fdy_ref[l, rows, :] + d_z * fdz_ref[l, rows, :]
            if not first:
                sum_vel = vel_in[l, rows, :] + sum_vel
                sum_den = den_in[l, rows, :] + sum_den
            vel_ref[l, rows, :] = sum_vel
            den_ref[l, rows, :] = sum_den


def adjoint_x_kernel(
    part, last, f_ref, on_ref, off_ref, part_ref, s1_ref, scale_ref, before_ref,
    source_ref, fdx_ref, den_in, *refs,
):
    if last:
        vel_in, fapplied_ref, vmodel_ref = refs[:3]
        a_ref, half_ref, den_ref, send_ref, shot_ref = refs[-5:]
    else:
        a_ref, half_ref, den_ref, q_ref, send_ref = refs[-5:]
    layers, width, _ = part_ref.shape
    shift = before_ref.shape[1] != width
    if part == 0:
        zero_pads(a_ref)

    def body(rows, off_rows, wide, send_rows):
        own = [f_ref[l, wide, :] for l in range(layers)]
        values = x_values(own, on_ref, off_ref, rows, off_rows)
        for l in range(layers):
            lap, d_x = weighted(x_pairs(values, l))
            applied = part_ref[l, rows, :] + (lap - s1_ref[l, rows, :] * d_x)
            before = before_ref[l, wide if shift else rows, :]
            later = 2.0 * own[l] - before + scale_ref[l, rows, :] * applied
            if not last:
                q_ref[l, rows, :] = later
            adjoint = later + source_ref[l, wide, :]
            a_ref[l, wide, :] = adjoint
            narrow = adjoint.astype(BF16)
            half_ref[l, rows, :] = narrow
            send_ref[l, send_rows, :] = narrow
            den_ref[l, rows, :] = den_in[l, rows, :] + d_x * fdx_ref[l, rows, :]
            if last:
                total = vel_in[l, rows, :] + adjoint * fapplied_ref[l, rows, :]
                v = vmodel_ref[l, rows, :].astype(F32)
                shot_ref[l, send_rows, :] = ((2.0 * SPEED) * v * total).astype(BF16)

    part_rows(part, width, off_ref, body)


def last_yz_kernel(f_ref, matrix_ref, fdy_ref, fdz_ref, den_in, den_ref, z_ref):
    layers, width, depth = den_ref.shape
    z_terms(f_ref, matrix_ref, z_ref)

    @pl.loop(0, width // 8)
    def _(j):
        at = pl.multiple_of(8 * j, 8)
        rows = pl.ds(at, 8)
        for l in range(layers):
            d_y = weighted(y_pairs(f_ref, l, at + PAD, 8))[1]
            d_z = z_ref[l, rows, pl.ds(depth, depth)]
            den_ref[l, rows, :] = den_in[l, rows, :] + (
                d_y * fdy_ref[l, rows, :] + d_z * fdz_ref[l, rows, :]
            )


def last_x_kernel(part, f_ref, on_ref, off_ref, fdx_ref, den_in, scale_ref, dmodel_ref, shot_ref):
    layers, width, _ = den_in.shape

    def body(rows, off_rows, wide, send_rows):
        own = [f_ref[l, wide, :] for l in range(layers)]
        values = x_values(own, on_ref, off_ref, rows, off_rows)
        for l in range(layers):
            d_x = weighted(x_pairs(values, l))[1]
            total = den_in[l, rows, :] + d_x * fdx_ref[l, rows, :]
            density = dmodel_ref[l, rows, :].astype(F32)
            shot_ref[l, send_rows, :] = (scale_ref[l, rows, :] / density * total).astype(BF16)

    part_rows(part, width, off_ref, body)


def swap_over(axis, count, bit, value):
    return lax.ppermute(value, axis, [(i, i ^ bit) for i in range(count)])


def paired(half):
    count = lax.axis_size("sub")
    return lax.ppermute(half, "sub", [(i, i ^ 1) for i in range(count)])


def across(half, fill=True):
    groups, count = lax.axis_size("shot"), lax.axis_size("sub")
    pairs = []
    for s in range(groups):
        for i in range(1, count - 1, 2):
            pairs += [(s * count + i, s * count + i + 1), (s * count + i + 1, s * count + i)]
        if fill and groups % 2 == 0:
            for i in (0, count - 1):
                pairs.append((s * count + i, (s ^ 1) * count + i))
    return lax.ppermute(half, ("shot", "sub"), pairs)


def bits_of(groups):
    return [1 << k for k in range(groups.bit_length() - 1)]


def routes_kernel(cover_ref, out_ref):
    column = lax.axis_index("sub")
    for g in range(out_ref.shape[0]):
        out_ref[g, :, :] = jnp.full(out_ref.shape[1:], cover_ref[g, column], jnp.int32)


def masked_sum(out_ref, first, terms):
    layers, width, _ = terms[0][1].shape

    @pl.loop(0, width // 16)
    def _(j):
        rows = pl.ds(pl.multiple_of(16 * j, 16), 16)
        for l in range(layers):
            total = None
            for mask, ref in terms:
                term = jnp.where(mask, ref[l, rows, :].astype(F32), 0.0)
                total = term if total is None else total + term
            out_ref[first + l, rows, :] = total.astype(out_ref.dtype)


def pick_kernel(offsets, bits, route_ref, *refs):
    me = lax.axis_index("shot")
    outs = refs[-2:]
    count = len(refs) // 2 - 1
    for way in range(2):
        row = route_ref[me ^ bits[way]]
        held = refs[way * count : (way + 1) * count]
        masked_sum(outs[way], 0, [(row == (me ^ o), ref) for o, ref in zip(offsets[way], held)])


def gather_kernel(offsets, bits, route_ref, *refs):
    me = lax.axis_index("shot")
    out_ref = refs[-1]
    count = (len(refs) - 1) // 2
    mine = route_ref[me]
    layers = out_ref.shape[0] // 2
    for way in range(2):
        *near, far = refs[way * count : (way + 1) * count]
        terms = [(mine == (me ^ o), ref) for o, ref in zip(offsets[way], near)]
        terms.append(((mine & bits[way]) != (me & bits[way]), far))
        masked_sum(out_ref, way * layers, terms)


def fetch(tile, route, tie=lambda x: x):
    groups = route.shape[0]
    layers = tile.shape[0] // 2
    small = (layers, *tile.shape[1:])
    ways = [bits_of(groups), bits_of(groups)[::-1]]
    held = [[tile[:layers]], [tile[layers:]]]
    offsets = [[0], [0]]
    for stage in range(len(ways[0]) - 1):
        for way in range(2):
            bit = ways[way][stage]
            block = jnp.concatenate(held[way], axis=0) if len(held[way]) > 1 else held[way][0]
            got = swap_over("shot", groups, bit, block)
            held[way] = held[way] + [
                lax.slice_in_dim(got, n * layers, (n + 1) * layers, axis=0)
                for n in range(len(held[way]))
            ]
            offsets[way] = offsets[way] + [o ^ bit for o in offsets[way]]
    last = [way[-1] for way in ways]
    held = tie(held)
    sends = call(
        lambda *refs: pick_kernel(offsets, last, *refs),
        [(small, BF16)] * 2, [route, *held[0], *held[1]],
    )
    far = [swap_over("shot", groups, last[way], sends[way]) for way in range(2)]
    (out,) = call(
        lambda *refs: gather_kernel(offsets, last, *refs),
        [(tile.shape, BF16)], [route, *held[0], far[0], *held[1], far[1]],
    )
    return out


def bucket_kernel(offsets, bit, route_ref, own_ref, got_ref, *outs):
    me = lax.axis_index("shot")
    mine, theirs = route_ref[me], route_ref[me ^ bit]
    for offset, out in zip(offsets, outs):
        row = me ^ offset
        masked_sum(out, 0, [(mine == row, own_ref), (theirs == row, got_ref)])


def give_back(part, way, route):
    groups = route.shape[0]
    layers = part.shape[0]
    bits = bits_of(groups)[:: 1 if way == 0 else -1]
    got = swap_over("shot", groups, bits[0], part)
    offsets = [0]
    for b in reversed(bits[1:]):
        offsets = offsets + [o ^ b for o in offsets]
    types = [BF16 if o & bits[1] else F32 for o in offsets]
    sums = call(
        lambda *refs: bucket_kernel(offsets, bits[0], *refs),
        [(part.shape, kind) for kind in types], [route, part, got],
    )
    left = dict(zip(offsets, sums))
    for b in bits[1:]:
        away = [o for o in left if o & b]
        block = jnp.concatenate([left[o].astype(BF16) for o in away], axis=0)
        came = swap_over("shot", groups, b, block)
        left = {
            o ^ b: left[o ^ b] + came[n * layers : (n + 1) * layers].astype(F32)
            for n, o in enumerate(away)
        }
    return left[0]


def inner(vel_model, den_model, cover, receivers, observed, p_now, p_before, q_now, q_before):
    layers, width, depth = p_now.shape[1:]
    tall = width + 2 * PAD
    narrow, padded = ((layers, width, depth), F32), ((layers, tall, depth), F32)
    half, flat = ((layers, width, depth), BF16), ((layers * tall, depth), F32)
    z_scratch = [pltpu.VMEM((layers, width, 2 * depth), F32)]
    matrix = z_matrix(depth)
    seen = observed[0]

    size = width // PARTS
    part_half = ((layers, size, depth), BF16)
    parts = range(PARTS)

    groups = cover.shape[0]
    (route,) = call(routes_kernel, [((groups, 16, depth), jnp.int32)], [cover], [SM])

    p, p_half = call(prepare_kernel, [padded, half], [p_now[0]])
    n_rec = receivers.shape[1]
    (lists,) = call(
        lambda rec, out: list_kernel(rec, layers, width, depth, out),
        [((4, n_rec), jnp.int32)], [receivers],
    )
    on, off = paired(p_half), across(p_half)
    kept = {}

    def tie(held):
        held, kept["p"] = lax.optimization_barrier((held, p))
        return held

    den = fetch(den_model[0], route, tie)
    vel = fetch(vel_model[0], route)
    p, offs = kept["p"], [off] * PARTS

    before = p_before[0]
    log_den, s2, s3 = call(log_kernel, [padded, narrow, narrow], [den, matrix, before], scratch=z_scratch)
    s1, scale = call(slope_x_kernel, [narrow, narrow], [log_den, paired(den), across(den), vel])

    stored, fields = [], []
    for step in range(ITERS):
        part, d_y, d_z = call(forward_yz_kernel, [narrow] * 3, [p, s2, s3, matrix], scratch=z_scratch)
        if step > 0:
            fields.append(p.reshape(flat[0]))
        sending = step < ITERS - 1
        made, sends = (), []
        for k in parts:
            ins = [p, on, offs[k], part, s1, scale, before]
            outs = call(
                lambda *refs, k=k, sending=sending: forward_x_kernel(k, sending, *refs),
                [narrow, narrow, padded] + ([half, part_half] if sending else []), [*ins, *made],
                aliases={len(ins) + n: n for n in range(len(made))},
            )
            made = outs[: 4 if sending else 3]
            if sending:
                sends.append(across(outs[4]))
        d_x, applied, later = made[:3]
        if sending:
            on, offs = paired(made[3]), sends
        stored.append((applied, d_x, d_y, d_z))
        before, p = p, later

    (q,) = call(prepare_kernel, [padded], [q_now[0]])
    a, a_half, *sends = call(
        lambda *refs: first_adjoint_kernel(ITERS - 1, *refs),
        [flat, half] + [part_half] * PARTS, [p.reshape(flat[0]), q.reshape(flat[0]), lists, seen],
        [VM, VM, SM, SM],
    )
    offs = [across(send) for send in sends]
    on = paired(a_half)
    a = a.reshape(padded[0])
    sources = call(
        receivers_kernel, [flat] * len(fields), [*fields, lists, seen],
        [VM] * len(fields) + [SM, SM],
    )
    sources = [source.reshape(padded[0]) for source in sources]
    before, current = q_before[0], q
    sums = ()
    for step in range(ITERS - 1):
        f_applied, f_dx, f_dy, f_dz = stored[ITERS - 1 - step]
        last = step == ITERS - 2
        part, sum_vel, sum_den = call(
            lambda *refs, first=step == 0: adjoint_yz_kernel(first, *refs),
            [narrow] * 3, [a, s2, s3, matrix, f_dy, f_dz, f_applied, *sums], scratch=z_scratch,
        )
        extra = [sum_vel, stored[0][0], vel] if last else []
        made, sends, shot_vel = (), [], []
        for k in parts:
            ins = [
                a, on, offs[k], part, s1, scale, before, sources[ITERS - 2 - step], f_dx, sum_den, *extra,
            ]
            kinds = [padded, half, narrow] + ([] if last else [narrow])
            outs = call(
                lambda *refs, k=k, last=last: adjoint_x_kernel(k, last, *refs),
                kinds + [part_half] * (2 if last else 1), [*ins, *made],
                aliases={len(ins) + n: n for n in range(len(made))},
            )
            made = outs[: len(kinds)]
            sends.append(across(outs[len(kinds)]))
            shot_vel += outs[len(kinds) + 1 :]
        a, a_half, sum_den, *later = made
        on, offs = paired(a_half), sends
        if not last:
            before, current = current, later[0]
        sums = (sum_vel, sum_den)
    _, f_dx, f_dy, f_dz = stored[0]
    grad_vel = [give_back(shot_vel[k], k, route) for k in parts]
    (sum_den,) = call(last_yz_kernel, [narrow], [a, matrix, f_dy, f_dz, sum_den], scratch=z_scratch)
    grad_den = []
    for k in parts:
        (shot_den,) = call(
            lambda *refs, k=k: last_x_kernel(k, *refs),
            [part_half], [a, on, offs[k], f_dx, sum_den, scale, den],
        )
        grad_den.append(give_back(shot_den, k, route))
    return jnp.concatenate(grad_vel, axis=1)[None], jnp.concatenate(grad_den, axis=1)[None]


def solution(mesh):
    spec = P("shot", "sub", None, None)
    return jax.shard_map(
        inner,
        mesh=mesh,
        in_specs=(spec, spec, P(), P("shot", None), P("shot", None, None), spec, spec, spec, spec),
        out_specs=(spec, spec),
        check_vma=False,
    )
```

```python
import math

import jax
import jax.numpy as jnp
import numpy as np
from jax import lax
from jax.experimental import pallas as pl
from jax.experimental.pallas import tpu as pltpu
from jax.sharding import PartitionSpec as P


ITERS = 4
SECOND = (-205.0 / 72.0, 8.0 / 5.0, -1.0 / 5.0, 8.0 / 315.0, -1.0 / 560.0)
FIRST = (4.0 / 5.0, -1.0 / 5.0, 4.0 / 105.0, -1.0 / 280.0)
SPEED = 0.15
PAD = 8
PARTS = 2
UNROLL = 4
F32, BF16 = jnp.float32, jnp.bfloat16
VMEM_LIMIT = 4 << 20

VM = pl.BlockSpec(memory_space=pltpu.VMEM)
SM = pl.BlockSpec(memory_space=pltpu.SMEM)


def call(kernel, outs, ins, specs=None, out_specs=None, scratch=(), flops=0, aliases=None):
    outs = tuple(jax.ShapeDtypeStruct(shape, dtype) for shape, dtype in outs)
    moved_bytes = sum(math.prod(x.shape) * x.dtype.itemsize for x in (*ins, *outs))
    return pl.pallas_call(
        kernel,
        out_shape=outs,
        in_specs=list(specs or [VM] * len(ins)),
        out_specs=tuple(out_specs or [VM] * len(outs)),
        scratch_shapes=list(scratch),
        input_output_aliases=aliases or {},
        cost_estimate=pl.CostEstimate(flops=flops, bytes_accessed=moved_bytes, transcendentals=0),
        compiler_params=pltpu.CompilerParams(vmem_limit_bytes=VMEM_LIMIT),
    )(*ins)


def weighted(pairs):
    lap, first = None, None
    for m, (ahead, behind) in enumerate(pairs, 1):
        s = SECOND[m] * (ahead + behind)
        t = FIRST[m - 1] * (ahead - behind)
        lap = s if lap is None else lap + s
        first = t if first is None else first + t
    return lap, first


def y_pairs(ref, layer, row, rows):
    return [
        (ref[layer, pl.ds(row + m, rows), :], ref[layer, pl.ds(row - m, rows), :])
        for m in range(1, 5)
    ]


def z_matrix(depth):
    both = np.zeros((depth, 2 * depth), np.float64)
    for out in range(depth):
        for m in range(1, 5):
            for source, sign in ((out + m, 1.0), (out - m, -1.0)):
                if 0 <= source < depth:
                    both[source, out] += SECOND[m]
                    both[source, depth + out] += sign * FIRST[m - 1]
    high = both.astype(np.float32).astype(jnp.bfloat16)
    low = (both - high.astype(np.float64)).astype(np.float32).astype(jnp.bfloat16)
    return jnp.asarray(np.concatenate([high, high, low], axis=0))


def z_terms(f_ref, matrix_ref, z_ref):
    layers, width, _ = z_ref.shape
    for l in range(layers):
        f = f_ref[l, pl.ds(PAD, width), :]
        high = f.astype(BF16)
        low = (f - high.astype(F32)).astype(BF16)
        split = jnp.concatenate([high, low, high], axis=1)
        z_ref[l, :, :] = jnp.dot(split, matrix_ref[...], preferred_element_type=F32)


def where_am_i():
    column, columns = lax.axis_index("sub"), lax.axis_size("sub")
    even = (column & 1) == 0
    valid = jnp.logical_and(column > 0, column < columns - 1)
    return even, valid


def x_values(own, on_ref, off_ref, rows, off_rows):
    even, valid = where_am_i()
    count = len(own)
    on = [on_ref[l, rows, :].astype(F32) for l in range(count)]
    off = [jnp.where(valid, off_ref[l, off_rows, :].astype(F32), 0.0) for l in range(count)]
    low = [jnp.where(even, b, a) for a, b in zip(on, off)]
    high = [jnp.where(even, a, b) for a, b in zip(on, off)]
    return low[count - 4 :] + own + high[:4]


def part_rows(part, width, off_ref, body):
    size = width // PARTS
    first = part * size
    back = first if off_ref.shape[1] == size else 0

    @pl.loop(0, size // 16)
    def _(j):
        at = pl.multiple_of(first + 16 * j, 16)
        off_at = pl.multiple_of(first - back + 16 * j, 16)
        body(pl.ds(at, 16), pl.ds(off_at, 16), pl.ds(at + PAD, 16), pl.ds(pl.multiple_of(16 * j, 16), 16))


def x_pairs(values, layer):
    return [(values[4 + layer + m], values[4 + layer - m]) for m in range(1, 5)]


def zero_pads(ref):
    layers, tall, depth = ref.shape
    zeros = jnp.zeros((PAD, depth), F32)
    for l in range(layers):
        ref[l, pl.ds(0, PAD), :] = zeros
        ref[l, pl.ds(tall - PAD, PAD), :] = zeros


def prepare_kernel(p_ref, pw_ref, *half_refs):
    layers, width, _ = p_ref.shape
    zero_pads(pw_ref)

    @pl.loop(0, width // 16)
    def _(j):
        at = pl.multiple_of(16 * j, 16)
        for l in range(layers):
            v = p_ref[l, pl.ds(at, 16), :]
            pw_ref[l, pl.ds(at + PAD, 16), :] = v
            for half_ref in half_refs:
                half_ref[l, pl.ds(at, 16), :] = v.astype(BF16)


def list_kernel(rec_ref, layers, width, depth, list_ref):
    total = rec_ref.shape[1]
    cells = layers * width * depth
    local = rec_ref[...] - lax.axis_index("sub") * cells
    inside = jnp.logical_and(local >= 0, local < cells)
    line = lax.shift_right_arithmetic(local, depth.bit_length() - 1)
    row = line + PAD
    for l in range(1, layers):
        row += jnp.where(line >= l * width, 2 * PAD, 0)
    number = lax.broadcasted_iota(jnp.int32, (1, total), 1)
    down = lax.broadcasted_iota(jnp.int32, (total, total), 0)
    across_ = lax.broadcasted_iota(jnp.int32, (total, total), 1)
    earlier = jnp.where(down < across_, 1.0, 0.0).astype(BF16)
    counted = jnp.broadcast_to(jnp.where(inside, 1.0, 0.0), (8, total))
    place = jnp.dot(counted.astype(BF16), earlier, preferred_element_type=F32)[:1]
    place = jnp.where(inside, place.astype(jnp.int32), -1)
    spots = jnp.where(down == place, 1.0, 0.0).astype(BF16)
    pieces = [local & (depth - 1), row & 255, row >> 8, number & 255, number >> 8]
    kind = lax.broadcasted_iota(jnp.int32, (8, total), 0)
    values = jnp.zeros((8, total), jnp.int32)
    for n, piece in enumerate(pieces):
        values = jnp.where(kind == n, piece, values)
    listed = lax.dot_general(
        values.astype(F32).astype(BF16), spots, (((1,), (1,)), ((), ())), preferred_element_type=F32
    ).astype(jnp.int32)
    count = jnp.sum(counted[:1], axis=1, keepdims=True).astype(jnp.int32)
    list_ref[0:1, :] = listed[2:3] * 256 + listed[1:2]
    list_ref[1:2, :] = listed[3:4] + 256 * listed[4:5]
    list_ref[2:3, :] = jnp.broadcast_to(count, (1, total))
    list_ref[3:4, :] = jnp.where(number < count, listed[0:1], depth)


def add_receivers(n, field_ref, into_ref, list_ref, observed_ref):
    depth = field_ref.shape[1]
    lane = lax.broadcasted_iota(jnp.int32, (1, depth), 1)
    count = list_ref[2, 0]

    @pl.loop(0, (count + UNROLL - 1) // UNROLL)
    def _(c):
        rows, terms = [], []
        for k in range(UNROLL):
            row = list_ref[0, c * UNROLL + k]
            spot = list_ref[3, c * UNROLL + k]
            seen = observed_ref[n, list_ref[1, c * UNROLL + k]]
            rows.append(row)
            terms.append(jnp.where(lane == spot, field_ref[pl.ds(row, 1), :] - seen, 0.0))
        for row, term in zip(rows, terms):
            into_ref[pl.ds(row, 1), :] += term


def receivers_kernel(first, *refs):
    count = (len(refs) - 2) // 2
    fields, (list_ref, observed_ref), outs = refs[:count], refs[count : count + 2], refs[count + 2 :]
    for n, (field_ref, source_ref) in enumerate(zip(fields, outs)):
        source_ref[...] = jnp.zeros(source_ref.shape, F32)
        add_receivers(first + n, field_ref, source_ref, list_ref, observed_ref)


def first_adjoint_kernel(n, p_ref, q_ref, list_ref, observed_ref, a_ref, half_ref, *part_refs):
    a_ref[...] = q_ref[...]
    add_receivers(n, p_ref, a_ref, list_ref, observed_ref)
    layers, width, _ = half_ref.shape
    tall = width + 2 * PAD

    for n, part_ref in enumerate(part_refs):
        size = part_ref.shape[1]

        @pl.loop(0, size // 16)
        def _(j, n=n, size=size, part_ref=part_ref):
            at = pl.multiple_of(16 * j, 16)
            for l in range(layers):
                from_row = pl.multiple_of(at + n * size + l * tall + PAD, 8)
                value = a_ref[pl.ds(from_row, 16), :].astype(BF16)
                half_ref[l, pl.ds(pl.multiple_of(at + n * size, 16), 16), :] = value
                part_ref[l, pl.ds(at, 16), :] = value


def log_kernel(den_ref, matrix_ref, before_ref, log_ref, s2_ref, s3_ref, z_ref):
    layers, width, depth = den_ref.shape
    zero_pads(log_ref)

    @pl.loop(0, width // 16)
    def _(j):
        at = pl.multiple_of(16 * j, 16)
        for l in range(layers):
            log_ref[l, pl.ds(at + PAD, 16), :] = jnp.log(den_ref[l, pl.ds(at, 16), :].astype(F32))

    z_terms(log_ref, matrix_ref, z_ref)

    @pl.loop(0, width // 8)
    def _(j):
        at = pl.multiple_of(8 * j, 8)
        for l in range(layers):
            s2_ref[l, pl.ds(at, 8), :] = weighted(y_pairs(log_ref, l, at + PAD, 8))[1]
            s3_ref[l, pl.ds(at, 8), :] = z_ref[l, pl.ds(at, 8), pl.ds(depth, depth)]


def slope_x_kernel(part, log_ref, on_ref, off_ref, vel_ref, *refs):
    s1_ref, scale_ref = refs[-2:]
    layers, width, _ = s1_ref.shape
    even, valid = where_am_i()

    def body(rows, off_rows, wide, send_rows):
        own = [log_ref[l, wide, :] for l in range(layers)]
        on = [jnp.log(on_ref[l, rows, :].astype(F32)) for l in range(layers)]
        off = [jnp.log(jnp.where(valid, off_ref[l, off_rows, :].astype(F32), 1.0)) for l in range(layers)]
        low = [jnp.where(even, b, a) for a, b in zip(on, off)]
        high = [jnp.where(even, a, b) for a, b in zip(on, off)]
        values = low[layers - 4 :] + own + high[:4]
        for l in range(layers):
            s1_ref[l, rows, :] = weighted(x_pairs(values, l))[1]
            v = vel_ref[l, rows, :].astype(F32)
            scale_ref[l, rows, :] = SPEED * v * v

    part_rows(part, width, off_ref, body)


def yz_terms(f_ref, s2_ref, s3_ref, z_ref, l, at):
    f = f_ref[l, pl.ds(at + PAD, 8), :]
    lap_y, d_y = weighted(y_pairs(f_ref, l, at + PAD, 8))
    rows, depth = pl.ds(at, 8), f.shape[1]
    lap_z, d_z = z_ref[l, rows, pl.ds(0, depth)], z_ref[l, rows, pl.ds(depth, depth)]
    part = (3.0 * SECOND[0]) * f + lap_y + lap_z
    part = part - (s2_ref[l, rows, :] * d_y + s3_ref[l, rows, :] * d_z)
    return f, part, d_y, d_z


def forward_yz_kernel(f_ref, s2_ref, s3_ref, matrix_ref, part_ref, dy_ref, dz_ref, z_ref):
    layers, width, _ = part_ref.shape
    z_terms(f_ref, matrix_ref, z_ref)

    @pl.loop(0, width // 8)
    def _(j):
        at = pl.multiple_of(8 * j, 8)
        rows = pl.ds(at, 8)
        for l in range(layers):
            _, part, d_y, d_z = yz_terms(f_ref, s2_ref, s3_ref, z_ref, l, at)
            part_ref[l, rows, :] = part
            dy_ref[l, rows, :] = d_y
            dz_ref[l, rows, :] = d_z


def forward_x_kernel(part, send, f_ref, on_ref, off_ref, part_ref, s1_ref, scale_ref, before_ref, *refs):
    sending = send
    if sending:
        dx_ref, applied_ref, next_ref, half_ref, send_ref = refs[-5:]
    else:
        dx_ref, applied_ref, next_ref = refs[-3:]
    layers, width, _ = part_ref.shape
    shift = before_ref.shape[1] != width
    if part == 0:
        zero_pads(next_ref)

    def body(rows, off_rows, wide, send_rows):
        own = [f_ref[l, wide, :] for l in range(layers)]
        values = x_values(own, on_ref, off_ref, rows, off_rows)
        for l in range(layers):
            lap, d_x = weighted(x_pairs(values, l))
            applied = part_ref[l, rows, :] + (lap - s1_ref[l, rows, :] * d_x)
            before = before_ref[l, wide if shift else rows, :]
            later = 2.0 * own[l] - before + scale_ref[l, rows, :] * applied
            dx_ref[l, rows, :] = d_x
            applied_ref[l, rows, :] = applied
            next_ref[l, wide, :] = later
            if sending:
                narrow = later.astype(BF16)
                half_ref[l, rows, :] = narrow
                send_ref[l, send_rows, :] = narrow

    part_rows(part, width, off_ref, body)


def adjoint_yz_kernel(
    first, f_ref, s2_ref, s3_ref, matrix_ref, fdy_ref, fdz_ref, fapplied_ref, *refs,
):
    if first:
        part_ref, vel_ref, den_ref, z_ref = refs
    else:
        vel_in, den_in, part_ref, vel_ref, den_ref, z_ref = refs
    layers, width, _ = part_ref.shape
    z_terms(f_ref, matrix_ref, z_ref)

    @pl.loop(0, width // 8)
    def _(j):
        at = pl.multiple_of(8 * j, 8)
        rows = pl.ds(at, 8)
        for l in range(layers):
            f, part, d_y, d_z = yz_terms(f_ref, s2_ref, s3_ref, z_ref, l, at)
            part_ref[l, rows, :] = part
            sum_vel = f * fapplied_ref[l, rows, :]
            sum_den = d_y * fdy_ref[l, rows, :] + d_z * fdz_ref[l, rows, :]
            if not first:
                sum_vel = vel_in[l, rows, :] + sum_vel
                sum_den = den_in[l, rows, :] + sum_den
            vel_ref[l, rows, :] = sum_vel
            den_ref[l, rows, :] = sum_den


def adjoint_x_kernel(
    part, last, f_ref, on_ref, off_ref, part_ref, s1_ref, scale_ref, before_ref,
    source_ref, fdx_ref, den_in, *refs,
):
    if last:
        vel_in, fapplied_ref, vmodel_ref = refs[:3]
        a_ref, half_ref, den_ref, send_ref, shot_ref = refs[-5:]
    else:
        a_ref, half_ref, den_ref, q_ref, send_ref = refs[-5:]
    layers, width, _ = part_ref.shape
    shift = before_ref.shape[1] != width
    if part == 0:
        zero_pads(a_ref)

    def body(rows, off_rows, wide, send_rows):
        own = [f_ref[l, wide, :] for l in range(layers)]
        values = x_values(own, on_ref, off_ref, rows, off_rows)
        for l in range(layers):
            lap, d_x = weighted(x_pairs(values, l))
            applied = part_ref[l, rows, :] + (lap - s1_ref[l, rows, :] * d_x)
            before = before_ref[l, wide if shift else rows, :]
            later = 2.0 * own[l] - before + scale_ref[l, rows, :] * applied
            if not last:
                q_ref[l, rows, :] = later
            adjoint = later + source_ref[l, wide, :]
            a_ref[l, wide, :] = adjoint
            narrow = adjoint.astype(BF16)
            half_ref[l, rows, :] = narrow
            send_ref[l, send_rows, :] = narrow
            den_ref[l, rows, :] = den_in[l, rows, :] + d_x * fdx_ref[l, rows, :]
            if last:
                total = vel_in[l, rows, :] + adjoint * fapplied_ref[l, rows, :]
                v = vmodel_ref[l, rows, :].astype(F32)
                shot_ref[l, send_rows, :] = ((2.0 * SPEED) * v * total).astype(BF16)

    part_rows(part, width, off_ref, body)


def last_yz_kernel(f_ref, matrix_ref, fdy_ref, fdz_ref, den_in, den_ref, z_ref):
    layers, width, depth = den_ref.shape
    z_terms(f_ref, matrix_ref, z_ref)

    @pl.loop(0, width // 8)
    def _(j):
        at = pl.multiple_of(8 * j, 8)
        rows = pl.ds(at, 8)
        for l in range(layers):
            d_y = weighted(y_pairs(f_ref, l, at + PAD, 8))[1]
            d_z = z_ref[l, rows, pl.ds(depth, depth)]
            den_ref[l, rows, :] = den_in[l, rows, :] + (
                d_y * fdy_ref[l, rows, :] + d_z * fdz_ref[l, rows, :]
            )


def last_x_kernel(part, f_ref, on_ref, off_ref, fdx_ref, den_in, scale_ref, dmodel_ref, shot_ref):
    layers, width, _ = den_in.shape

    def body(rows, off_rows, wide, send_rows):
        own = [f_ref[l, wide, :] for l in range(layers)]
        values = x_values(own, on_ref, off_ref, rows, off_rows)
        for l in range(layers):
            d_x = weighted(x_pairs(values, l))[1]
            total = den_in[l, rows, :] + d_x * fdx_ref[l, rows, :]
            density = dmodel_ref[l, rows, :].astype(F32)
            shot_ref[l, send_rows, :] = (scale_ref[l, rows, :] / density * total).astype(BF16)

    part_rows(part, width, off_ref, body)


def swap_over(axis, count, bit, value):
    return lax.ppermute(value, axis, [(i, i ^ bit) for i in range(count)])


def paired(half):
    count = lax.axis_size("sub")
    return lax.ppermute(half, "sub", [(i, i ^ 1) for i in range(count)])


def across(half, fill=True):
    groups, count = lax.axis_size("shot"), lax.axis_size("sub")
    pairs = []
    for s in range(groups):
        for i in range(1, count - 1, 2):
            pairs += [(s * count + i, s * count + i + 1), (s * count + i + 1, s * count + i)]
        if fill and groups % 2 == 0:
            for i in (0, count - 1):
                pairs.append((s * count + i, (s ^ 1) * count + i))
    return lax.ppermute(half, ("shot", "sub"), pairs)


def bits_of(groups):
    return [1 << k for k in range(groups.bit_length() - 1)]


def routes_kernel(cover_ref, out_ref):
    column = lax.axis_index("sub")
    for g in range(out_ref.shape[0]):
        out_ref[g, :, :] = jnp.full(out_ref.shape[1:], cover_ref[g, column], jnp.int32)


def masked_sum(out_ref, first, terms):
    layers, width, _ = terms[0][1].shape

    @pl.loop(0, width // 16)
    def _(j):
        rows = pl.ds(pl.multiple_of(16 * j, 16), 16)
        for l in range(layers):
            total = None
            for mask, ref in terms:
                term = jnp.where(mask, ref[l, rows, :].astype(F32), 0.0)
                total = term if total is None else total + term
            out_ref[first + l, rows, :] = total.astype(out_ref.dtype)


def pick_kernel(offsets, bits, route_ref, *refs):
    me = lax.axis_index("shot")
    outs = refs[-2:]
    count = len(refs) // 2 - 1
    for way in range(2):
        row = route_ref[me ^ bits[way]]
        held = refs[way * count : (way + 1) * count]
        masked_sum(outs[way], 0, [(row == (me ^ o), ref) for o, ref in zip(offsets[way], held)])


def gather_kernel(offsets, bits, parts, route_ref, *refs):
    me = lax.axis_index("shot")
    part_refs = refs[len(refs) - parts :]
    refs = refs[: len(refs) - parts]
    out_ref = refs[-1]
    count = (len(refs) - 1) // 2
    mine = route_ref[me]
    layers = out_ref.shape[0] // 2
    for way in range(2):
        *near, far = refs[way * count : (way + 1) * count]
        terms = [(mine == (me ^ o), ref) for o, ref in zip(offsets[way], near)]
        terms.append(((mine & bits[way]) != (me & bits[way]), far))
        masked_sum(out_ref, way * layers, terms)
    for n, part_ref in enumerate(part_refs):
        size = part_ref.shape[1]
        part_ref[...] = out_ref[:, n * size : (n + 1) * size, :]


def fetch(tile, route, parts=0, tie=lambda x: x):
    groups = route.shape[0]
    layers = tile.shape[0] // 2
    small = (layers, *tile.shape[1:])
    ways = [bits_of(groups), bits_of(groups)[::-1]]
    held = [[tile[:layers]], [tile[layers:]]]
    offsets = [[0], [0]]
    for stage in range(len(ways[0]) - 1):
        for way in range(2):
            bit = ways[way][stage]
            block = jnp.concatenate(held[way], axis=0) if len(held[way]) > 1 else held[way][0]
            got = swap_over("shot", groups, bit, block)
            held[way] = held[way] + [
                lax.slice_in_dim(got, n * layers, (n + 1) * layers, axis=0)
                for n in range(len(held[way]))
            ]
            offsets[way] = offsets[way] + [o ^ bit for o in offsets[way]]
    last = [way[-1] for way in ways]
    held = tie(held)
    sends = call(
        lambda *refs: pick_kernel(offsets, last, *refs),
        [(small, BF16)] * 2, [route, *held[0], *held[1]],
    )
    far = [swap_over("shot", groups, last[way], sends[way]) for way in range(2)]
    part_shape = (tile.shape[0], tile.shape[1] // PARTS, tile.shape[2])
    return call(
        lambda *refs: gather_kernel(offsets, last, parts, *refs),
        [(tile.shape, BF16)] + [(part_shape, BF16)] * parts, [route, *held[0], far[0], *held[1], far[1]],
    )


def bucket_kernel(offsets, bit, route_ref, own_ref, got_ref, *outs):
    me = lax.axis_index("shot")
    mine, theirs = route_ref[me], route_ref[me ^ bit]
    for offset, out in zip(offsets, outs):
        row = me ^ offset
        masked_sum(out, 0, [(mine == row, own_ref), (theirs == row, got_ref)])


def give_back(part, way, route):
    groups = route.shape[0]
    layers = part.shape[0]
    bits = bits_of(groups)[:: 1 if way == 0 else -1]
    got = swap_over("shot", groups, bits[0], part)
    offsets = [0]
    for b in reversed(bits[1:]):
        offsets = offsets + [o ^ b for o in offsets]
    types = [BF16 if o & bits[1] else F32 for o in offsets]
    sums = call(
        lambda *refs: bucket_kernel(offsets, bits[0], *refs),
        [(part.shape, kind) for kind in types], [route, part, got],
    )
    left = dict(zip(offsets, sums))
    for b in bits[1:]:
        away = [o for o in left if o & b]
        block = jnp.concatenate([left[o].astype(BF16) for o in away], axis=0)
        came = swap_over("shot", groups, b, block)
        left = {
            o ^ b: left[o ^ b] + came[n * layers : (n + 1) * layers].astype(F32)
            for n, o in enumerate(away)
        }
    return left[0]


def inner(vel_model, den_model, cover, receivers, observed, p_now, p_before, q_now, q_before):
    layers, width, depth = p_now.shape[1:]
    tall = width + 2 * PAD
    narrow, padded = ((layers, width, depth), F32), ((layers, tall, depth), F32)
    half, flat = ((layers, width, depth), BF16), ((layers * tall, depth), F32)
    z_scratch = [pltpu.VMEM((layers, width, 2 * depth), F32)]
    matrix = z_matrix(depth)
    seen = observed[0]

    size = width // PARTS
    part_half = ((layers, size, depth), BF16)
    parts = range(PARTS)

    groups = cover.shape[0]
    (route,) = call(routes_kernel, [((groups, 16, depth), jnp.int32)], [cover], [SM])

    p, p_half = call(prepare_kernel, [padded, half], [p_now[0]])
    n_rec = receivers.shape[1]
    (lists,) = call(
        lambda rec, out: list_kernel(rec, layers, width, depth, out),
        [((4, n_rec), jnp.int32)], [receivers],
    )
    on, off = paired(p_half), across(p_half)
    kept = {}

    def tie(held):
        held, kept["p"] = lax.optimization_barrier((held, p))
        return held

    den, *den_parts = fetch(den_model[0], route, PARTS, tie)
    (vel,) = fetch(vel_model[0], route)
    p, offs = kept["p"], [off] * PARTS

    before = p_before[0]
    log_den, s2, s3 = call(log_kernel, [padded, narrow, narrow], [den, matrix, before], scratch=z_scratch)
    on_den = paired(den)
    off_den = [across(den_part) for den_part in den_parts]
    slopes = [()]
    for k in parts:
        ins = [log_den, on_den, off_den[k], vel]
        slopes.append(
            call(
                lambda *refs, k=k: slope_x_kernel(k, *refs),
                [narrow, narrow], [*ins, *slopes[-1]],
                aliases={len(ins) + n: n for n in range(len(slopes[-1]))},
            )
        )

    stored, fields = [], []
    for step in range(ITERS):
        part, d_y, d_z = call(forward_yz_kernel, [narrow] * 3, [p, s2, s3, matrix], scratch=z_scratch)
        if step > 0:
            fields.append(p.reshape(flat[0]))
        sending = step < ITERS - 1
        made, sends = (), []
        for k in parts:
            s1, scale = slopes[1 + k] if step == 0 else slopes[-1]
            ins = [p, on, offs[k], part, s1, scale, before]
            outs = call(
                lambda *refs, k=k, sending=sending: forward_x_kernel(k, sending, *refs),
                [narrow, narrow, padded] + ([half, part_half] if sending else []), [*ins, *made],
                aliases={len(ins) + n: n for n in range(len(made))},
            )
            made = outs[: 4 if sending else 3]
            if sending:
                sends.append(across(outs[4]))
        d_x, applied, later = made[:3]
        if sending:
            on, offs = paired(made[3]), sends
        stored.append((applied, d_x, d_y, d_z))
        before, p = p, later

    (q,) = call(prepare_kernel, [padded], [q_now[0]])
    a, a_half, *sends = call(
        lambda *refs: first_adjoint_kernel(ITERS - 1, *refs),
        [flat, half] + [part_half] * PARTS, [p.reshape(flat[0]), q.reshape(flat[0]), lists, seen],
        [VM, VM, SM, SM],
    )
    offs = [across(send) for send in sends]
    on = paired(a_half)
    a = a.reshape(padded[0])
    sources = []
    for first, some in ((0, fields[:-1]), (len(fields) - 1, fields[-1:])):
        sources += call(
            lambda *refs, first=first: receivers_kernel(first, *refs),
            [flat] * len(some), [*some, lists, seen], [VM] * len(some) + [SM, SM],
        )
    sources = [source.reshape(padded[0]) for source in sources]
    before, current = q_before[0], q
    sums = ()
    for step in range(ITERS - 1):
        f_applied, f_dx, f_dy, f_dz = stored[ITERS - 1 - step]
        last = step == ITERS - 2
        part, sum_vel, sum_den = call(
            lambda *refs, first=step == 0: adjoint_yz_kernel(first, *refs),
            [narrow] * 3, [a, s2, s3, matrix, f_dy, f_dz, f_applied, *sums], scratch=z_scratch,
        )
        extra = [sum_vel, stored[0][0], vel] if last else []
        made, sends, shot_vel = (), [], []
        for k in parts:
            ins = [
                a, on, offs[k], part, s1, scale, before, sources[ITERS - 2 - step], f_dx, sum_den, *extra,
            ]
            kinds = [padded, half, narrow] + ([] if last else [narrow])
            outs = call(
                lambda *refs, k=k, last=last: adjoint_x_kernel(k, last, *refs),
                kinds + [part_half] * (2 if last else 1), [*ins, *made],
                aliases={len(ins) + n: n for n in range(len(made))},
            )
            made = outs[: len(kinds)]
            sends.append(across(outs[len(kinds)]))
            shot_vel += outs[len(kinds) + 1 :]
        a, a_half, sum_den, *later = made
        on, offs = paired(a_half), sends
        if not last:
            before, current = current, later[0]
        sums = (sum_vel, sum_den)
    _, f_dx, f_dy, f_dz = stored[0]
    grad_vel = [give_back(shot_vel[k], k, route) for k in parts]
    (sum_den,) = call(last_yz_kernel, [narrow], [a, matrix, f_dy, f_dz, sum_den], scratch=z_scratch)
    grad_den = []
    for k in parts:
        (shot_den,) = call(
            lambda *refs, k=k: last_x_kernel(k, *refs),
            [part_half], [a, on, offs[k], f_dx, sum_den, scale, den],
        )
        grad_den.append(give_back(shot_den, k, route))
    return jnp.concatenate(grad_vel, axis=1)[None], jnp.concatenate(grad_den, axis=1)[None]


def solution(mesh):
    spec = P("shot", "sub", None, None)
    return jax.shard_map(
        inner,
        mesh=mesh,
        in_specs=(spec, spec, P(), P("shot", None), P("shot", None, None), spec, spec, spec, spec),
        out_specs=(spec, spec),
        check_vma=False,
    )
```

```python
import math

import jax
import jax.numpy as jnp
import numpy as np
from jax import lax
from jax.experimental import pallas as pl
from jax.experimental.pallas import tpu as pltpu
from jax.sharding import PartitionSpec as P


ITERS = 4
SECOND = (-205.0 / 72.0, 8.0 / 5.0, -1.0 / 5.0, 8.0 / 315.0, -1.0 / 560.0)
FIRST = (4.0 / 5.0, -1.0 / 5.0, 4.0 / 105.0, -1.0 / 280.0)
SPEED = 0.15
PAD = 8
PARTS = 2
UNROLL = 4
F32, BF16 = jnp.float32, jnp.bfloat16
VMEM_LIMIT = 4 << 20

VM = pl.BlockSpec(memory_space=pltpu.VMEM)
SM = pl.BlockSpec(memory_space=pltpu.SMEM)


def call(kernel, outs, ins, specs=None, out_specs=None, scratch=(), flops=0, aliases=None):
    outs = tuple(jax.ShapeDtypeStruct(shape, dtype) for shape, dtype in outs)
    moved_bytes = sum(math.prod(x.shape) * x.dtype.itemsize for x in (*ins, *outs))
    return pl.pallas_call(
        kernel,
        out_shape=outs,
        in_specs=list(specs or [VM] * len(ins)),
        out_specs=tuple(out_specs or [VM] * len(outs)),
        scratch_shapes=list(scratch),
        input_output_aliases=aliases or {},
        cost_estimate=pl.CostEstimate(flops=flops, bytes_accessed=moved_bytes, transcendentals=0),
        compiler_params=pltpu.CompilerParams(vmem_limit_bytes=VMEM_LIMIT),
    )(*ins)


def weighted(pairs):
    lap, first = None, None
    for m, (ahead, behind) in enumerate(pairs, 1):
        s = SECOND[m] * (ahead + behind)
        t = FIRST[m - 1] * (ahead - behind)
        lap = s if lap is None else lap + s
        first = t if first is None else first + t
    return lap, first


def y_pairs(ref, layer, row, rows):
    return [
        (ref[layer, pl.ds(row + m, rows), :], ref[layer, pl.ds(row - m, rows), :])
        for m in range(1, 5)
    ]


def z_matrix(depth):
    both = np.zeros((depth, 2 * depth), np.float64)
    for out in range(depth):
        for m in range(1, 5):
            for source, sign in ((out + m, 1.0), (out - m, -1.0)):
                if 0 <= source < depth:
                    both[source, out] += SECOND[m]
                    both[source, depth + out] += sign * FIRST[m - 1]
    high = both.astype(np.float32).astype(jnp.bfloat16)
    low = (both - high.astype(np.float64)).astype(np.float32).astype(jnp.bfloat16)
    return jnp.asarray(np.concatenate([high, high, low], axis=0))


def z_terms(f_ref, matrix_ref, z_ref):
    layers, width, _ = z_ref.shape
    for l in range(layers):
        f = f_ref[l, pl.ds(PAD, width), :]
        high = f.astype(BF16)
        low = (f - high.astype(F32)).astype(BF16)
        split = jnp.concatenate([high, low, high], axis=1)
        z_ref[l, :, :] = jnp.dot(split, matrix_ref[...], preferred_element_type=F32)


def where_am_i():
    column, columns = lax.axis_index("sub"), lax.axis_size("sub")
    even = (column & 1) == 0
    valid = jnp.logical_and(column > 0, column < columns - 1)
    return even, valid


def x_values(own, on_ref, off_ref, rows, off_rows):
    even, valid = where_am_i()
    count = len(own)
    on = [on_ref[l, rows, :].astype(F32) for l in range(count)]
    off = [jnp.where(valid, off_ref[l, off_rows, :].astype(F32), 0.0) for l in range(count)]
    low = [jnp.where(even, b, a) for a, b in zip(on, off)]
    high = [jnp.where(even, a, b) for a, b in zip(on, off)]
    return low[count - 4 :] + own + high[:4]


def part_rows(part, width, off_ref, body):
    size = width // PARTS
    first = part * size
    back = first if off_ref.shape[1] == size else 0

    @pl.loop(0, size // 16)
    def _(j):
        at = pl.multiple_of(first + 16 * j, 16)
        off_at = pl.multiple_of(first - back + 16 * j, 16)
        body(pl.ds(at, 16), pl.ds(off_at, 16), pl.ds(at + PAD, 16), pl.ds(pl.multiple_of(16 * j, 16), 16))


def x_pairs(values, layer):
    return [(values[4 + layer + m], values[4 + layer - m]) for m in range(1, 5)]


def zero_pads(ref):
    layers, tall, depth = ref.shape
    zeros = jnp.zeros((PAD, depth), F32)
    for l in range(layers):
        ref[l, pl.ds(0, PAD), :] = zeros
        ref[l, pl.ds(tall - PAD, PAD), :] = zeros


def prepare_kernel(p_ref, pw_ref, *half_refs):
    layers, width, _ = p_ref.shape
    zero_pads(pw_ref)

    @pl.loop(0, width // 16)
    def _(j):
        at = pl.multiple_of(16 * j, 16)
        for l in range(layers):
            v = p_ref[l, pl.ds(at, 16), :]
            pw_ref[l, pl.ds(at + PAD, 16), :] = v
            for half_ref in half_refs:
                half_ref[l, pl.ds(at, 16), :] = v.astype(BF16)


def list_kernel(rec_ref, layers, width, depth, list_ref):
    total = rec_ref.shape[1]
    cells = layers * width * depth
    local = rec_ref[...] - lax.axis_index("sub") * cells
    inside = jnp.logical_and(local >= 0, local < cells)
    line = lax.shift_right_arithmetic(local, depth.bit_length() - 1)
    row = line + PAD
    for l in range(1, layers):
        row += jnp.where(line >= l * width, 2 * PAD, 0)
    number = lax.broadcasted_iota(jnp.int32, (1, total), 1)
    down = lax.broadcasted_iota(jnp.int32, (total, total), 0)
    across_ = lax.broadcasted_iota(jnp.int32, (total, total), 1)
    earlier = jnp.where(down < across_, 1.0, 0.0).astype(BF16)
    counted = jnp.broadcast_to(jnp.where(inside, 1.0, 0.0), (8, total))
    place = jnp.dot(counted.astype(BF16), earlier, preferred_element_type=F32)[:1]
    place = jnp.where(inside, place.astype(jnp.int32), -1)
    spots = jnp.where(down == place, 1.0, 0.0).astype(BF16)
    pieces = [local & (depth - 1), row & 255, row >> 8, number & 255, number >> 8]
    kind = lax.broadcasted_iota(jnp.int32, (8, total), 0)
    values = jnp.zeros((8, total), jnp.int32)
    for n, piece in enumerate(pieces):
        values = jnp.where(kind == n, piece, values)
    listed = lax.dot_general(
        values.astype(F32).astype(BF16), spots, (((1,), (1,)), ((), ())), preferred_element_type=F32
    ).astype(jnp.int32)
    count = jnp.sum(counted[:1], axis=1, keepdims=True).astype(jnp.int32)
    list_ref[0:1, :] = listed[2:3] * 256 + listed[1:2]
    list_ref[1:2, :] = listed[3:4] + 256 * listed[4:5]
    list_ref[2:3, :] = jnp.broadcast_to(count, (1, total))
    list_ref[3:4, :] = jnp.where(number < count, listed[0:1], depth)


def add_receivers(n, field_ref, into_ref, list_ref, observed_ref):
    depth = field_ref.shape[1]
    lane = lax.broadcasted_iota(jnp.int32, (1, depth), 1)
    count = list_ref[2, 0]

    @pl.loop(0, (count + UNROLL - 1) // UNROLL)
    def _(c):
        rows, terms = [], []
        for k in range(UNROLL):
            row = list_ref[0, c * UNROLL + k]
            spot = list_ref[3, c * UNROLL + k]
            seen = observed_ref[n, list_ref[1, c * UNROLL + k]]
            rows.append(row)
            terms.append(jnp.where(lane == spot, field_ref[pl.ds(row, 1), :] - seen, 0.0))
        for row, term in zip(rows, terms):
            into_ref[pl.ds(row, 1), :] += term


def receivers_kernel(first, *refs):
    count = (len(refs) - 2) // 2
    fields, (list_ref, observed_ref), outs = refs[:count], refs[count : count + 2], refs[count + 2 :]
    for n, (field_ref, source_ref) in enumerate(zip(fields, outs)):
        source_ref[...] = jnp.zeros(source_ref.shape, F32)
        add_receivers(first + n, field_ref, source_ref, list_ref, observed_ref)


def first_adjoint_kernel(n, p_ref, q_ref, list_ref, observed_ref, a_ref, half_ref, *part_refs):
    a_ref[...] = q_ref[...]
    add_receivers(n, p_ref, a_ref, list_ref, observed_ref)
    layers, width, _ = half_ref.shape
    tall = width + 2 * PAD

    for n, part_ref in enumerate(part_refs):
        size = part_ref.shape[1]

        @pl.loop(0, size // 16)
        def _(j, n=n, size=size, part_ref=part_ref):
            at = pl.multiple_of(16 * j, 16)
            for l in range(layers):
                from_row = pl.multiple_of(at + n * size + l * tall + PAD, 8)
                value = a_ref[pl.ds(from_row, 16), :].astype(BF16)
                half_ref[l, pl.ds(pl.multiple_of(at + n * size, 16), 16), :] = value
                part_ref[l, pl.ds(at, 16), :] = value


def log_kernel(den_ref, matrix_ref, before_ref, log_ref, s2_ref, s3_ref, z_ref):
    layers, width, depth = den_ref.shape
    zero_pads(log_ref)

    @pl.loop(0, width // 16)
    def _(j):
        at = pl.multiple_of(16 * j, 16)
        for l in range(layers):
            log_ref[l, pl.ds(at + PAD, 16), :] = jnp.log(den_ref[l, pl.ds(at, 16), :].astype(F32))

    z_terms(log_ref, matrix_ref, z_ref)

    @pl.loop(0, width // 8)
    def _(j):
        at = pl.multiple_of(8 * j, 8)
        for l in range(layers):
            s2_ref[l, pl.ds(at, 8), :] = weighted(y_pairs(log_ref, l, at + PAD, 8))[1]
            s3_ref[l, pl.ds(at, 8), :] = z_ref[l, pl.ds(at, 8), pl.ds(depth, depth)]


def slope_x_kernel(part, log_ref, on_ref, off_ref, vel_ref, *refs):
    s1_ref, scale_ref = refs[-2:]
    layers, width, _ = s1_ref.shape
    even, valid = where_am_i()

    def body(rows, off_rows, wide, send_rows):
        own = [log_ref[l, wide, :] for l in range(layers)]
        on = [jnp.log(on_ref[l, rows, :].astype(F32)) for l in range(layers)]
        off = [jnp.log(jnp.where(valid, off_ref[l, off_rows, :].astype(F32), 1.0)) for l in range(layers)]
        low = [jnp.where(even, b, a) for a, b in zip(on, off)]
        high = [jnp.where(even, a, b) for a, b in zip(on, off)]
        values = low[layers - 4 :] + own + high[:4]
        for l in range(layers):
            s1_ref[l, rows, :] = weighted(x_pairs(values, l))[1]
            v = vel_ref[l, rows, :].astype(F32)
            scale_ref[l, rows, :] = SPEED * v * v

    part_rows(part, width, off_ref, body)


def yz_terms(f_ref, s2_ref, s3_ref, z_ref, l, at):
    f = f_ref[l, pl.ds(at + PAD, 8), :]
    lap_y, d_y = weighted(y_pairs(f_ref, l, at + PAD, 8))
    rows, depth = pl.ds(at, 8), f.shape[1]
    lap_z, d_z = z_ref[l, rows, pl.ds(0, depth)], z_ref[l, rows, pl.ds(depth, depth)]
    part = (3.0 * SECOND[0]) * f + lap_y + lap_z
    part = part - (s2_ref[l, rows, :] * d_y + s3_ref[l, rows, :] * d_z)
    return f, part, d_y, d_z


def forward_yz_kernel(f_ref, s2_ref, s3_ref, matrix_ref, part_ref, dy_ref, dz_ref, z_ref):
    layers, width, _ = part_ref.shape
    z_terms(f_ref, matrix_ref, z_ref)

    @pl.loop(0, width // 8)
    def _(j):
        at = pl.multiple_of(8 * j, 8)
        rows = pl.ds(at, 8)
        for l in range(layers):
            _, part, d_y, d_z = yz_terms(f_ref, s2_ref, s3_ref, z_ref, l, at)
            part_ref[l, rows, :] = part
            dy_ref[l, rows, :] = d_y
            dz_ref[l, rows, :] = d_z


def plain_yz_kernel(f_ref, matrix_ref, part_ref, dy_ref, dz_ref, z_ref):
    layers, width, depth = part_ref.shape
    z_terms(f_ref, matrix_ref, z_ref)

    @pl.loop(0, width // 8)
    def _(j):
        at = pl.multiple_of(8 * j, 8)
        rows = pl.ds(at, 8)
        for l in range(layers):
            lap_y, d_y = weighted(y_pairs(f_ref, l, at + PAD, 8))
            f = f_ref[l, pl.ds(at + PAD, 8), :]
            part_ref[l, rows, :] = (3.0 * SECOND[0]) * f + lap_y + z_ref[l, rows, pl.ds(0, depth)]
            dy_ref[l, rows, :] = d_y
            dz_ref[l, rows, :] = z_ref[l, rows, pl.ds(depth, depth)]


def forward_x_kernel(
    part, send, plain, f_ref, on_ref, off_ref, part_ref, s1_ref, scale_ref, before_ref, *refs
):
    if plain:
        s2_ref, s3_ref, dy_ref, dz_ref = refs[:4]
    sending = send
    if sending:
        dx_ref, applied_ref, next_ref, half_ref, send_ref = refs[-5:]
    else:
        dx_ref, applied_ref, next_ref = refs[-3:]
    layers, width, _ = part_ref.shape
    shift = before_ref.shape[1] != width
    if part == 0:
        zero_pads(next_ref)

    def body(rows, off_rows, wide, send_rows):
        own = [f_ref[l, wide, :] for l in range(layers)]
        values = x_values(own, on_ref, off_ref, rows, off_rows)
        for l in range(layers):
            lap, d_x = weighted(x_pairs(values, l))
            applied = part_ref[l, rows, :] + (lap - s1_ref[l, rows, :] * d_x)
            if plain:
                applied = applied - (
                    s2_ref[l, rows, :] * dy_ref[l, rows, :] + s3_ref[l, rows, :] * dz_ref[l, rows, :]
                )
            before = before_ref[l, wide if shift else rows, :]
            later = 2.0 * own[l] - before + scale_ref[l, rows, :] * applied
            dx_ref[l, rows, :] = d_x
            applied_ref[l, rows, :] = applied
            next_ref[l, wide, :] = later
            if sending:
                narrow = later.astype(BF16)
                half_ref[l, rows, :] = narrow
                send_ref[l, send_rows, :] = narrow

    part_rows(part, width, off_ref, body)


def adjoint_yz_kernel(
    first, f_ref, s2_ref, s3_ref, matrix_ref, fdy_ref, fdz_ref, fapplied_ref, *refs,
):
    if first:
        part_ref, vel_ref, den_ref, z_ref = refs
    else:
        vel_in, den_in, part_ref, vel_ref, den_ref, z_ref = refs
    layers, width, _ = part_ref.shape
    z_terms(f_ref, matrix_ref, z_ref)

    @pl.loop(0, width // 8)
    def _(j):
        at = pl.multiple_of(8 * j, 8)
        rows = pl.ds(at, 8)
        for l in range(layers):
            f, part, d_y, d_z = yz_terms(f_ref, s2_ref, s3_ref, z_ref, l, at)
            part_ref[l, rows, :] = part
            sum_vel = f * fapplied_ref[l, rows, :]
            sum_den = d_y * fdy_ref[l, rows, :] + d_z * fdz_ref[l, rows, :]
            if not first:
                sum_vel = vel_in[l, rows, :] + sum_vel
                sum_den = den_in[l, rows, :] + sum_den
            vel_ref[l, rows, :] = sum_vel
            den_ref[l, rows, :] = sum_den


def adjoint_x_kernel(
    part, last, f_ref, on_ref, off_ref, part_ref, s1_ref, scale_ref, before_ref,
    source_ref, fdx_ref, den_in, *refs,
):
    if last:
        vel_in, fapplied_ref, vmodel_ref = refs[:3]
        a_ref, half_ref, den_ref, send_ref, shot_ref = refs[-5:]
    else:
        a_ref, half_ref, den_ref, q_ref, send_ref = refs[-5:]
    layers, width, _ = part_ref.shape
    shift = before_ref.shape[1] != width
    if part == 0:
        zero_pads(a_ref)

    def body(rows, off_rows, wide, send_rows):
        own = [f_ref[l, wide, :] for l in range(layers)]
        values = x_values(own, on_ref, off_ref, rows, off_rows)
        for l in range(layers):
            lap, d_x = weighted(x_pairs(values, l))
            applied = part_ref[l, rows, :] + (lap - s1_ref[l, rows, :] * d_x)
            before = before_ref[l, wide if shift else rows, :]
            later = 2.0 * own[l] - before + scale_ref[l, rows, :] * applied
            if not last:
                q_ref[l, rows, :] = later
            adjoint = later + source_ref[l, wide, :]
            a_ref[l, wide, :] = adjoint
            narrow = adjoint.astype(BF16)
            half_ref[l, rows, :] = narrow
            send_ref[l, send_rows, :] = narrow
            den_ref[l, rows, :] = den_in[l, rows, :] + d_x * fdx_ref[l, rows, :]
            if last:
                total = vel_in[l, rows, :] + adjoint * fapplied_ref[l, rows, :]
                v = vmodel_ref[l, rows, :].astype(F32)
                shot_ref[l, send_rows, :] = ((2.0 * SPEED) * v * total).astype(BF16)

    part_rows(part, width, off_ref, body)


def last_yz_kernel(f_ref, matrix_ref, fdy_ref, fdz_ref, den_in, den_ref, z_ref):
    layers, width, depth = den_ref.shape
    z_terms(f_ref, matrix_ref, z_ref)

    @pl.loop(0, width // 8)
    def _(j):
        at = pl.multiple_of(8 * j, 8)
        rows = pl.ds(at, 8)
        for l in range(layers):
            d_y = weighted(y_pairs(f_ref, l, at + PAD, 8))[1]
            d_z = z_ref[l, rows, pl.ds(depth, depth)]
            den_ref[l, rows, :] = den_in[l, rows, :] + (
                d_y * fdy_ref[l, rows, :] + d_z * fdz_ref[l, rows, :]
            )


def last_x_kernel(part, f_ref, on_ref, off_ref, fdx_ref, den_in, scale_ref, dmodel_ref, shot_ref):
    layers, width, _ = den_in.shape

    def body(rows, off_rows, wide, send_rows):
        own = [f_ref[l, wide, :] for l in range(layers)]
        values = x_values(own, on_ref, off_ref, rows, off_rows)
        for l in range(layers):
            d_x = weighted(x_pairs(values, l))[1]
            total = den_in[l, rows, :] + d_x * fdx_ref[l, rows, :]
            density = dmodel_ref[l, rows, :].astype(F32)
            shot_ref[l, send_rows, :] = (scale_ref[l, rows, :] / density * total).astype(BF16)

    part_rows(part, width, off_ref, body)


def swap_over(axis, count, bit, value):
    return lax.ppermute(value, axis, [(i, i ^ bit) for i in range(count)])


def paired(half):
    count = lax.axis_size("sub")
    return lax.ppermute(half, "sub", [(i, i ^ 1) for i in range(count)])


def across(half, ring=False):
    groups, count = lax.axis_size("shot"), lax.axis_size("sub")
    pairs = []
    for s in range(groups):
        for i in range(1, count - 1, 2):
            pairs += [(s * count + i, s * count + i + 1), (s * count + i + 1, s * count + i)]
        if ring:
            pairs += [(s * count, s * count + count - 1), (s * count + count - 1, s * count)]
        elif groups % 2 == 0:
            for i in (0, count - 1):
                pairs.append((s * count + i, (s ^ 1) * count + i))
    return lax.ppermute(half, ("shot", "sub"), pairs)


def bits_of(groups):
    return [1 << k for k in range(groups.bit_length() - 1)]


def routes_kernel(cover_ref, out_ref):
    column = lax.axis_index("sub")
    for g in range(out_ref.shape[0]):
        out_ref[g, :, :] = jnp.full(out_ref.shape[1:], cover_ref[g, column], jnp.int32)


def masked_sum(out_ref, first, terms):
    layers, width, _ = terms[0][1].shape

    @pl.loop(0, width // 16)
    def _(j):
        rows = pl.ds(pl.multiple_of(16 * j, 16), 16)
        for l in range(layers):
            total = None
            for mask, ref in terms:
                term = jnp.where(mask, ref[l, rows, :].astype(F32), 0.0)
                total = term if total is None else total + term
            out_ref[first + l, rows, :] = total.astype(out_ref.dtype)


def pick_kernel(offsets, bits, route_ref, *refs):
    me = lax.axis_index("shot")
    outs = refs[-2:]
    count = len(refs) // 2 - 1
    for way in range(2):
        row = route_ref[me ^ bits[way]]
        held = refs[way * count : (way + 1) * count]
        masked_sum(outs[way], 0, [(row == (me ^ o), ref) for o, ref in zip(offsets[way], held)])


def gather_kernel(offsets, bits, parts, route_ref, *refs):
    me = lax.axis_index("shot")
    part_refs = refs[len(refs) - parts :]
    refs = refs[: len(refs) - parts]
    out_ref = refs[-1]
    count = (len(refs) - 1) // 2
    mine = route_ref[me]
    layers = out_ref.shape[0] // 2
    for way in range(2):
        *near, far = refs[way * count : (way + 1) * count]
        terms = [(mine == (me ^ o), ref) for o, ref in zip(offsets[way], near)]
        terms.append(((mine & bits[way]) != (me & bits[way]), far))
        masked_sum(out_ref, way * layers, terms)
    for n, part_ref in enumerate(part_refs):
        size = part_ref.shape[1]
        part_ref[...] = out_ref[:, n * size : (n + 1) * size, :]


def fetch(tile, route, parts=0, tie=lambda x: x):
    groups = route.shape[0]
    layers = tile.shape[0] // 2
    small = (layers, *tile.shape[1:])
    ways = [bits_of(groups), bits_of(groups)[::-1]]
    held = [[tile[:layers]], [tile[layers:]]]
    offsets = [[0], [0]]
    for stage in range(len(ways[0]) - 1):
        for way in range(2):
            bit = ways[way][stage]
            block = jnp.concatenate(held[way], axis=0) if len(held[way]) > 1 else held[way][0]
            got = swap_over("shot", groups, bit, block)
            held[way] = held[way] + [
                lax.slice_in_dim(got, n * layers, (n + 1) * layers, axis=0)
                for n in range(len(held[way]))
            ]
            offsets[way] = offsets[way] + [o ^ bit for o in offsets[way]]
    last = [way[-1] for way in ways]
    held = tie(held)
    sends = call(
        lambda *refs: pick_kernel(offsets, last, *refs),
        [(small, BF16)] * 2, [route, *held[0], *held[1]],
    )
    far = [swap_over("shot", groups, last[way], sends[way]) for way in range(2)]
    part_shape = (tile.shape[0], tile.shape[1] // PARTS, tile.shape[2])
    return call(
        lambda *refs: gather_kernel(offsets, last, parts, *refs),
        [(tile.shape, BF16)] + [(part_shape, BF16)] * parts, [route, *held[0], far[0], *held[1], far[1]],
    )


def bucket_kernel(offsets, bit, route_ref, own_ref, got_ref, *outs):
    me = lax.axis_index("shot")
    mine, theirs = route_ref[me], route_ref[me ^ bit]
    for offset, out in zip(offsets, outs):
        row = me ^ offset
        masked_sum(out, 0, [(mine == row, own_ref), (theirs == row, got_ref)])


def give_back(part, way, route):
    groups = route.shape[0]
    layers = part.shape[0]
    bits = bits_of(groups)[:: 1 if way == 0 else -1]
    got = swap_over("shot", groups, bits[0], part)
    offsets = [0]
    for b in reversed(bits[1:]):
        offsets = offsets + [o ^ b for o in offsets]
    types = [BF16 if o & bits[1] else F32 for o in offsets]
    sums = call(
        lambda *refs: bucket_kernel(offsets, bits[0], *refs),
        [(part.shape, kind) for kind in types], [route, part, got],
    )
    left = dict(zip(offsets, sums))
    for b in bits[1:]:
        away = [o for o in left if o & b]
        block = jnp.concatenate([left[o].astype(BF16) for o in away], axis=0)
        came = swap_over("shot", groups, b, block)
        left = {
            o ^ b: left[o ^ b] + came[n * layers : (n + 1) * layers].astype(F32)
            for n, o in enumerate(away)
        }
    return left[0]


def inner(vel_model, den_model, cover, receivers, observed, p_now, p_before, q_now, q_before):
    layers, width, depth = p_now.shape[1:]
    tall = width + 2 * PAD
    narrow, padded = ((layers, width, depth), F32), ((layers, tall, depth), F32)
    half, flat = ((layers, width, depth), BF16), ((layers * tall, depth), F32)
    z_scratch = [pltpu.VMEM((layers, width, 2 * depth), F32)]
    matrix = z_matrix(depth)
    seen = observed[0]

    size = width // PARTS
    part_half = ((layers, size, depth), BF16)
    parts = range(PARTS)

    groups = cover.shape[0]
    (route,) = call(routes_kernel, [((groups, 16, depth), jnp.int32)], [cover], [SM])

    p, p_half = call(prepare_kernel, [padded, half], [p_now[0]])
    n_rec = receivers.shape[1]
    (lists,) = call(
        lambda rec, out: list_kernel(rec, layers, width, depth, out),
        [((4, n_rec), jnp.int32)], [receivers],
    )
    on, off = paired(p_half), across(p_half, ring=True)
    kept = {}

    def tie(held):
        held, kept["p"] = lax.optimization_barrier((held, p))
        return held

    den, *den_parts = fetch(den_model[0], route, PARTS, tie)
    (vel,) = fetch(vel_model[0], route)
    p, offs = kept["p"], [off] * PARTS

    before = p_before[0]
    log_den, s2, s3 = call(log_kernel, [padded, narrow, narrow], [den, matrix, before], scratch=z_scratch)
    on_den = paired(den)
    off_den = [across(den_part) for den_part in den_parts]
    slopes = [()]
    for k in parts:
        ins = [log_den, on_den, off_den[k], vel]
        slopes.append(
            call(
                lambda *refs, k=k: slope_x_kernel(k, *refs),
                [narrow, narrow], [*ins, *slopes[-1]],
                aliases={len(ins) + n: n for n in range(len(slopes[-1]))},
            )
        )

    stored, fields = [], []
    for step in range(ITERS):
        plain = step == 0
        part, d_y, d_z = call(
            plain_yz_kernel if plain else forward_yz_kernel, [narrow] * 3,
            [p, matrix] if plain else [p, s2, s3, matrix], scratch=z_scratch,
        )
        if step > 0:
            fields.append(p.reshape(flat[0]))
        sending = step < ITERS - 1
        made, sends = (), []
        for k in parts:
            s1, scale = slopes[1 + k] if step == 0 else slopes[-1]
            ins = [p, on, offs[k], part, s1, scale, before] + ([s2, s3, d_y, d_z] if plain else [])
            outs = call(
                lambda *refs, k=k, sending=sending, plain=plain: forward_x_kernel(k, sending, plain, *refs),
                [narrow, narrow, padded] + ([half, part_half] if sending else []), [*ins, *made],
                aliases={len(ins) + n: n for n in range(len(made))},
            )
            made = outs[: 4 if sending else 3]
            if sending:
                sends.append(across(outs[4]))
        d_x, applied, later = made[:3]
        if sending:
            on, offs = paired(made[3]), sends
        stored.append((applied, d_x, d_y, d_z))
        before, p = p, later

    (q,) = call(prepare_kernel, [padded], [q_now[0]])
    a, a_half, *sends = call(
        lambda *refs: first_adjoint_kernel(ITERS - 1, *refs),
        [flat, half] + [part_half] * PARTS, [p.reshape(flat[0]), q.reshape(flat[0]), lists, seen],
        [VM, VM, SM, SM],
    )
    offs = [across(send) for send in sends]
    on = paired(a_half)
    a = a.reshape(padded[0])
    sources = []
    for first, some in ((0, fields[:1]), (1, fields[1:])):
        sources += call(
            lambda *refs, first=first: receivers_kernel(first, *refs),
            [flat] * len(some), [*some, lists, seen], [VM] * len(some) + [SM, SM],
        )
    sources = [source.reshape(padded[0]) for source in sources]
    before, current = q_before[0], q
    sums = ()
    for step in range(ITERS - 1):
        f_applied, f_dx, f_dy, f_dz = stored[ITERS - 1 - step]
        last = step == ITERS - 2
        part, sum_vel, sum_den = call(
            lambda *refs, first=step == 0: adjoint_yz_kernel(first, *refs),
            [narrow] * 3, [a, s2, s3, matrix, f_dy, f_dz, f_applied, *sums], scratch=z_scratch,
        )
        extra = [sum_vel, stored[0][0], vel] if last else []
        made, sends, shot_vel = (), [], []
        for k in parts:
            ins = [
                a, on, offs[k], part, s1, scale, before, sources[ITERS - 2 - step], f_dx, sum_den, *extra,
            ]
            kinds = [padded, half, narrow] + ([] if last else [narrow])
            outs = call(
                lambda *refs, k=k, last=last: adjoint_x_kernel(k, last, *refs),
                kinds + [part_half] * (2 if last else 1), [*ins, *made],
                aliases={len(ins) + n: n for n in range(len(made))},
            )
            made = outs[: len(kinds)]
            sends.append(across(outs[len(kinds)]))
            shot_vel += outs[len(kinds) + 1 :]
        a, a_half, sum_den, *later = made
        on, offs = paired(a_half), sends
        if not last:
            before, current = current, later[0]
        sums = (sum_vel, sum_den)
    _, f_dx, f_dy, f_dz = stored[0]
    grad_vel = [give_back(shot_vel[k], k, route) for k in parts]
    (sum_den,) = call(last_yz_kernel, [narrow], [a, matrix, f_dy, f_dz, sum_den], scratch=z_scratch)
    grad_den = []
    for k in parts:
        (shot_den,) = call(
            lambda *refs, k=k: last_x_kernel(k, *refs),
            [part_half], [a, on, offs[k], f_dx, sum_den, scale, den],
        )
        grad_den.append(give_back(shot_den, k, route))
    return jnp.concatenate(grad_vel, axis=1)[None], jnp.concatenate(grad_den, axis=1)[None]


def solution(mesh):
    spec = P("shot", "sub", None, None)
    return jax.shard_map(
        inner,
        mesh=mesh,
        in_specs=(spec, spec, P(), P("shot", None), P("shot", None, None), spec, spec, spec, spec),
        out_specs=(spec, spec),
        check_vma=False,
    )
```

```python
import math

import jax
import jax.numpy as jnp
import numpy as np
from jax import lax
from jax.experimental import pallas as pl
from jax.experimental.pallas import tpu as pltpu
from jax.sharding import PartitionSpec as P


ITERS = 4
SECOND = (-205.0 / 72.0, 8.0 / 5.0, -1.0 / 5.0, 8.0 / 315.0, -1.0 / 560.0)
FIRST = (4.0 / 5.0, -1.0 / 5.0, 4.0 / 105.0, -1.0 / 280.0)
SPEED = 0.15
SHOT, SUB = "shot", "sub"
PAD = 8
PARTS = 2
UNROLL = 4
F32, BF16 = jnp.float32, jnp.bfloat16
VMEM_LIMIT = 4 << 20

VM = pl.BlockSpec(memory_space=pltpu.VMEM)
SM = pl.BlockSpec(memory_space=pltpu.SMEM)


def call(kernel, outs, ins, specs=None, out_specs=None, scratch=(), flops=0, aliases=None):
    outs = tuple(jax.ShapeDtypeStruct(shape, dtype) for shape, dtype in outs)
    moved_bytes = sum(math.prod(x.shape) * x.dtype.itemsize for x in (*ins, *outs))
    return pl.pallas_call(
        kernel,
        out_shape=outs,
        in_specs=list(specs or [VM] * len(ins)),
        out_specs=tuple(out_specs or [VM] * len(outs)),
        scratch_shapes=list(scratch),
        input_output_aliases=aliases or {},
        cost_estimate=pl.CostEstimate(flops=flops, bytes_accessed=moved_bytes, transcendentals=0),
        compiler_params=pltpu.CompilerParams(vmem_limit_bytes=VMEM_LIMIT),
    )(*ins)


def weighted(pairs):
    lap, first = None, None
    for m, (ahead, behind) in enumerate(pairs, 1):
        s = SECOND[m] * (ahead + behind)
        t = FIRST[m - 1] * (ahead - behind)
        lap = s if lap is None else lap + s
        first = t if first is None else first + t
    return lap, first


def y_pairs(ref, layer, row, rows):
    return [
        (ref[layer, pl.ds(row + m, rows), :], ref[layer, pl.ds(row - m, rows), :])
        for m in range(1, 5)
    ]


def z_matrix(depth):
    both = np.zeros((depth, 2 * depth), np.float64)
    for out in range(depth):
        for m in range(1, 5):
            for source, sign in ((out + m, 1.0), (out - m, -1.0)):
                if 0 <= source < depth:
                    both[source, out] += SECOND[m]
                    both[source, depth + out] += sign * FIRST[m - 1]
    high = both.astype(np.float32).astype(jnp.bfloat16)
    low = (both - high.astype(np.float64)).astype(np.float32).astype(jnp.bfloat16)
    return jnp.asarray(np.concatenate([high, high, low], axis=0))


def z_terms(f_ref, matrix_ref, z_ref):
    layers, width, _ = z_ref.shape
    for l in range(layers):
        f = f_ref[l, pl.ds(PAD, width), :]
        high = f.astype(BF16)
        low = (f - high.astype(F32)).astype(BF16)
        split = jnp.concatenate([high, low, high], axis=1)
        z_ref[l, :, :] = jnp.dot(split, matrix_ref[...], preferred_element_type=F32)


def where_am_i():
    column, columns = lax.axis_index(SUB), lax.axis_size(SUB)
    even = (column & 1) == 0
    valid = jnp.logical_and(column > 0, column < columns - 1)
    return even, valid


def x_values(own, on_ref, off_ref, rows, off_rows):
    even, valid = where_am_i()
    count = len(own)
    on = [on_ref[l, rows, :].astype(F32) for l in range(count)]
    off = [jnp.where(valid, off_ref[l, off_rows, :].astype(F32), 0.0) for l in range(count)]
    low = [jnp.where(even, b, a) for a, b in zip(on, off)]
    high = [jnp.where(even, a, b) for a, b in zip(on, off)]
    return low[count - 4 :] + own + high[:4]


def part_rows(part, width, off_ref, body):
    size = width // PARTS
    first = part * size
    back = first if off_ref.shape[1] == size else 0

    @pl.loop(0, size // 16)
    def _(j):
        at = pl.multiple_of(first + 16 * j, 16)
        off_at = pl.multiple_of(first - back + 16 * j, 16)
        body(pl.ds(at, 16), pl.ds(off_at, 16), pl.ds(at + PAD, 16), pl.ds(pl.multiple_of(16 * j, 16), 16))


def x_pairs(values, layer):
    return [(values[4 + layer + m], values[4 + layer - m]) for m in range(1, 5)]


def zero_pads(ref):
    layers, tall, depth = ref.shape
    zeros = jnp.zeros((PAD, depth), F32)
    for l in range(layers):
        ref[l, pl.ds(0, PAD), :] = zeros
        ref[l, pl.ds(tall - PAD, PAD), :] = zeros


def prepare_kernel(p_ref, pw_ref, *half_refs):
    layers, width, _ = p_ref.shape
    zero_pads(pw_ref)

    @pl.loop(0, width // 16)
    def _(j):
        at = pl.multiple_of(16 * j, 16)
        for l in range(layers):
            v = p_ref[l, pl.ds(at, 16), :]
            pw_ref[l, pl.ds(at + PAD, 16), :] = v
            for half_ref in half_refs:
                half_ref[l, pl.ds(at, 16), :] = v.astype(BF16)


def list_kernel(rec_ref, layers, width, depth, list_ref):
    total = rec_ref.shape[1]
    cells = layers * width * depth
    local = rec_ref[...] - lax.axis_index(SUB) * cells
    inside = jnp.logical_and(local >= 0, local < cells)
    line = lax.shift_right_arithmetic(local, depth.bit_length() - 1)
    row = line + PAD
    for l in range(1, layers):
        row += jnp.where(line >= l * width, 2 * PAD, 0)
    number = lax.broadcasted_iota(jnp.int32, (1, total), 1)
    down = lax.broadcasted_iota(jnp.int32, (total, total), 0)
    across_ = lax.broadcasted_iota(jnp.int32, (total, total), 1)
    earlier = jnp.where(down < across_, 1.0, 0.0).astype(BF16)
    counted = jnp.broadcast_to(jnp.where(inside, 1.0, 0.0), (8, total))
    place = jnp.dot(counted.astype(BF16), earlier, preferred_element_type=F32)[:1]
    place = jnp.where(inside, place.astype(jnp.int32), -1)
    spots = jnp.where(down == place, 1.0, 0.0).astype(BF16)
    pieces = [local & (depth - 1), row & 255, row >> 8, number & 255, number >> 8]
    kind = lax.broadcasted_iota(jnp.int32, (8, total), 0)
    values = jnp.zeros((8, total), jnp.int32)
    for n, piece in enumerate(pieces):
        values = jnp.where(kind == n, piece, values)
    listed = lax.dot_general(
        values.astype(F32).astype(BF16), spots, (((1,), (1,)), ((), ())), preferred_element_type=F32
    ).astype(jnp.int32)
    count = jnp.sum(counted[:1], axis=1, keepdims=True).astype(jnp.int32)
    list_ref[0:1, :] = listed[2:3] * 256 + listed[1:2]
    list_ref[1:2, :] = listed[3:4] + 256 * listed[4:5]
    list_ref[2:3, :] = jnp.broadcast_to(count, (1, total))
    list_ref[3:4, :] = jnp.where(number < count, listed[0:1], depth)


def add_receivers(jobs, list_ref, observed_ref):
    depth = jobs[0][1].shape[1]
    lane = lax.broadcasted_iota(jnp.int32, (1, depth), 1)
    count = list_ref[2, 0]

    @pl.loop(0, (count + UNROLL - 1) // UNROLL)
    def _(c):
        rows, terms = [], []
        for k in range(UNROLL):
            row = list_ref[0, c * UNROLL + k]
            number = list_ref[1, c * UNROLL + k]
            here = lane == list_ref[3, c * UNROLL + k]
            rows.append(row)
            terms.append(
                [
                    jnp.where(here, field_ref[pl.ds(row, 1), :] - observed_ref[n, number], 0.0)
                    for n, field_ref, _ in jobs
                ]
            )
        for row, parts in zip(rows, terms):
            for (_, _, into_ref), term in zip(jobs, parts):
                into_ref[pl.ds(row, 1), :] += term


def receivers_kernel(first, *refs):
    count = (len(refs) - 2) // 2
    fields, (list_ref, observed_ref), outs = refs[:count], refs[count : count + 2], refs[count + 2 :]
    for source_ref in outs:
        source_ref[...] = jnp.zeros(source_ref.shape, F32)
    steps = range(first, first + count)
    add_receivers(list(zip(steps, fields, outs)), list_ref, observed_ref)


def first_adjoint_kernel(n, p_ref, q_ref, list_ref, observed_ref, a_ref, half_ref, *part_refs):
    a_ref[...] = q_ref[...]
    add_receivers([(n, p_ref, a_ref)], list_ref, observed_ref)
    layers, width, _ = half_ref.shape
    tall = width + 2 * PAD

    for n, part_ref in enumerate(part_refs):
        size = part_ref.shape[1]

        @pl.loop(0, size // 16)
        def _(j, n=n, size=size, part_ref=part_ref):
            at = pl.multiple_of(16 * j, 16)
            for l in range(layers):
                from_row = pl.multiple_of(at + n * size + l * tall + PAD, 8)
                value = a_ref[pl.ds(from_row, 16), :].astype(BF16)
                half_ref[l, pl.ds(pl.multiple_of(at + n * size, 16), 16), :] = value
                part_ref[l, pl.ds(at, 16), :] = value


def log_kernel(den_ref, matrix_ref, before_ref, log_ref, s2_ref, s3_ref, z_ref):
    layers, width, depth = den_ref.shape
    zero_pads(log_ref)

    @pl.loop(0, width // 16)
    def _(j):
        at = pl.multiple_of(16 * j, 16)
        for l in range(layers):
            log_ref[l, pl.ds(at + PAD, 16), :] = jnp.log(den_ref[l, pl.ds(at, 16), :].astype(F32))

    z_terms(log_ref, matrix_ref, z_ref)

    @pl.loop(0, width // 8)
    def _(j):
        at = pl.multiple_of(8 * j, 8)
        for l in range(layers):
            s2_ref[l, pl.ds(at, 8), :] = weighted(y_pairs(log_ref, l, at + PAD, 8))[1]
            s3_ref[l, pl.ds(at, 8), :] = z_ref[l, pl.ds(at, 8), pl.ds(depth, depth)]


def slope_x_kernel(part, log_ref, on_ref, off_ref, vel_ref, *refs):
    s1_ref, scale_ref = refs[-2:]
    layers, width, _ = s1_ref.shape
    even, valid = where_am_i()

    def body(rows, off_rows, wide, send_rows):
        own = [log_ref[l, wide, :] for l in range(layers)]
        on = [jnp.log(on_ref[l, rows, :].astype(F32)) for l in range(layers)]
        off = [jnp.log(jnp.where(valid, off_ref[l, off_rows, :].astype(F32), 1.0)) for l in range(layers)]
        low = [jnp.where(even, b, a) for a, b in zip(on, off)]
        high = [jnp.where(even, a, b) for a, b in zip(on, off)]
        values = low[layers - 4 :] + own + high[:4]
        for l in range(layers):
            s1_ref[l, rows, :] = weighted(x_pairs(values, l))[1]
            v = vel_ref[l, rows, :].astype(F32)
            scale_ref[l, rows, :] = SPEED * v * v

    part_rows(part, width, off_ref, body)


def yz_terms(f_ref, s2_ref, s3_ref, z_ref, l, at):
    f = f_ref[l, pl.ds(at + PAD, 8), :]
    lap_y, d_y = weighted(y_pairs(f_ref, l, at + PAD, 8))
    rows, depth = pl.ds(at, 8), f.shape[1]
    lap_z, d_z = z_ref[l, rows, pl.ds(0, depth)], z_ref[l, rows, pl.ds(depth, depth)]
    part = (3.0 * SECOND[0]) * f + lap_y + lap_z
    part = part - (s2_ref[l, rows, :] * d_y + s3_ref[l, rows, :] * d_z)
    return f, part, d_y, d_z


def forward_yz_kernel(f_ref, s2_ref, s3_ref, matrix_ref, part_ref, dy_ref, dz_ref, z_ref):
    layers, width, _ = part_ref.shape
    z_terms(f_ref, matrix_ref, z_ref)

    @pl.loop(0, width // 8)
    def _(j):
        at = pl.multiple_of(8 * j, 8)
        rows = pl.ds(at, 8)
        for l in range(layers):
            _, part, d_y, d_z = yz_terms(f_ref, s2_ref, s3_ref, z_ref, l, at)
            part_ref[l, rows, :] = part
            dy_ref[l, rows, :] = d_y
            dz_ref[l, rows, :] = d_z


def plain_yz_kernel(f_ref, matrix_ref, part_ref, dy_ref, dz_ref, z_ref):
    layers, width, depth = part_ref.shape
    z_terms(f_ref, matrix_ref, z_ref)

    @pl.loop(0, width // 8)
    def _(j):
        at = pl.multiple_of(8 * j, 8)
        rows = pl.ds(at, 8)
        for l in range(layers):
            lap_y, d_y = weighted(y_pairs(f_ref, l, at + PAD, 8))
            f = f_ref[l, pl.ds(at + PAD, 8), :]
            part_ref[l, rows, :] = (3.0 * SECOND[0]) * f + lap_y + z_ref[l, rows, pl.ds(0, depth)]
            dy_ref[l, rows, :] = d_y
            dz_ref[l, rows, :] = z_ref[l, rows, pl.ds(depth, depth)]


def forward_x_kernel(
    part, send, plain, f_ref, on_ref, off_ref, part_ref, s1_ref, scale_ref, before_ref, *refs
):
    if plain:
        s2_ref, s3_ref, dy_ref, dz_ref = refs[:4]
    sending = send
    if sending:
        dx_ref, applied_ref, next_ref, half_ref, send_ref = refs[-5:]
    else:
        dx_ref, applied_ref, next_ref = refs[-3:]
    layers, width, _ = part_ref.shape
    shift = before_ref.shape[1] != width
    if part == 0:
        zero_pads(next_ref)

    def body(rows, off_rows, wide, send_rows):
        own = [f_ref[l, wide, :] for l in range(layers)]
        values = x_values(own, on_ref, off_ref, rows, off_rows)
        for l in range(layers):
            lap, d_x = weighted(x_pairs(values, l))
            applied = part_ref[l, rows, :] + (lap - s1_ref[l, rows, :] * d_x)
            if plain:
                applied = applied - (
                    s2_ref[l, rows, :] * dy_ref[l, rows, :] + s3_ref[l, rows, :] * dz_ref[l, rows, :]
                )
            before = before_ref[l, wide if shift else rows, :]
            later = 2.0 * own[l] - before + scale_ref[l, rows, :] * applied
            dx_ref[l, rows, :] = d_x
            applied_ref[l, rows, :] = applied
            next_ref[l, wide, :] = later
            if sending:
                narrow = later.astype(BF16)
                half_ref[l, rows, :] = narrow
                send_ref[l, send_rows, :] = narrow

    part_rows(part, width, off_ref, body)


def adjoint_yz_kernel(
    first, f_ref, s2_ref, s3_ref, matrix_ref, fdy_ref, fdz_ref, fapplied_ref, *refs,
):
    if first:
        part_ref, vel_ref, den_ref, z_ref = refs
    else:
        vel_in, den_in, part_ref, vel_ref, den_ref, z_ref = refs
    layers, width, _ = part_ref.shape
    z_terms(f_ref, matrix_ref, z_ref)

    @pl.loop(0, width // 8)
    def _(j):
        at = pl.multiple_of(8 * j, 8)
        rows = pl.ds(at, 8)
        for l in range(layers):
            f, part, d_y, d_z = yz_terms(f_ref, s2_ref, s3_ref, z_ref, l, at)
            part_ref[l, rows, :] = part
            sum_vel = f * fapplied_ref[l, rows, :]
            sum_den = d_y * fdy_ref[l, rows, :] + d_z * fdz_ref[l, rows, :]
            if not first:
                sum_vel = vel_in[l, rows, :] + sum_vel
                sum_den = den_in[l, rows, :] + sum_den
            vel_ref[l, rows, :] = sum_vel
            den_ref[l, rows, :] = sum_den


def adjoint_x_kernel(
    part, last, f_ref, on_ref, off_ref, part_ref, s1_ref, scale_ref, before_ref,
    source_ref, fdx_ref, den_in, *refs,
):
    if last:
        vel_in, fapplied_ref, vmodel_ref = refs[:3]
        a_ref, half_ref, den_ref, send_ref, shot_ref = refs[-5:]
    else:
        a_ref, half_ref, den_ref, q_ref, send_ref = refs[-5:]
    layers, width, _ = part_ref.shape
    shift = before_ref.shape[1] != width
    if part == 0:
        zero_pads(a_ref)

    def body(rows, off_rows, wide, send_rows):
        own = [f_ref[l, wide, :] for l in range(layers)]
        values = x_values(own, on_ref, off_ref, rows, off_rows)
        for l in range(layers):
            lap, d_x = weighted(x_pairs(values, l))
            applied = part_ref[l, rows, :] + (lap - s1_ref[l, rows, :] * d_x)
            before = before_ref[l, wide if shift else rows, :]
            later = 2.0 * own[l] - before + scale_ref[l, rows, :] * applied
            if not last:
                q_ref[l, rows, :] = later
            adjoint = later + source_ref[l, wide, :]
            a_ref[l, wide, :] = adjoint
            narrow = adjoint.astype(BF16)
            half_ref[l, rows, :] = narrow
            send_ref[l, send_rows, :] = narrow
            den_ref[l, rows, :] = den_in[l, rows, :] + d_x * fdx_ref[l, rows, :]
            if last:
                total = vel_in[l, rows, :] + adjoint * fapplied_ref[l, rows, :]
                v = vmodel_ref[l, rows, :].astype(F32)
                shot_ref[l, send_rows, :] = ((2.0 * SPEED) * v * total).astype(BF16)

    part_rows(part, width, off_ref, body)


def last_yz_kernel(f_ref, matrix_ref, fdy_ref, fdz_ref, den_in, den_ref, z_ref):
    layers, width, depth = den_ref.shape
    z_terms(f_ref, matrix_ref, z_ref)

    @pl.loop(0, width // 8)
    def _(j):
        at = pl.multiple_of(8 * j, 8)
        rows = pl.ds(at, 8)
        for l in range(layers):
            d_y = weighted(y_pairs(f_ref, l, at + PAD, 8))[1]
            d_z = z_ref[l, rows, pl.ds(depth, depth)]
            den_ref[l, rows, :] = den_in[l, rows, :] + (
                d_y * fdy_ref[l, rows, :] + d_z * fdz_ref[l, rows, :]
            )


def last_x_kernel(part, f_ref, on_ref, off_ref, fdx_ref, den_in, scale_ref, dmodel_ref, shot_ref):
    layers, width, _ = den_in.shape

    def body(rows, off_rows, wide, send_rows):
        own = [f_ref[l, wide, :] for l in range(layers)]
        values = x_values(own, on_ref, off_ref, rows, off_rows)
        for l in range(layers):
            d_x = weighted(x_pairs(values, l))[1]
            total = den_in[l, rows, :] + d_x * fdx_ref[l, rows, :]
            density = dmodel_ref[l, rows, :].astype(F32)
            shot_ref[l, send_rows, :] = (scale_ref[l, rows, :] / density * total).astype(BF16)

    part_rows(part, width, off_ref, body)


def swap_over(axis, count, bit, value):
    return lax.ppermute(value, axis, [(i, i ^ bit) for i in range(count)])


def paired(half):
    count = lax.axis_size(SUB)
    return lax.ppermute(half, SUB, [(i, i ^ 1) for i in range(count)])


def across(half, ring=False):
    groups, count = lax.axis_size(SHOT), lax.axis_size(SUB)
    pairs = []
    for s in range(groups):
        for i in range(1, count - 1, 2):
            pairs += [(s * count + i, s * count + i + 1), (s * count + i + 1, s * count + i)]
        if ring:
            pairs += [(s * count, s * count + count - 1), (s * count + count - 1, s * count)]
        elif groups % 2 == 0:
            for i in (0, count - 1):
                pairs.append((s * count + i, (s ^ 1) * count + i))
    return lax.ppermute(half, (SHOT, SUB), pairs)


def bits_of(groups):
    return [1 << k for k in range(groups.bit_length() - 1)]


def routes_kernel(cover_ref, out_ref):
    column = lax.axis_index(SUB)
    for g in range(out_ref.shape[0]):
        out_ref[g, :, :] = jnp.full(out_ref.shape[1:], cover_ref[g, column], jnp.int32)


def masked_sum(out_ref, first, terms):
    layers, width, _ = terms[0][1].shape
    tiles = next(n for n in (4, 2, 1) if width % (16 * n) == 0)

    @pl.loop(0, width // (16 * tiles))
    def _(j):
        for n in range(tiles):
            rows = pl.ds(pl.multiple_of(16 * tiles * j + 16 * n, 16), 16)
            for l in range(layers):
                total = None
                for mask, ref in terms:
                    term = jnp.where(mask, ref[l, rows, :].astype(F32), 0.0)
                    total = term if total is None else total + term
                out_ref[first + l, rows, :] = total.astype(out_ref.dtype)


def pick_kernel(offsets, bits, route_ref, *refs):
    me = lax.axis_index(SHOT)
    outs = refs[-2:]
    count = len(refs) // 2 - 1
    for way in range(2):
        row = route_ref[me ^ bits[way]]
        held = refs[way * count : (way + 1) * count]
        masked_sum(outs[way], 0, [(row == (me ^ o), ref) for o, ref in zip(offsets[way], held)])


def gather_kernel(offsets, bits, parts, route_ref, *refs):
    me = lax.axis_index(SHOT)
    part_refs = refs[len(refs) - parts :]
    refs = refs[: len(refs) - parts]
    out_ref = refs[-1]
    count = (len(refs) - 1) // 2
    mine = route_ref[me]
    layers = out_ref.shape[0] // 2
    for way in range(2):
        *near, far = refs[way * count : (way + 1) * count]
        terms = [(mine == (me ^ o), ref) for o, ref in zip(offsets[way], near)]
        terms.append(((mine & bits[way]) != (me & bits[way]), far))
        masked_sum(out_ref, way * layers, terms)
    for n, part_ref in enumerate(part_refs):
        size = part_ref.shape[1]
        part_ref[...] = out_ref[:, n * size : (n + 1) * size, :]


def fetch(tile, route, parts=0, tie=lambda x: x):
    groups = route.shape[0]
    layers = tile.shape[0] // 2
    small = (layers, *tile.shape[1:])
    ways = [bits_of(groups), bits_of(groups)[::-1]]
    held = [[tile[:layers]], [tile[layers:]]]
    offsets = [[0], [0]]
    for stage in range(len(ways[0]) - 1):
        for way in range(2):
            bit = ways[way][stage]
            block = jnp.concatenate(held[way], axis=0) if len(held[way]) > 1 else held[way][0]
            got = swap_over(SHOT, groups, bit, block)
            held[way] = held[way] + [
                lax.slice_in_dim(got, n * layers, (n + 1) * layers, axis=0)
                for n in range(len(held[way]))
            ]
            offsets[way] = offsets[way] + [o ^ bit for o in offsets[way]]
    last = [way[-1] for way in ways]
    held = tie(held)
    sends = call(
        lambda *refs: pick_kernel(offsets, last, *refs),
        [(small, BF16)] * 2, [route, *held[0], *held[1]],
    )
    far = [swap_over(SHOT, groups, last[way], sends[way]) for way in range(2)]
    part_shape = (tile.shape[0], tile.shape[1] // PARTS, tile.shape[2])
    return call(
        lambda *refs: gather_kernel(offsets, last, parts, *refs),
        [(tile.shape, BF16)] + [(part_shape, BF16)] * parts, [route, *held[0], far[0], *held[1], far[1]],
    )


def bucket_kernel(offsets, bit, route_ref, own_ref, got_ref, *outs):
    me = lax.axis_index(SHOT)
    mine, theirs = route_ref[me], route_ref[me ^ bit]
    for offset, out in zip(offsets, outs):
        row = me ^ offset
        masked_sum(out, 0, [(mine == row, own_ref), (theirs == row, got_ref)])


def give_back(part, way, route):
    groups = route.shape[0]
    layers = part.shape[0]
    bits = bits_of(groups)[:: 1 if way == 0 else -1]
    got = swap_over(SHOT, groups, bits[0], part)
    offsets = [0]
    for b in reversed(bits[1:]):
        offsets = offsets + [o ^ b for o in offsets]
    types = [BF16 if o & bits[1] else F32 for o in offsets]
    sums = call(
        lambda *refs: bucket_kernel(offsets, bits[0], *refs),
        [(part.shape, kind) for kind in types], [route, part, got],
    )
    left = dict(zip(offsets, sums))
    for b in bits[1:]:
        away = [o for o in left if o & b]
        block = jnp.concatenate([left[o].astype(BF16) for o in away], axis=0)
        came = swap_over(SHOT, groups, b, block)
        left = {
            o ^ b: left[o ^ b] + came[n * layers : (n + 1) * layers].astype(F32)
            for n, o in enumerate(away)
        }
    return left[0]


def inner(vel_model, den_model, cover, receivers, observed, p_now, p_before, q_now, q_before):
    layers, width, depth = p_now.shape[1:]
    tall = width + 2 * PAD
    narrow, padded = ((layers, width, depth), F32), ((layers, tall, depth), F32)
    half, flat = ((layers, width, depth), BF16), ((layers * tall, depth), F32)
    z_scratch = [pltpu.VMEM((layers, width, 2 * depth), F32)]
    matrix = z_matrix(depth)
    seen = observed[0]

    size = width // PARTS
    part_half = ((layers, size, depth), BF16)
    parts = range(PARTS)

    groups = cover.shape[0]
    (route,) = call(routes_kernel, [((groups, 16, depth), jnp.int32)], [cover], [SM])

    p, p_half = call(prepare_kernel, [padded, half], [p_now[0]])
    n_rec = receivers.shape[1]
    (lists,) = call(
        lambda rec, out: list_kernel(rec, layers, width, depth, out),
        [((4, n_rec), jnp.int32)], [receivers],
    )
    on, off = paired(p_half), across(p_half, ring=True)
    kept = {}

    def tie(held):
        held, kept["p"] = lax.optimization_barrier((held, p))
        return held

    den, *den_parts = fetch(den_model[0], route, PARTS, tie)
    (vel,) = fetch(vel_model[0], route)
    p, offs = kept["p"], [off] * PARTS

    before = p_before[0]
    log_den, s2, s3 = call(log_kernel, [padded, narrow, narrow], [den, matrix, before], scratch=z_scratch)
    on_den = paired(den)
    off_den = [across(den_part) for den_part in den_parts]
    slopes = [()]
    for k in parts:
        ins = [log_den, on_den, off_den[k], vel]
        slopes.append(
            call(
                lambda *refs, k=k: slope_x_kernel(k, *refs),
                [narrow, narrow], [*ins, *slopes[-1]],
                aliases={len(ins) + n: n for n in range(len(slopes[-1]))},
            )
        )

    stored, fields = [], []
    for step in range(ITERS):
        plain = step == 0
        part, d_y, d_z = call(
            plain_yz_kernel if plain else forward_yz_kernel, [narrow] * 3,
            [p, matrix] if plain else [p, s2, s3, matrix], scratch=z_scratch,
        )
        if step > 0:
            fields.append(p.reshape(flat[0]))
        sending = step < ITERS - 1
        made, sends = (), []
        for k in parts:
            s1, scale = slopes[1 + k] if step == 0 else slopes[-1]
            ins = [p, on, offs[k], part, s1, scale, before] + ([s2, s3, d_y, d_z] if plain else [])
            outs = call(
                lambda *refs, k=k, sending=sending, plain=plain: forward_x_kernel(k, sending, plain, *refs),
                [narrow, narrow, padded] + ([half, part_half] if sending else []), [*ins, *made],
                aliases={len(ins) + n: n for n in range(len(made))},
            )
            made = outs[: 4 if sending else 3]
            if sending:
                sends.append(across(outs[4]))
        d_x, applied, later = made[:3]
        if sending:
            on, offs = paired(made[3]), sends
        stored.append((applied, d_x, d_y, d_z))
        before, p = p, later

    (q,) = call(prepare_kernel, [padded], [q_now[0]])
    a, a_half, *sends = call(
        lambda *refs: first_adjoint_kernel(ITERS - 1, *refs),
        [flat, half] + [part_half] * PARTS, [p.reshape(flat[0]), q.reshape(flat[0]), lists, seen],
        [VM, VM, SM, SM],
    )
    offs = [across(send) for send in sends]
    on = paired(a_half)
    a = a.reshape(padded[0])
    sources = []
    for first, some in ((0, fields[:1]), (1, fields[1:])):
        sources += call(
            lambda *refs, first=first: receivers_kernel(first, *refs),
            [flat] * len(some), [*some, lists, seen], [VM] * len(some) + [SM, SM],
        )
    sources = [source.reshape(padded[0]) for source in sources]
    before, current = q_before[0], q
    sums = ()
    for step in range(ITERS - 1):
        f_applied, f_dx, f_dy, f_dz = stored[ITERS - 1 - step]
        last = step == ITERS - 2
        part, sum_vel, sum_den = call(
            lambda *refs, first=step == 0: adjoint_yz_kernel(first, *refs),
            [narrow] * 3, [a, s2, s3, matrix, f_dy, f_dz, f_applied, *sums], scratch=z_scratch,
        )
        extra = [sum_vel, stored[0][0], vel] if last else []
        made, sends, shot_vel = (), [], []
        for k in parts:
            ins = [
                a, on, offs[k], part, s1, scale, before, sources[ITERS - 2 - step], f_dx, sum_den, *extra,
            ]
            kinds = [padded, half, narrow] + ([] if last else [narrow])
            outs = call(
                lambda *refs, k=k, last=last: adjoint_x_kernel(k, last, *refs),
                kinds + [part_half] * (2 if last else 1), [*ins, *made],
                aliases={len(ins) + n: n for n in range(len(made))},
            )
            made = outs[: len(kinds)]
            sends.append(across(outs[len(kinds)]))
            shot_vel += outs[len(kinds) + 1 :]
        a, a_half, sum_den, *later = made
        on, offs = paired(a_half), sends
        if not last:
            before, current = current, later[0]
        sums = (sum_vel, sum_den)
    _, f_dx, f_dy, f_dz = stored[0]
    grad_vel = [give_back(shot_vel[k], k, route) for k in parts]
    (sum_den,) = call(last_yz_kernel, [narrow], [a, matrix, f_dy, f_dz, sum_den], scratch=z_scratch)
    grad_den = []
    for k in parts:
        (shot_den,) = call(
            lambda *refs, k=k: last_x_kernel(k, *refs),
            [part_half], [a, on, offs[k], f_dx, sum_den, scale, den],
        )
        grad_den.append(give_back(shot_den, k, route))
    return jnp.concatenate(grad_vel, axis=1)[None], jnp.concatenate(grad_den, axis=1)[None]


def solution(mesh):
    spec = P(SHOT, SUB, None, None)
    return jax.shard_map(
        inner,
        mesh=mesh,
        in_specs=(spec, spec, P(), P(SHOT, None), P(SHOT, None, None), spec, spec, spec, spec),
        out_specs=(spec, spec),
        check_vma=False,
    )
```

```python
import math

import jax
import jax.numpy as jnp
import numpy as np
from jax import lax
from jax.experimental import pallas as pl
from jax.experimental.pallas import tpu as pltpu
from jax.sharding import PartitionSpec as P


ITERS = 4
SECOND = (-205.0 / 72.0, 8.0 / 5.0, -1.0 / 5.0, 8.0 / 315.0, -1.0 / 560.0)
FIRST = (4.0 / 5.0, -1.0 / 5.0, 4.0 / 105.0, -1.0 / 280.0)
SPEED = 0.15
SHOT, SUB = "shot", "sub"
PAD = 8
PARTS = 2
UNROLL = 8
F32, BF16 = jnp.float32, jnp.bfloat16
VMEM_LIMIT = 4 << 20

VM = pl.BlockSpec(memory_space=pltpu.VMEM)
SM = pl.BlockSpec(memory_space=pltpu.SMEM)


def call(kernel, outs, ins, specs=None, out_specs=None, scratch=(), flops=0, aliases=None):
    outs = tuple(jax.ShapeDtypeStruct(shape, dtype) for shape, dtype in outs)
    moved_bytes = sum(math.prod(x.shape) * x.dtype.itemsize for x in (*ins, *outs))
    return pl.pallas_call(
        kernel,
        out_shape=outs,
        in_specs=list(specs or [VM] * len(ins)),
        out_specs=tuple(out_specs or [VM] * len(outs)),
        scratch_shapes=list(scratch),
        input_output_aliases=aliases or {},
        cost_estimate=pl.CostEstimate(flops=flops, bytes_accessed=moved_bytes, transcendentals=0),
        compiler_params=pltpu.CompilerParams(vmem_limit_bytes=VMEM_LIMIT),
    )(*ins)


def weighted(pairs):
    lap, first = None, None
    for m, (ahead, behind) in enumerate(pairs, 1):
        s = SECOND[m] * (ahead + behind)
        t = FIRST[m - 1] * (ahead - behind)
        lap = s if lap is None else lap + s
        first = t if first is None else first + t
    return lap, first


def y_pairs(ref, layer, row, rows):
    return [
        (ref[layer, pl.ds(row + m, rows), :], ref[layer, pl.ds(row - m, rows), :])
        for m in range(1, 5)
    ]


def z_matrix(depth):
    both = np.zeros((depth, 2 * depth), np.float64)
    for out in range(depth):
        for m in range(1, 5):
            for source, sign in ((out + m, 1.0), (out - m, -1.0)):
                if 0 <= source < depth:
                    both[source, out] += SECOND[m]
                    both[source, depth + out] += sign * FIRST[m - 1]
    high = both.astype(np.float32).astype(jnp.bfloat16)
    low = (both - high.astype(np.float64)).astype(np.float32).astype(jnp.bfloat16)
    return jnp.asarray(np.concatenate([high, high, low], axis=0))


def z_terms(f_ref, matrix_ref, z_ref):
    layers, width, _ = z_ref.shape
    for l in range(layers):
        f = f_ref[l, pl.ds(PAD, width), :]
        high = f.astype(BF16)
        low = (f - high.astype(F32)).astype(BF16)
        split = jnp.concatenate([high, low, high], axis=1)
        z_ref[l, :, :] = jnp.dot(split, matrix_ref[...], preferred_element_type=F32)


def where_am_i():
    column, columns = lax.axis_index(SUB), lax.axis_size(SUB)
    even = (column & 1) == 0
    valid = jnp.logical_and(column > 0, column < columns - 1)
    return even, valid


def x_values(own, on_ref, off_ref, rows, off_rows):
    even, valid = where_am_i()
    count = len(own)
    on = [on_ref[l, rows, :].astype(F32) for l in range(count)]
    off = [jnp.where(valid, off_ref[l, off_rows, :].astype(F32), 0.0) for l in range(count)]
    low = [jnp.where(even, b, a) for a, b in zip(on, off)]
    high = [jnp.where(even, a, b) for a, b in zip(on, off)]
    return low[count - 4 :] + own + high[:4]


def part_rows(part, width, off_ref, body):
    size = width // PARTS
    first = part * size
    back = first if off_ref.shape[1] == size else 0

    @pl.loop(0, size // 16)
    def _(j):
        at = pl.multiple_of(first + 16 * j, 16)
        off_at = pl.multiple_of(first - back + 16 * j, 16)
        body(pl.ds(at, 16), pl.ds(off_at, 16), pl.ds(at + PAD, 16), pl.ds(pl.multiple_of(16 * j, 16), 16))


def x_pairs(values, layer):
    return [(values[4 + layer + m], values[4 + layer - m]) for m in range(1, 5)]


def zero_pads(ref):
    layers, tall, depth = ref.shape
    zeros = jnp.zeros((PAD, depth), F32)
    for l in range(layers):
        ref[l, pl.ds(0, PAD), :] = zeros
        ref[l, pl.ds(tall - PAD, PAD), :] = zeros


def prepare_kernel(p_ref, pw_ref, *half_refs):
    layers, width, _ = p_ref.shape
    zero_pads(pw_ref)

    @pl.loop(0, width // 16)
    def _(j):
        at = pl.multiple_of(16 * j, 16)
        for l in range(layers):
            v = p_ref[l, pl.ds(at, 16), :]
            pw_ref[l, pl.ds(at + PAD, 16), :] = v
            for half_ref in half_refs:
                half_ref[l, pl.ds(at, 16), :] = v.astype(BF16)


def list_kernel(rec_ref, layers, width, depth, *list_refs):
    total = rec_ref.shape[1]
    cells, size = layers * width * depth, width // PARTS
    local = rec_ref[...] - lax.axis_index(SUB) * cells
    inside = jnp.logical_and(local >= 0, local < cells)
    line = lax.shift_right_arithmetic(local, depth.bit_length() - 1)
    layer = jnp.zeros_like(line)
    for l in range(1, layers):
        layer += jnp.where(line >= l * width, 1, 0)
    y = line - layer * width
    row = line + PAD + layer * (2 * PAD)
    number = lax.broadcasted_iota(jnp.int32, (1, total), 1)
    down = lax.broadcasted_iota(jnp.int32, (total, total), 0)
    across_ = lax.broadcasted_iota(jnp.int32, (total, total), 1)
    earlier = jnp.where(down < across_, 1.0, 0.0).astype(BF16)
    kind = lax.broadcasted_iota(jnp.int32, (8, total), 0)
    for k, list_ref in enumerate(list_refs):
        mine = jnp.logical_and(inside, jnp.logical_and(y >= k * size, y < (k + 1) * size))
        counted = jnp.broadcast_to(jnp.where(mine, 1.0, 0.0), (8, total))
        place = jnp.dot(counted.astype(BF16), earlier, preferred_element_type=F32)[:1]
        place = jnp.where(mine, place.astype(jnp.int32), -1)
        spots = jnp.where(down == place, 1.0, 0.0).astype(BF16)
        near = layer * size + y - k * size
        pieces = [local & (depth - 1)]
        for value in (row, number, near):
            pieces += [value & 255, (value >> 8) & 255]
        values = jnp.zeros((8, total), jnp.int32)
        for n, piece in enumerate(pieces):
            values = jnp.where(kind == n, piece, values)
        listed = lax.dot_general(
            values.astype(F32).astype(BF16), spots, (((1,), (1,)), ((), ())), preferred_element_type=F32
        ).astype(jnp.int32)
        count = jnp.sum(counted[:1], axis=1, keepdims=True).astype(jnp.int32)
        list_ref[0:1, :] = listed[1:2] + 256 * listed[2:3]
        list_ref[1:2, :] = listed[3:4] + 256 * listed[4:5] + 65536 * count
        list_ref[2:3, :] = listed[5:6] + 256 * listed[6:7]
        list_ref[3:4, :] = jnp.where(number < count, listed[0:1], depth)


def add_receivers(jobs, list_ref, observed_ref, near=False):
    depth = jobs[0][1].shape[1]
    lane = lax.broadcasted_iota(jnp.int32, (1, depth), 1)
    count = lax.shift_right_logical(list_ref[1, 0], 16)

    @pl.loop(0, (count + UNROLL - 1) // UNROLL)
    def _(c):
        rows, terms = [], []
        for k in range(UNROLL):
            row = list_ref[0, c * UNROLL + k]
            seen_row = list_ref[2, c * UNROLL + k] if near else row
            number = list_ref[1, c * UNROLL + k] & 65535
            here = lane == list_ref[3, c * UNROLL + k]
            rows.append(row)
            terms.append(
                [
                    jnp.where(here, field_ref[pl.ds(seen_row, 1), :] - observed_ref[n, number], 0.0)
                    for n, field_ref, _ in jobs
                ]
            )
        for row, parts in zip(rows, terms):
            for (_, _, into_ref), term in zip(jobs, parts):
                into_ref[pl.ds(row, 1), :] += term


def receivers_kernel(fields, observed_ref, *refs):
    lists, refs = refs[:PARTS], refs[PARTS:]
    jobs = list(zip(range(fields), refs[:fields], refs[fields:]))
    for _, _, source_ref in jobs:
        source_ref[...] = jnp.zeros(source_ref.shape, F32)
    for list_ref in lists:
        add_receivers(jobs, list_ref, observed_ref)


def first_adjoint_kernel(n, part, p_ref, q_ref, list_ref, observed_ref, *refs):
    a_ref, half_ref, send_ref = refs[-3:]
    layers, width, _ = half_ref.shape
    size, tall = width // PARTS, width + 2 * PAD
    for l in range(layers):
        first = l * tall + (PAD + part * size if part else 0)
        last = l * tall + (PAD + (part + 1) * size if part < PARTS - 1 else tall)
        a_ref[first:last, :] = q_ref[first:last, :]
    add_receivers([(n, p_ref, a_ref)], list_ref, observed_ref, near=True)

    @pl.loop(0, size // 16)
    def _(j):
        at = pl.multiple_of(16 * j, 16)
        for l in range(layers):
            from_row = pl.multiple_of(at + part * size + l * tall + PAD, 8)
            value = a_ref[pl.ds(from_row, 16), :].astype(BF16)
            half_ref[l, pl.ds(pl.multiple_of(at + part * size, 16), 16), :] = value
            send_ref[l, pl.ds(at, 16), :] = value


def log_kernel(den_ref, matrix_ref, before_ref, log_ref, s2_ref, s3_ref, z_ref):
    layers, width, depth = den_ref.shape
    zero_pads(log_ref)

    @pl.loop(0, width // 16)
    def _(j):
        at = pl.multiple_of(16 * j, 16)
        for l in range(layers):
            log_ref[l, pl.ds(at + PAD, 16), :] = jnp.log(den_ref[l, pl.ds(at, 16), :].astype(F32))

    z_terms(log_ref, matrix_ref, z_ref)

    @pl.loop(0, width // 8)
    def _(j):
        at = pl.multiple_of(8 * j, 8)
        for l in range(layers):
            s2_ref[l, pl.ds(at, 8), :] = weighted(y_pairs(log_ref, l, at + PAD, 8))[1]
            s3_ref[l, pl.ds(at, 8), :] = z_ref[l, pl.ds(at, 8), pl.ds(depth, depth)]


def slope_x_kernel(part, log_ref, on_ref, off_ref, vel_ref, *refs):
    s1_ref, scale_ref = refs[-2:]
    layers, width, _ = s1_ref.shape
    even, valid = where_am_i()

    def body(rows, off_rows, wide, send_rows):
        own = [log_ref[l, wide, :] for l in range(layers)]
        on = [jnp.log(on_ref[l, rows, :].astype(F32)) for l in range(layers)]
        off = [jnp.log(jnp.where(valid, off_ref[l, off_rows, :].astype(F32), 1.0)) for l in range(layers)]
        low = [jnp.where(even, b, a) for a, b in zip(on, off)]
        high = [jnp.where(even, a, b) for a, b in zip(on, off)]
        values = low[layers - 4 :] + own + high[:4]
        for l in range(layers):
            s1_ref[l, rows, :] = weighted(x_pairs(values, l))[1]
            v = vel_ref[l, rows, :].astype(F32)
            scale_ref[l, rows, :] = SPEED * v * v

    part_rows(part, width, off_ref, body)


def yz_terms(f_ref, s2_ref, s3_ref, z_ref, l, at):
    f = f_ref[l, pl.ds(at + PAD, 8), :]
    lap_y, d_y = weighted(y_pairs(f_ref, l, at + PAD, 8))
    rows, depth = pl.ds(at, 8), f.shape[1]
    lap_z, d_z = z_ref[l, rows, pl.ds(0, depth)], z_ref[l, rows, pl.ds(depth, depth)]
    part = (3.0 * SECOND[0]) * f + lap_y + lap_z
    part = part - (s2_ref[l, rows, :] * d_y + s3_ref[l, rows, :] * d_z)
    return f, part, d_y, d_z


def forward_yz_kernel(f_ref, s2_ref, s3_ref, matrix_ref, part_ref, dy_ref, dz_ref, z_ref):
    layers, width, _ = part_ref.shape
    z_terms(f_ref, matrix_ref, z_ref)

    @pl.loop(0, width // 8)
    def _(j):
        at = pl.multiple_of(8 * j, 8)
        rows = pl.ds(at, 8)
        for l in range(layers):
            _, part, d_y, d_z = yz_terms(f_ref, s2_ref, s3_ref, z_ref, l, at)
            part_ref[l, rows, :] = part
            dy_ref[l, rows, :] = d_y
            dz_ref[l, rows, :] = d_z


def plain_yz_kernel(f_ref, matrix_ref, part_ref, dy_ref, dz_ref, z_ref):
    layers, width, depth = part_ref.shape
    z_terms(f_ref, matrix_ref, z_ref)

    @pl.loop(0, width // 8)
    def _(j):
        at = pl.multiple_of(8 * j, 8)
        rows = pl.ds(at, 8)
        for l in range(layers):
            lap_y, d_y = weighted(y_pairs(f_ref, l, at + PAD, 8))
            f = f_ref[l, pl.ds(at + PAD, 8), :]
            part_ref[l, rows, :] = (3.0 * SECOND[0]) * f + lap_y + z_ref[l, rows, pl.ds(0, depth)]
            dy_ref[l, rows, :] = d_y
            dz_ref[l, rows, :] = z_ref[l, rows, pl.ds(depth, depth)]


def forward_x_kernel(
    part, send, plain, f_ref, on_ref, off_ref, part_ref, s1_ref, scale_ref, before_ref, *refs
):
    if plain:
        s2_ref, s3_ref, dy_ref, dz_ref = refs[:4]
    sending = send
    if sending:
        dx_ref, applied_ref, next_ref, half_ref, send_ref = refs[-5:]
    else:
        dx_ref, applied_ref, next_ref = refs[-3:]
    layers, width, _ = part_ref.shape
    shift = before_ref.shape[1] != width
    if part == 0 and sending:
        zero_pads(next_ref)

    def body(rows, off_rows, wide, send_rows):
        own = [f_ref[l, wide, :] for l in range(layers)]
        values = x_values(own, on_ref, off_ref, rows, off_rows)
        for l in range(layers):
            lap, d_x = weighted(x_pairs(values, l))
            applied = part_ref[l, rows, :] + (lap - s1_ref[l, rows, :] * d_x)
            if plain:
                applied = applied - (
                    s2_ref[l, rows, :] * dy_ref[l, rows, :] + s3_ref[l, rows, :] * dz_ref[l, rows, :]
                )
            before = before_ref[l, wide if shift else rows, :]
            later = 2.0 * own[l] - before + scale_ref[l, rows, :] * applied
            dx_ref[l, rows, :] = d_x
            applied_ref[l, rows, :] = applied
            next_ref[l, wide if sending else send_rows, :] = later
            if sending:
                narrow = later.astype(BF16)
                half_ref[l, rows, :] = narrow
                send_ref[l, send_rows, :] = narrow

    part_rows(part, width, off_ref, body)


def adjoint_yz_kernel(
    first, f_ref, s2_ref, s3_ref, matrix_ref, fdy_ref, fdz_ref, fapplied_ref, *refs,
):
    if first:
        part_ref, vel_ref, den_ref, z_ref = refs
    else:
        vel_in, den_in, part_ref, vel_ref, den_ref, z_ref = refs
    layers, width, _ = part_ref.shape
    z_terms(f_ref, matrix_ref, z_ref)

    @pl.loop(0, width // 8)
    def _(j):
        at = pl.multiple_of(8 * j, 8)
        rows = pl.ds(at, 8)
        for l in range(layers):
            f, part, d_y, d_z = yz_terms(f_ref, s2_ref, s3_ref, z_ref, l, at)
            part_ref[l, rows, :] = part
            sum_vel = f * fapplied_ref[l, rows, :]
            sum_den = d_y * fdy_ref[l, rows, :] + d_z * fdz_ref[l, rows, :]
            if not first:
                sum_vel = vel_in[l, rows, :] + sum_vel
                sum_den = den_in[l, rows, :] + sum_den
            vel_ref[l, rows, :] = sum_vel
            den_ref[l, rows, :] = sum_den


def adjoint_x_kernel(
    part, last, f_ref, on_ref, off_ref, part_ref, s1_ref, scale_ref, before_ref,
    source_ref, fdx_ref, den_in, *refs,
):
    if last:
        vel_in, fapplied_ref, vmodel_ref = refs[:3]
        a_ref, half_ref, den_ref, send_ref, shot_ref = refs[-5:]
    else:
        a_ref, half_ref, den_ref, q_ref, send_ref = refs[-5:]
    layers, width, _ = part_ref.shape
    shift = before_ref.shape[1] != width
    if part == 0:
        zero_pads(a_ref)

    def body(rows, off_rows, wide, send_rows):
        own = [f_ref[l, wide, :] for l in range(layers)]
        values = x_values(own, on_ref, off_ref, rows, off_rows)
        for l in range(layers):
            lap, d_x = weighted(x_pairs(values, l))
            applied = part_ref[l, rows, :] + (lap - s1_ref[l, rows, :] * d_x)
            before = before_ref[l, wide if shift else rows, :]
            later = 2.0 * own[l] - before + scale_ref[l, rows, :] * applied
            if not last:
                q_ref[l, rows, :] = later
            adjoint = later + source_ref[l, wide, :]
            a_ref[l, wide, :] = adjoint
            narrow = adjoint.astype(BF16)
            half_ref[l, rows, :] = narrow
            send_ref[l, send_rows, :] = narrow
            den_ref[l, rows, :] = den_in[l, rows, :] + d_x * fdx_ref[l, rows, :]
            if last:
                total = vel_in[l, rows, :] + adjoint * fapplied_ref[l, rows, :]
                v = vmodel_ref[l, rows, :].astype(F32)
                shot_ref[l, send_rows, :] = ((2.0 * SPEED) * v * total).astype(BF16)

    part_rows(part, width, off_ref, body)


def last_yz_kernel(f_ref, matrix_ref, fdy_ref, fdz_ref, den_in, den_ref, z_ref):
    layers, width, depth = den_ref.shape
    z_terms(f_ref, matrix_ref, z_ref)

    @pl.loop(0, width // 8)
    def _(j):
        at = pl.multiple_of(8 * j, 8)
        rows = pl.ds(at, 8)
        for l in range(layers):
            d_y = weighted(y_pairs(f_ref, l, at + PAD, 8))[1]
            d_z = z_ref[l, rows, pl.ds(depth, depth)]
            den_ref[l, rows, :] = den_in[l, rows, :] + (
                d_y * fdy_ref[l, rows, :] + d_z * fdz_ref[l, rows, :]
            )


def last_x_kernel(part, f_ref, on_ref, off_ref, fdx_ref, den_in, scale_ref, dmodel_ref, shot_ref):
    layers, width, _ = den_in.shape

    def body(rows, off_rows, wide, send_rows):
        own = [f_ref[l, wide, :] for l in range(layers)]
        values = x_values(own, on_ref, off_ref, rows, off_rows)
        for l in range(layers):
            d_x = weighted(x_pairs(values, l))[1]
            total = den_in[l, rows, :] + d_x * fdx_ref[l, rows, :]
            density = dmodel_ref[l, rows, :].astype(F32)
            shot_ref[l, send_rows, :] = (scale_ref[l, rows, :] / density * total).astype(BF16)

    part_rows(part, width, off_ref, body)


def swap_over(axis, count, bit, value):
    return lax.ppermute(value, axis, [(i, i ^ bit) for i in range(count)])


def paired(half):
    count = lax.axis_size(SUB)
    return lax.ppermute(half, SUB, [(i, i ^ 1) for i in range(count)])


def across(half, ring=False):
    groups, count = lax.axis_size(SHOT), lax.axis_size(SUB)
    pairs = []
    for s in range(groups):
        for i in range(1, count - 1, 2):
            pairs += [(s * count + i, s * count + i + 1), (s * count + i + 1, s * count + i)]
        if ring:
            pairs += [(s * count, s * count + count - 1), (s * count + count - 1, s * count)]
        elif groups % 2 == 0:
            for i in (0, count - 1):
                pairs.append((s * count + i, (s ^ 1) * count + i))
    return lax.ppermute(half, (SHOT, SUB), pairs)


def bits_of(groups):
    return [1 << k for k in range(groups.bit_length() - 1)]


def routes_kernel(cover_ref, out_ref):
    column = lax.axis_index(SUB)
    for g in range(out_ref.shape[0]):
        out_ref[g, :, :] = jnp.full(out_ref.shape[1:], cover_ref[g, column], jnp.int32)


def masked_sum(out_ref, first, terms):
    layers, width, _ = terms[0][1].shape
    tiles = next(n for n in (4, 2, 1) if width % (16 * n) == 0)

    @pl.loop(0, width // (16 * tiles))
    def _(j):
        for n in range(tiles):
            rows = pl.ds(pl.multiple_of(16 * tiles * j + 16 * n, 16), 16)
            for l in range(layers):
                total = None
                for mask, ref in terms:
                    term = jnp.where(mask, ref[l, rows, :].astype(F32), 0.0)
                    total = term if total is None else total + term
                out_ref[first + l, rows, :] = total.astype(out_ref.dtype)


def pick_kernel(offsets, bits, route_ref, *refs):
    me = lax.axis_index(SHOT)
    outs = refs[-2:]
    count = len(refs) // 2 - 1
    for way in range(2):
        row = route_ref[me ^ bits[way]]
        held = refs[way * count : (way + 1) * count]
        masked_sum(outs[way], 0, [(row == (me ^ o), ref) for o, ref in zip(offsets[way], held)])


def gather_kernel(offsets, bits, parts, route_ref, *refs):
    me = lax.axis_index(SHOT)
    part_refs = refs[len(refs) - parts :]
    refs = refs[: len(refs) - parts]
    out_ref = refs[-1]
    count = (len(refs) - 1) // 2
    mine = route_ref[me]
    layers = out_ref.shape[0] // 2
    for way in range(2):
        *near, far = refs[way * count : (way + 1) * count]
        terms = [(mine == (me ^ o), ref) for o, ref in zip(offsets[way], near)]
        terms.append(((mine & bits[way]) != (me & bits[way]), far))
        masked_sum(out_ref, way * layers, terms)
    for n, part_ref in enumerate(part_refs):
        size = part_ref.shape[1]
        part_ref[...] = out_ref[:, n * size : (n + 1) * size, :]


def fetch(tile, route, parts=0, tie=lambda x: x):
    groups = route.shape[0]
    layers = tile.shape[0] // 2
    small = (layers, *tile.shape[1:])
    ways = [bits_of(groups), bits_of(groups)[::-1]]
    held = [[tile[:layers]], [tile[layers:]]]
    offsets = [[0], [0]]
    for stage in range(len(ways[0]) - 1):
        for way in range(2):
            bit = ways[way][stage]
            block = jnp.concatenate(held[way], axis=0) if len(held[way]) > 1 else held[way][0]
            got = swap_over(SHOT, groups, bit, block)
            held[way] = held[way] + [
                lax.slice_in_dim(got, n * layers, (n + 1) * layers, axis=0)
                for n in range(len(held[way]))
            ]
            offsets[way] = offsets[way] + [o ^ bit for o in offsets[way]]
    last = [way[-1] for way in ways]
    held = tie(held)
    sends = call(
        lambda *refs: pick_kernel(offsets, last, *refs),
        [(small, BF16)] * 2, [route, *held[0], *held[1]],
    )
    far = [swap_over(SHOT, groups, last[way], sends[way]) for way in range(2)]
    part_shape = (tile.shape[0], tile.shape[1] // PARTS, tile.shape[2])
    return call(
        lambda *refs: gather_kernel(offsets, last, parts, *refs),
        [(tile.shape, BF16)] + [(part_shape, BF16)] * parts, [route, *held[0], far[0], *held[1], far[1]],
    )


def bucket_kernel(offsets, bit, route_ref, own_ref, got_ref, *outs):
    me = lax.axis_index(SHOT)
    mine, theirs = route_ref[me], route_ref[me ^ bit]
    for offset, out in zip(offsets, outs):
        row = me ^ offset
        masked_sum(out, 0, [(mine == row, own_ref), (theirs == row, got_ref)])


def give_back(part, way, route):
    groups = route.shape[0]
    layers = part.shape[0]
    bits = bits_of(groups)[:: 1 if way == 0 else -1]
    got = swap_over(SHOT, groups, bits[0], part)
    offsets = [0]
    for b in reversed(bits[1:]):
        offsets = offsets + [o ^ b for o in offsets]
    types = [BF16 if o & bits[1] else F32 for o in offsets]
    sums = call(
        lambda *refs: bucket_kernel(offsets, bits[0], *refs),
        [(part.shape, kind) for kind in types], [route, part, got],
    )
    left = dict(zip(offsets, sums))
    for b in bits[1:]:
        away = [o for o in left if o & b]
        block = jnp.concatenate([left[o].astype(BF16) for o in away], axis=0)
        came = swap_over(SHOT, groups, b, block)
        left = {
            o ^ b: left[o ^ b] + came[n * layers : (n + 1) * layers].astype(F32)
            for n, o in enumerate(away)
        }
    return left[0]


def inner(vel_model, den_model, cover, receivers, observed, p_now, p_before, q_now, q_before):
    layers, width, depth = p_now.shape[1:]
    tall = width + 2 * PAD
    narrow, padded = ((layers, width, depth), F32), ((layers, tall, depth), F32)
    half, flat = ((layers, width, depth), BF16), ((layers * tall, depth), F32)
    z_scratch = [pltpu.VMEM((layers, width, 2 * depth), F32)]
    matrix = z_matrix(depth)
    seen = observed[0]

    size = width // PARTS
    part_half, part_full = ((layers, size, depth), BF16), ((layers, size, depth), F32)
    parts = range(PARTS)

    groups = cover.shape[0]
    (route,) = call(routes_kernel, [((groups, 16, depth), jnp.int32)], [cover], [SM])

    p, p_half = call(prepare_kernel, [padded, half], [p_now[0]])
    n_rec = receivers.shape[1]
    lists = call(
        lambda rec, seen_ref, *outs: list_kernel(rec, layers, width, depth, *outs),
        [((4, n_rec), jnp.int32)] * PARTS, [receivers, seen],
    )
    on, off = paired(p_half), across(p_half, ring=True)
    kept = {}

    def tie(held):
        held, kept["p"] = lax.optimization_barrier((held, p))
        return held

    den, *den_parts = fetch(den_model[0], route, PARTS, tie)
    (vel,) = fetch(vel_model[0], route)
    p, offs = kept["p"], [off] * PARTS

    before = p_before[0]
    log_den, s2, s3 = call(log_kernel, [padded, narrow, narrow], [den, matrix, before], scratch=z_scratch)
    on_den = paired(den)
    off_den = [across(den_part) for den_part in den_parts]
    slopes = [()]
    for k in parts:
        ins = [log_den, on_den, off_den[k], vel]
        slopes.append(
            call(
                lambda *refs, k=k: slope_x_kernel(k, *refs),
                [narrow, narrow], [*ins, *slopes[-1]],
                aliases={len(ins) + n: n for n in range(len(slopes[-1]))},
            )
        )

    stored, fields, ends = [], [], []
    for step in range(ITERS):
        plain = step == 0
        part, d_y, d_z = call(
            plain_yz_kernel if plain else forward_yz_kernel, [narrow] * 3,
            [p, matrix] if plain else [p, s2, s3, matrix], scratch=z_scratch,
        )
        if step > 0:
            fields.append(p.reshape(flat[0]))
        sending = step < ITERS - 1
        made, sends = (), []
        for k in parts:
            s1, scale = slopes[1 + k] if step == 0 else slopes[-1]
            ins = [p, on, offs[k], part, s1, scale, before] + ([s2, s3, d_y, d_z] if plain else [])
            outs = call(
                lambda *refs, k=k, sending=sending, plain=plain: forward_x_kernel(k, sending, plain, *refs),
                [narrow, narrow] + ([padded, half, part_half] if sending else [part_full]), [*ins, *made],
                aliases={len(ins) + n: n for n in range(len(made))},
            )
            made = outs[: 4 if sending else 2]
            if sending:
                sends.append(across(outs[4]))
            else:
                ends.append(outs[2].reshape(layers * size, depth))
        d_x, applied = made[:2]
        later = made[2] if sending else None
        if sending:
            on, offs = paired(made[3]), sends
        stored.append((applied, d_x, d_y, d_z))
        before, p = p, later

    (q,) = call(prepare_kernel, [padded], [q_now[0]])
    made, offs = (), []
    for k in parts:
        ins = [ends[k], q.reshape(flat[0]), lists[k], seen]
        *made, send = call(
            lambda *refs, k=k: first_adjoint_kernel(ITERS - 1, k, *refs),
            [flat, half, part_half], [*ins, *made], [VM, VM, SM, SM] + [VM] * len(made),
            aliases={len(ins) + n: n for n in range(len(made))},
        )
        offs.append(across(send))
    a, a_half = made
    on = paired(a_half)
    a = a.reshape(padded[0])
    sources = call(
        lambda *refs: receivers_kernel(len(fields), *refs), [flat] * len(fields),
        [seen, *lists, *fields], [SM] * (1 + PARTS) + [VM] * len(fields),
    )
    sources = [source.reshape(padded[0]) for source in sources]
    before, current = q_before[0], q
    sums = ()
    for step in range(ITERS - 1):
        f_applied, f_dx, f_dy, f_dz = stored[ITERS - 1 - step]
        last = step == ITERS - 2
        part, sum_vel, sum_den = call(
            lambda *refs, first=step == 0: adjoint_yz_kernel(first, *refs),
            [narrow] * 3, [a, s2, s3, matrix, f_dy, f_dz, f_applied, *sums], scratch=z_scratch,
        )
        extra = [sum_vel, stored[0][0], vel] if last else []
        made, sends, shot_vel = (), [], []
        for k in parts:
            ins = [
                a, on, offs[k], part, s1, scale, before, sources[ITERS - 2 - step], f_dx, sum_den, *extra,
            ]
            kinds = [padded, half, narrow] + ([] if last else [narrow])
            outs = call(
                lambda *refs, k=k, last=last: adjoint_x_kernel(k, last, *refs),
                kinds + [part_half] * (2 if last else 1), [*ins, *made],
                aliases={len(ins) + n: n for n in range(len(made))},
            )
            made = outs[: len(kinds)]
            sends.append(across(outs[len(kinds)]))
            shot_vel += outs[len(kinds) + 1 :]
        a, a_half, sum_den, *later = made
        on, offs = paired(a_half), sends
        if not last:
            before, current = current, later[0]
        sums = (sum_vel, sum_den)
    _, f_dx, f_dy, f_dz = stored[0]
    grad_vel = [give_back(shot_vel[k], k, route) for k in parts]
    (sum_den,) = call(last_yz_kernel, [narrow], [a, matrix, f_dy, f_dz, sum_den], scratch=z_scratch)
    grad_den = []
    for k in parts:
        (shot_den,) = call(
            lambda *refs, k=k: last_x_kernel(k, *refs),
            [part_half], [a, on, offs[k], f_dx, sum_den, scale, den],
        )
        grad_den.append(give_back(shot_den, k, route))
    return jnp.concatenate(grad_vel, axis=1)[None], jnp.concatenate(grad_den, axis=1)[None]


def solution(mesh):
    spec = P(SHOT, SUB, None, None)
    return jax.shard_map(
        inner,
        mesh=mesh,
        in_specs=(spec, spec, P(), P(SHOT, None), P(SHOT, None, None), spec, spec, spec, spec),
        out_specs=(spec, spec),
        check_vma=False,
    )
```
